32 devices in a mesh: dp: 4 (over z), mp: 8 (over y, x, core).
Axes of the slice: x: 2, y: 2, z: 4, core: 2. Of those that a mesh axis runs over, the one named last changes fastest.
Arguments:
- grad_partial: bfloat16 [4, 4, 576, 576], P('dp', None, 'mp'), may hold values from -1.796875 to 1.796875
- owner: int32 [4], replicated, may hold values from 0 to 7, as said below
- offset: int32 [4], replicated, may hold values from 0 to 3, each once
- left_factor: float32 [8, 576, 576], P('mp', None, 'dp'), may hold values from -3 to 3
- right_factor: float32 [8, 576, 576], P('mp', None, 'dp'), may hold values from -3 to 3
- left_basis: bfloat16 [8, 576, 576], P('mp'), may hold values from -0.25 to 0.25
- right_basis: bfloat16 [8, 576, 576], P('mp'), may hold values from -0.25 to 0.25
- momentum: bfloat16 [8, 576, 576], P('mp'), may hold values from -6 to 6
- second_moment: float32 [8, 576, 576], P('mp'), may hold values from 0.2 to 2
Outputs:
- update: bfloat16 [4, 576, 576], P(None, 'mp', 'dp')
- new_left: float32 [8, 576, 576], P('mp', None, 'dp')
- new_right: float32 [8, 576, 576], P('mp', None, 'dp')
- new_momentum: bfloat16 [8, 576, 576], P('mp')
- new_second: float32 [8, 576, 576], P('mp')
The draws below stay inside these ranges and needn't reach their ends.
Inputs may be any that keep to these rules, and one draw needn't show every extreme that they name: No two blocks have the same owner. `offset`: every position belongs to exactly one block.
All inputs are finite; a program needn't handle non-finite values.
Results may differ from the reference program's by a relative error of at most 0.015.
Values may be sent and summed in bfloat16 or wider, within the bound.
No kernel may reach another device: no remote copies, remote signals or barrier semaphores. Data moves between devices by JAX's collectives and lax.ppermute only.
A program may use at most 64 MiB of HBM per device.

```python
import math
import jax
import jax.numpy as jnp
from jax import lax

BS = 576
BLOCKS = 4
N_DP = 4
N_MP = 8


def draw_owner(key, part):
    return jax.random.permutation(key, N_MP)[:BLOCKS].astype(jnp.int32)


def steps_of(key, dims, split, least, largest):
    def one(position, parts):
        steps = jax.random.uniform(jax.random.fold_in(jax.random.fold_in(key, 6), position), (parts,), jnp.float32, least / len(split), largest / len(split))
        return jnp.repeat(jnp.exp(steps), dims[position] // parts).reshape((-1,) + (1,) * (len(dims) - position - 1))

    factor_of = one(*split[0])
    for cut in split[1:]:
        factor_of = factor_of * one(*cut)
    return factor_of


def bell_draw(key, extent, width, bound, pieces=(), kind=jnp.bfloat16):
    drawn = jax.random.normal(key, extent, jnp.float32) * width
    if len(pieces) > 0:
        drawn = steps_of(key, extent, pieces, -0.22, 0.18) * drawn
    return jnp.clip(drawn, min=-bound, max=bound).astype(kind)


def setup_inputs(seed: int = 0) -> dict:
    key_of = jax.random.split(jax.random.key(seed), 10)
    grad_partial = bell_draw(key_of[0], (N_DP, BLOCKS, BS, BS), 0.3, 1.796875, ((0, 4), (2, 8)))
    owner = draw_owner(jax.random.fold_in(key_of[9], 71), 0)
    offset = jax.random.permutation(key_of[2], BLOCKS).astype(jnp.int32)
    left_factor = bell_draw(key_of[3], (N_MP, BS, BS), 0.5, 3.0, ((0, 8), (2, 4)), jnp.float32)
    right_factor = bell_draw(key_of[4], (N_MP, BS, BS), 0.5, 3.0, ((0, 8), (2, 4)), jnp.float32)
    left_basis = bell_draw(key_of[5], (N_MP, BS, BS), BS ** -0.5, 0.25, ((0, 8),))
    right_basis = bell_draw(key_of[6], (N_MP, BS, BS), BS ** -0.5, 0.25, ((0, 8),))
    momentum = bell_draw(key_of[7], (N_MP, BS, BS), 1.0, 6.0, ((0, 8),))
    second_moment = jnp.clip(jnp.exp(math.log(2.0) - 2.3025851 * jax.random.uniform(key_of[8], (N_MP, BS, BS), jnp.float32) ** steps_of(key_of[8], (N_MP, BS, BS), ((0, 8),), -0.2, 0.2)), 0.2, 2.0)
    return {"grad_partial": grad_partial, "owner": owner, "offset": offset, "left_factor": left_factor, "right_factor": right_factor, "left_basis": left_basis, "right_basis": right_basis, "momentum": momentum, "second_moment": second_moment}


def contract_first(matrix_a, matrix_b):
    return lax.dot_general(matrix_a, matrix_b, (((0,), (0,)), ((), ())), preferred_element_type=jnp.float32)

def contract_last(matrix_a, matrix_b):
    return lax.dot_general(matrix_a, matrix_b, (((1,), (1,)), ((), ())), preferred_element_type=jnp.float32)

def soap_slot(gradient, left_fac, right_fac, left_basis, right_basis, moment, second, back_rows):
    new_left = 0.95 * left_fac + 0.05 * contract_last(gradient, gradient)
    new_right = 0.95 * right_fac + 0.05 * contract_first(gradient, gradient)
    new_moment = (0.9 * moment.astype(jnp.float32) + 0.1 * gradient.astype(jnp.float32)).astype(jnp.bfloat16)
    turned = contract_first(left_basis, gradient).astype(jnp.bfloat16)
    rotated = jnp.dot(turned, right_basis, preferred_element_type=jnp.float32)
    turned_mom = contract_first(left_basis, new_moment).astype(jnp.bfloat16)
    rotated_mom = jnp.dot(turned_mom, right_basis, preferred_element_type=jnp.float32)
    new_second = 0.95 * second + 0.05 * rotated * rotated
    scaled = (rotated_mom / (jnp.sqrt(new_second) + 1e-08)).astype(jnp.bfloat16)
    unrotated = jnp.dot(left_basis, scaled, preferred_element_type=jnp.float32).astype(jnp.bfloat16)
    return (new_left, new_right, new_moment, new_second, contract_last(unrotated, back_rows))

def reference(grad_partial, owner, offset, left_factor, right_factor, left_basis, right_basis, momentum, second_moment):
    summed = lax.optimization_barrier(jnp.sum(grad_partial, axis=0, dtype=jnp.float32)).astype(jnp.bfloat16)
    slot_ids = jnp.arange(N_MP, dtype=jnp.int32)
    matches = owner[None, :] == slot_ids[:, None]
    occupied = jnp.any(matches, axis=1)
    chosen = jnp.argmax(matches, axis=1).astype(jnp.int32)
    slot_grads = summed[offset[chosen]]

    def per_slot(operands):
        gradient, left_fac, right_fac, lbasis, rbasis, moment, second = operands
        return soap_slot(gradient, left_fac, right_fac, lbasis, rbasis, moment, second, rbasis)
    new_left, new_right, new_moment, new_second, turned_back = lax.map(per_slot, (slot_grads, left_factor, right_factor, left_basis, right_basis, momentum, second_moment))
    keep_mask = occupied[:, None, None]
    new_left = jnp.where(keep_mask, new_left, left_factor)
    new_right = jnp.where(keep_mask, new_right, right_factor)
    new_moment = jnp.where(keep_mask, new_moment, momentum)
    new_second = jnp.where(keep_mask, new_second, second_moment)
    result = turned_back.astype(jnp.bfloat16)
    update = jnp.zeros((BLOCKS, BS, BS), jnp.bfloat16).at[offset].set(result[owner])
    return (update, new_left, new_right, new_moment, new_second)
```

```python
import jax
import jax.numpy as jnp
from jax import lax
from jax.experimental import pallas as pl
from jax.experimental.pallas import tpu as pltpu
from jax.sharding import PartitionSpec as P

LANES = 128
SUBLANES = 8
VMEM = pl.BlockSpec(memory_space=pltpu.VMEM)
SMEM = pl.BlockSpec(memory_space=pltpu.SMEM)

def contract_first(matrix_a, matrix_b):
    return lax.dot_general(
        matrix_a, matrix_b, (((0,), (0,)), ((), ())), preferred_element_type=jnp.float32
    )


def contract_last(matrix_a, matrix_b):
    return lax.dot_general(
        matrix_a, matrix_b, (((1,), (1,)), ((), ())), preferred_element_type=jnp.float32
    )


def matmul(matrix_a, matrix_b):
    return jnp.dot(matrix_a, matrix_b, preferred_element_type=jnp.float32)


def tail_start(share):
    return jnp.where(share == 0, 0, 2 * share + 1) if not isinstance(share, int) else (
        0 if share == 0 else 2 * share + 1
    )


def packed_fits(rows, columns, replicas):
    return (
        columns == replicas * LANES + LANES // 2
        and rows == (2 * replicas + 1) * SUBLANES
        and rows % SUBLANES == 0
    )


def pack_kernel(me_ref, grad_ref, *outs):
    replicas = len(outs)
    blocks, rows, columns = grad_ref.shape
    half = LANES // 2
    for step in range(replicas):
        share = lax.rem(me_ref[0] + step, replicas)
        col = pl.multiple_of(share * LANES, LANES)
        start = tail_start(share)
        row = pl.multiple_of(start * SUBLANES, SUBLANES)
        row_third = pl.multiple_of(
            jnp.minimum(start + 2, rows // SUBLANES - 1) * SUBLANES, SUBLANES
        )
        out = outs[step]
        for b in range(blocks):
            out[b, :rows, :] = grad_ref[b, :, pl.ds(col, LANES)]
            out[b, rows : rows + SUBLANES, :half] = grad_ref[
                b, pl.ds(row, SUBLANES), columns - half :
            ]
            row_next = pl.multiple_of(row + SUBLANES, SUBLANES)
            out[b, rows + SUBLANES :, :half] = grad_ref[
                b, pl.ds(row_next, SUBLANES), columns - half :
            ]
            out[b, rows : rows + SUBLANES, half:] = grad_ref[
                b, pl.ds(row_third, SUBLANES), columns - half :
            ]
            out[b, rows + SUBLANES :, half:] = jnp.zeros((SUBLANES, half), out.dtype)


def slot_of(owner_ref, group):
    found = jnp.int32(0)
    block = jnp.int32(0)
    for b in range(owner_ref.shape[0]):
        hit = owner_ref[b] == group
        block = jnp.where(hit, b, block)
        found = jnp.where(hit, 1, found)
    return block, found


def route_kernel(owner_ref, offset_ref, *refs):
    parts, out, summed = refs[:-2], refs[-2], refs[-1]
    replicas = len(parts)
    groups = out.shape[0] // replicas
    blocks = summed.shape[0]
    for b in range(blocks):
        total = parts[0][b].astype(jnp.float32)
        for part in parts[1:]:
            total = total + part[b].astype(jnp.float32)
        summed[b] = total.astype(jnp.bfloat16)
    for group in range(groups):
        block, _ = slot_of(owner_ref, group)
        piece = summed[offset_ref[block]]
        for r in range(replicas):
            out[r * groups + group] = piece


def prepare_kernel(group_ref, owner_ref, lbasis, rbasis, moment, lbasis_t, turned_back):
    _, found = slot_of(owner_ref, group_ref[0])

    @pl.when(found == 1)
    def _():
        transposed = lbasis[...].T
        lbasis_t[...] = transposed
        turned = matmul(transposed, moment[...]).astype(jnp.bfloat16)
        turned_back[...] = 0.9 * matmul(turned, rbasis[...])


def owner_kernel(
    group_ref, share_ref, owner_ref, arrived, lbasis, rbasis, lbasis_t, old_part, second,
    gradient, new_second, back, turned, unrotated,
):
    _, found = slot_of(owner_ref, group_ref[0])
    groups, rows, col_share = back.shape
    columns = gradient.shape[1]
    replicas = arrived.shape[0] // groups
    half = LANES // 2
    tail = columns - half

    @pl.when(found == 1)
    def _():
        for r in range(replicas):
            start = tail_start(r)
            count = 3 if r == 0 else 2
            for m in range(groups):
                piece = r * groups + m
                base = m * rows
                gradient[base : base + rows, r * LANES : (r + 1) * LANES] = arrived[piece, :rows, :]
                for g in range(count):
                    row = base + (start + g) * SUBLANES
                    below = rows + (g % 2) * SUBLANES
                    beside = (g // 2) * half
                    gradient[row : row + SUBLANES, tail:] = arrived[
                        piece, below : below + SUBLANES, beside : beside + half
                    ]
        turned[...] = matmul(lbasis_t[...], gradient[...]).astype(jnp.bfloat16)
        cut = 2 * LANES
        for first in range(0, columns, cut):
            cols = slice(first, min(first + cut, columns))
            rotated = matmul(turned[...], rbasis[:, cols])
            fresh = 0.95 * second[:, cols] + 0.05 * rotated * rotated
            new_second[:, cols] = fresh
            rotated_mom = old_part[:, cols] + 0.1 * rotated
            scaled = (rotated_mom / (jnp.sqrt(fresh) + 1e-08)).astype(jnp.bfloat16)
            unrotated[:, cols] = matmul(lbasis[...], scaled).astype(jnp.bfloat16)
        own = pl.ds(pl.multiple_of(share_ref[0] * col_share, 16), col_share)
        result = contract_last(unrotated[...], rbasis[own, :]).astype(jnp.bfloat16)
        for m in range(groups):
            back[m] = result[m * rows : (m + 1) * rows]

    @pl.when(found == 0)
    def _():
        new_second[...] = second[...]


def factor_kernel(
    group_ref, share_ref, owner_ref, gradient, left_t, right_t, moment, new_left_t, new_right_t,
    new_moment,
):
    _, found = slot_of(owner_ref, group_ref[0])
    col_share, columns = left_t.shape

    @pl.when(found == 1)
    def _():
        first = pl.multiple_of(share_ref[0] * col_share, 16)
        grad = gradient[...]
        new_left_t[...] = 0.95 * left_t[...] + 0.05 * contract_last(
            gradient[pl.ds(first, col_share), :], grad
        )
        rows = lax.broadcasted_iota(jnp.int32, (col_share, columns), 0) + first
        cols = lax.broadcasted_iota(jnp.int32, (col_share, columns), 1)
        pick = jnp.where(rows == cols, 1.0, 0.0).astype(jnp.bfloat16)
        grad_cols_t = contract_last(pick, grad).astype(jnp.bfloat16)
        new_right_t[...] = 0.95 * right_t[...] + 0.05 * matmul(grad_cols_t, grad)
        new_moment[...] = (
            0.9 * moment[...].astype(jnp.float32) + 0.1 * grad.astype(jnp.float32)
        ).astype(jnp.bfloat16)

    @pl.when(found == 0)
    def _():
        new_left_t[...] = left_t[...]
        new_right_t[...] = right_t[...]
        new_moment[...] = moment[...]


def place_kernel(owner_ref, offset_ref, returned, update):
    for b in range(update.shape[0]):
        update[offset_ref[b]] = returned[owner_ref[b]]


def cost(flops, *arrays):
    return pl.CostEstimate(
        flops=flops, bytes_accessed=sum(a.size * a.dtype.itemsize for a in arrays), transcendentals=0
    )


def per_device_packed(
    grad_partial,
    owner,
    offset,
    left_factor,
    right_factor,
    left_basis,
    right_basis,
    momentum,
    second_moment,
):
    pieces = grad_partial[0]
    blocks, rows, columns = pieces.shape
    groups = lax.axis_size("mp")
    replicas = lax.axis_size("dp")
    col_share = columns // replicas
    share = lax.axis_index("dp").astype(jnp.int32).reshape(1)
    group = lax.axis_index("mp").astype(jnp.int32).reshape(1)
    bf16, f32 = jnp.bfloat16, jnp.float32
    shape = jax.ShapeDtypeStruct
    packed = shape((blocks, rows + 2 * SUBLANES, LANES), bf16)
    square = (columns, columns)
    lbasis, rbasis, moment, second = left_basis[0], right_basis[0], momentum[0], second_moment[0]
    left_t, right_t = left_factor[0].T, right_factor[0].T
    product = 2 * columns**3

    parts = pl.pallas_call(
        pack_kernel,
        out_shape=[packed] * replicas,
        in_specs=[SMEM, VMEM],
        out_specs=[VMEM] * replicas,
        name="pack",
    )(share, pieces)
    parts = [parts[0]] + [
        lax.ppermute(parts[s], "dp", [(i, (i + s) % replicas) for i in range(replicas)])
        for s in range(1, replicas)
    ]
    lbasis_t, old_part = pl.pallas_call(
        prepare_kernel,
        out_shape=[shape(square, bf16), shape(square, f32)],
        in_specs=[SMEM, SMEM] + [VMEM] * 3,
        out_specs=[VMEM] * 2,
        cost_estimate=cost(2 * product, lbasis, rbasis, moment, lbasis, second),
        name="prepare",
    )(group, owner, lbasis, rbasis, moment)
    outgoing = pl.pallas_call(
        route_kernel,
        out_shape=shape((replicas * groups,) + packed.shape[1:], bf16),
        in_specs=[SMEM, SMEM] + [VMEM] * replicas,
        out_specs=VMEM,
        scratch_shapes=[pltpu.VMEM(packed.shape, bf16)],
        name="route",
    )(owner, offset, *parts)
    arrived = lax.all_to_all(outgoing, ("dp", "mp"), split_axis=0, concat_axis=0, tiled=True)
    gradient, new_second, back = pl.pallas_call(
        owner_kernel,
        out_shape=[
            shape(square, bf16),
            shape(square, f32),
            shape((groups, rows, col_share), bf16),
        ],
        in_specs=[SMEM] * 3 + [VMEM] * 6,
        out_specs=[VMEM] * 3,
        scratch_shapes=[pltpu.VMEM(square, bf16), pltpu.VMEM(square, bf16)],
        cost_estimate=cost(3 * product, lbasis, rbasis, lbasis_t, old_part, second, second),
        name="owner_step",
    )(group, share, owner, arrived, lbasis, rbasis, lbasis_t, old_part, second)
    returned = lax.all_to_all(back, "mp", split_axis=0, concat_axis=0, tiled=True)
    new_left_t, new_right_t, new_moment = pl.pallas_call(
        factor_kernel,
        out_shape=[shape(left_t.shape, f32), shape(right_t.shape, f32), shape(square, bf16)],
        in_specs=[SMEM] * 3 + [VMEM] * 4,
        out_specs=[VMEM] * 3,
        cost_estimate=cost(product, left_t, left_t, right_t, right_t, moment, moment),
        name="factors",
    )(group, share, owner, gradient, left_t, right_t, moment)
    update = pl.pallas_call(
        place_kernel,
        out_shape=shape((blocks, rows, col_share), bf16),
        in_specs=[SMEM, SMEM, VMEM],
        out_specs=VMEM,
        name="place",
    )(owner, offset, returned)
    return (
        update,
        new_left_t.T[None],
        new_right_t.T[None],
        new_moment[None],
        new_second[None],
    )


def per_device(grad_partial, *rest):
    _, _, rows, columns = grad_partial.shape
    fits = packed_fits(rows, columns, lax.axis_size("dp"))
    return (per_device_packed if fits else per_device_general)(grad_partial, *rest)


def per_device_general(
    grad_partial,
    owner,
    offset,
    left_factor,
    right_factor,
    left_basis,
    right_basis,
    momentum,
    second_moment,
):
    pieces = grad_partial[0]
    blocks, row_count, columns = pieces.shape
    groups = lax.axis_size("mp")
    replicas = lax.axis_size("dp")
    col_share = columns // replicas
    column = lax.axis_index("dp") * col_share
    my_group = lax.axis_index("mp")
    targets = lax.broadcasted_iota(jnp.int32, (groups, blocks), 0)
    positions = lax.broadcasted_iota(jnp.int32, (blocks, blocks), 0)
    routing = (owner[None, :] == targets).astype(jnp.float32)
    where_at = (offset[None, :] == positions).astype(jnp.float32)
    select = contract_last(routing, where_at).astype(jnp.bfloat16)
    occupied = jnp.any(owner == my_group)
    swapped = lax.all_to_all(grad_partial, "dp", split_axis=3, concat_axis=0, tiled=True)
    summed = jnp.sum(swapped.astype(jnp.float32), axis=0).astype(jnp.bfloat16)
    outgoing = jnp.dot(
        select, summed.reshape(blocks, row_count * col_share), preferred_element_type=jnp.float32
    )
    outgoing = outgoing.astype(jnp.bfloat16).reshape(groups, row_count, col_share)
    landed = lax.all_to_all(outgoing, "mp", split_axis=0, concat_axis=0, tiled=True)
    arrived = lax.all_gather(landed, "dp", axis=2, tiled=True)
    gradient = arrived.reshape(groups * row_count, columns)

    def refresh(operands):
        grad_in, left_fac, right_fac, lbasis, rbasis, moment, second = operands
        grad_rows = lax.dynamic_slice_in_dim(grad_in, column, col_share, 0)
        grad_cols = lax.dynamic_slice_in_dim(grad_in, column, col_share, 1)
        new_left = 0.95 * left_fac + 0.05 * contract_last(grad_in, grad_rows)
        new_right = 0.95 * right_fac + 0.05 * contract_first(grad_in, grad_cols)
        new_moment = (0.9 * moment.astype(jnp.float32) + 0.1 * grad_in.astype(jnp.float32)).astype(
            jnp.bfloat16
        )
        turned = contract_first(lbasis, grad_in).astype(jnp.bfloat16)
        rotated = jnp.dot(turned, rbasis, preferred_element_type=jnp.float32)
        turned_mom = contract_first(lbasis, new_moment).astype(jnp.bfloat16)
        rotated_mom = jnp.dot(turned_mom, rbasis, preferred_element_type=jnp.float32)
        new_second = 0.95 * second + 0.05 * rotated * rotated
        scaled = (rotated_mom / (jnp.sqrt(new_second) + 1e-08)).astype(jnp.bfloat16)
        unrotated = jnp.dot(lbasis, scaled, preferred_element_type=jnp.float32).astype(jnp.bfloat16)
        back_rows = lax.dynamic_slice_in_dim(rbasis, column, col_share, 0)
        return (new_left, new_right, new_moment, new_second, contract_last(unrotated, back_rows))

    def keep_old(operands):
        grad_in, left_fac, right_fac, lbasis, rbasis, moment, second = operands
        return (left_fac, right_fac, moment, second, jnp.zeros((columns, col_share), jnp.float32))

    operands = (
        gradient,
        left_factor[0],
        right_factor[0],
        left_basis[0],
        right_basis[0],
        momentum[0],
        second_moment[0],
    )
    new_left, new_right, new_moment, new_second, turned_cols = lax.cond(
        occupied, refresh, keep_old, operands
    )
    outgoing_back = turned_cols.astype(jnp.bfloat16).reshape(groups, row_count, col_share)
    returned = lax.all_to_all(outgoing_back, "mp", split_axis=0, concat_axis=0, tiled=True)
    update = contract_first(select, returned.reshape(groups, row_count * col_share)).astype(
        jnp.bfloat16
    )
    update = update.reshape(blocks, row_count, col_share)
    return (update, new_left[None], new_right[None], new_moment[None], new_second[None])


def solution(mesh):
    placed = (
        P("dp", None, "mp", None),
        P(),
        P(),
        P("mp", None, "dp"),
        P("mp", None, "dp"),
        P("mp", None, None),
        P("mp", None, None),
        P("mp", None, None),
        P("mp", None, None),
    )
    return jax.shard_map(
        per_device,
        mesh=mesh,
        in_specs=placed,
        out_specs=(
            P(None, "mp", "dp"),
            P("mp", None, "dp"),
            P("mp", None, "dp"),
            P("mp", None, None),
            P("mp", None, None),
        ),
        check_vma=False,
    )
```

```python
import jax
import jax.numpy as jnp
from jax import lax
from jax.experimental import pallas as pl
from jax.experimental.pallas import tpu as pltpu
from jax.sharding import PartitionSpec as P

LANES = 128
SUBLANES = 8
VMEM = pl.BlockSpec(memory_space=pltpu.VMEM)
SMEM = pl.BlockSpec(memory_space=pltpu.SMEM)
VMEM_GRANT = 16 * 2**20

def contract_first(matrix_a, matrix_b):
    return lax.dot_general(
        matrix_a, matrix_b, (((0,), (0,)), ((), ())), preferred_element_type=jnp.float32
    )


def contract_last(matrix_a, matrix_b):
    return lax.dot_general(
        matrix_a, matrix_b, (((1,), (1,)), ((), ())), preferred_element_type=jnp.float32
    )


def matmul(matrix_a, matrix_b):
    return jnp.dot(matrix_a, matrix_b, preferred_element_type=jnp.float32)


def tail_start(share):
    return jnp.where(share == 0, 0, 2 * share + 1) if not isinstance(share, int) else (
        0 if share == 0 else 2 * share + 1
    )


def packed_fits(rows, columns, replicas):
    return (
        columns == replicas * LANES + LANES // 2
        and rows == (2 * replicas + 1) * SUBLANES
        and rows % SUBLANES == 0
    )


def pack_kernel(me_ref, grad_ref, *outs):
    replicas = len(outs)
    blocks, rows, columns = grad_ref.shape
    half = LANES // 2
    for step in range(replicas):
        share = lax.rem(me_ref[0] + step, replicas)
        col = pl.multiple_of(share * LANES, LANES)
        start = tail_start(share)
        row = pl.multiple_of(start * SUBLANES, SUBLANES)
        row_third = pl.multiple_of(
            jnp.minimum(start + 2, rows // SUBLANES - 1) * SUBLANES, SUBLANES
        )
        out = outs[step]
        for b in range(blocks):
            out[b, :rows, :] = grad_ref[b, :, pl.ds(col, LANES)]
            out[b, rows : rows + SUBLANES, :half] = grad_ref[
                b, pl.ds(row, SUBLANES), columns - half :
            ]
            row_next = pl.multiple_of(row + SUBLANES, SUBLANES)
            out[b, rows + SUBLANES :, :half] = grad_ref[
                b, pl.ds(row_next, SUBLANES), columns - half :
            ]
            out[b, rows : rows + SUBLANES, half:] = grad_ref[
                b, pl.ds(row_third, SUBLANES), columns - half :
            ]
            out[b, rows + SUBLANES :, half:] = jnp.zeros((SUBLANES, half), out.dtype)


def slot_of(owner_ref, group):
    found = jnp.int32(0)
    block = jnp.int32(0)
    for b in range(owner_ref.shape[0]):
        hit = owner_ref[b] == group
        block = jnp.where(hit, b, block)
        found = jnp.where(hit, 1, found)
    return block, found


def route_kernel(owner_ref, offset_ref, *refs):
    parts, out, summed = refs[:-2], refs[-2], refs[-1]
    replicas = len(parts)
    groups = out.shape[0] // replicas
    blocks = summed.shape[0]
    for b in range(blocks):
        total = parts[0][b].astype(jnp.float32)
        for part in parts[1:]:
            total = total + part[b].astype(jnp.float32)
        summed[b] = total.astype(jnp.bfloat16)
    for group in range(groups):
        block, _ = slot_of(owner_ref, group)
        piece = summed[offset_ref[block]]
        for r in range(replicas):
            out[r * groups + group] = piece


def prepare_kernel(group_ref, owner_ref, lbasis, rbasis, moment, lbasis_t, turned_back):
    _, found = slot_of(owner_ref, group_ref[0])

    @pl.when(found == 1)
    def _():
        transposed = lbasis[...].T
        lbasis_t[...] = transposed
        turned = matmul(transposed, moment[...]).astype(jnp.bfloat16)
        turned_back[...] = 0.9 * matmul(turned, rbasis[...])


def owner_kernel(
    group_ref, share_ref, owner_ref, arrived, lbasis, rbasis, lbasis_t, old_part, second, moment,
    left_t, right_t, back, new_second, new_moment, new_left_t, new_right_t, gradient, turned,
    unrotated,
):
    _, found = slot_of(owner_ref, group_ref[0])
    groups, rows, col_share = back.shape
    columns = gradient.shape[1]
    replicas = arrived.shape[0] // groups
    half = LANES // 2
    tail = columns - half

    @pl.when(found == 1)
    def _():
        for r in range(replicas):
            start = tail_start(r)
            count = 3 if r == 0 else 2
            for m in range(groups):
                piece = r * groups + m
                base = m * rows
                gradient[base : base + rows, r * LANES : (r + 1) * LANES] = arrived[piece, :rows, :]
                for g in range(count):
                    row = base + (start + g) * SUBLANES
                    below = rows + (g % 2) * SUBLANES
                    beside = (g // 2) * half
                    gradient[row : row + SUBLANES, tail:] = arrived[
                        piece, below : below + SUBLANES, beside : beside + half
                    ]
        first = pl.multiple_of(share_ref[0] * col_share, 16)
        own = pl.ds(first, col_share)
        turned[...] = matmul(lbasis_t[...], gradient[...]).astype(jnp.bfloat16)
        cut = 2 * LANES
        for low in range(0, columns, cut):
            cols = slice(low, min(low + cut, columns))
            rotated = matmul(turned[...], rbasis[:, cols])
            fresh = 0.95 * second[:, cols] + 0.05 * rotated * rotated
            new_second[:, cols] = fresh
            rotated_mom = old_part[:, cols] + 0.1 * rotated
            scaled = (rotated_mom / (jnp.sqrt(fresh) + 1e-08)).astype(jnp.bfloat16)
            unrotated[:, cols] = matmul(lbasis[...], scaled).astype(jnp.bfloat16)
        result = contract_last(unrotated[...], rbasis[own, :]).astype(jnp.bfloat16)
        for m in range(groups):
            back[m] = result[m * rows : (m + 1) * rows]
        grad = gradient[...]
        new_left_t[...] = 0.95 * left_t[...] + 0.05 * contract_last(gradient[own, :], grad)
        picked = lax.broadcasted_iota(jnp.int32, (col_share, columns), 0) + first
        places = lax.broadcasted_iota(jnp.int32, (col_share, columns), 1)
        pick = jnp.where(picked == places, 1.0, 0.0).astype(jnp.bfloat16)
        grad_cols_t = contract_last(pick, grad).astype(jnp.bfloat16)
        new_right_t[...] = 0.95 * right_t[...] + 0.05 * matmul(grad_cols_t, grad)
        new_moment[...] = (
            0.9 * moment[...].astype(jnp.float32) + 0.1 * grad.astype(jnp.float32)
        ).astype(jnp.bfloat16)

    @pl.when(found == 0)
    def _():
        new_second[...] = second[...]
        new_moment[...] = moment[...]
        new_left_t[...] = left_t[...]
        new_right_t[...] = right_t[...]


def place_kernel(owner_ref, offset_ref, returned, update):
    for b in range(update.shape[0]):
        update[offset_ref[b]] = returned[owner_ref[b]]


def run(name, kernel, scalars, arrays, outs, scratch=(), flops=0):
    moved = sum(a.size * a.dtype.itemsize for a in list(arrays) + list(outs))
    return pl.pallas_call(
        kernel,
        out_shape=[pltpu.VMEM(o.shape, o.dtype) for o in outs],
        in_specs=[SMEM] * len(scalars) + [VMEM] * len(arrays),
        out_specs=[VMEM] * len(outs),
        scratch_shapes=[pltpu.VMEM(o.shape, o.dtype) for o in scratch],
        compiler_params=pltpu.CompilerParams(vmem_limit_bytes=VMEM_GRANT),
        cost_estimate=pl.CostEstimate(flops=flops, bytes_accessed=moved, transcendentals=0),
        name=name,
    )(*scalars, *(pltpu.with_memory_space_constraint(a, pltpu.VMEM) for a in arrays))


def per_device_packed(
    grad_partial,
    owner,
    offset,
    left_factor,
    right_factor,
    left_basis,
    right_basis,
    momentum,
    second_moment,
):
    pieces = grad_partial[0]
    blocks, rows, columns = pieces.shape
    groups = lax.axis_size("mp")
    replicas = lax.axis_size("dp")
    col_share = columns // replicas
    share = lax.axis_index("dp").astype(jnp.int32).reshape(1)
    group = lax.axis_index("mp").astype(jnp.int32).reshape(1)
    bf16, f32 = jnp.bfloat16, jnp.float32
    shape = jax.ShapeDtypeStruct
    packed = shape((blocks, rows + 2 * SUBLANES, LANES), bf16)
    square = (columns, columns)
    lbasis, rbasis, moment, second = left_basis[0], right_basis[0], momentum[0], second_moment[0]
    left_t, right_t = left_factor[0].T, right_factor[0].T
    product = 2 * columns**3

    parts = run("pack", pack_kernel, [share], [pieces], [packed] * replicas)
    parts = [parts[0]] + [
        lax.ppermute(parts[s], "dp", [(i, (i + s) % replicas) for i in range(replicas)])
        for s in range(1, replicas)
    ]
    lbasis_t, old_part = run(
        "prepare",
        prepare_kernel,
        [group, owner],
        [lbasis, rbasis, moment],
        [shape(square, bf16), shape(square, f32)],
        flops=2 * product,
    )
    parts, lbasis_t, old_part = lax.optimization_barrier((parts, lbasis_t, old_part))
    (outgoing,) = run(
        "route",
        route_kernel,
        [owner, offset],
        parts,
        [shape((replicas * groups,) + packed.shape[1:], bf16)],
        scratch=[packed],
    )
    arrived = lax.all_to_all(outgoing, ("dp", "mp"), split_axis=0, concat_axis=0, tiled=True)
    back, new_second, new_moment, new_left_t, new_right_t = run(
        "owner_step",
        owner_kernel,
        [group, share, owner],
        [arrived, lbasis, rbasis, lbasis_t, old_part, second, moment, left_t, right_t],
        [
            shape((groups, rows, col_share), bf16),
            shape(square, f32),
            shape(square, bf16),
            shape(left_t.shape, f32),
            shape(right_t.shape, f32),
        ],
        scratch=[shape(square, bf16)] * 3,
        flops=4 * product,
    )
    returned = lax.all_to_all(back, "mp", split_axis=0, concat_axis=0, tiled=True)
    (update,) = run(
        "place",
        place_kernel,
        [owner, offset],
        [returned],
        [shape((blocks, rows, col_share), bf16)],
    )
    return (
        update,
        new_left_t.T[None],
        new_right_t.T[None],
        new_moment[None],
        new_second[None],
    )


def per_device(grad_partial, *rest):
    _, _, rows, columns = grad_partial.shape
    fits = packed_fits(rows, columns, lax.axis_size("dp"))
    return (per_device_packed if fits else per_device_general)(grad_partial, *rest)


def per_device_general(
    grad_partial,
    owner,
    offset,
    left_factor,
    right_factor,
    left_basis,
    right_basis,
    momentum,
    second_moment,
):
    pieces = grad_partial[0]
    blocks, row_count, columns = pieces.shape
    groups = lax.axis_size("mp")
    replicas = lax.axis_size("dp")
    col_share = columns // replicas
    column = lax.axis_index("dp") * col_share
    my_group = lax.axis_index("mp")
    targets = lax.broadcasted_iota(jnp.int32, (groups, blocks), 0)
    positions = lax.broadcasted_iota(jnp.int32, (blocks, blocks), 0)
    routing = (owner[None, :] == targets).astype(jnp.float32)
    where_at = (offset[None, :] == positions).astype(jnp.float32)
    select = contract_last(routing, where_at).astype(jnp.bfloat16)
    occupied = jnp.any(owner == my_group)
    swapped = lax.all_to_all(grad_partial, "dp", split_axis=3, concat_axis=0, tiled=True)
    summed = jnp.sum(swapped.astype(jnp.float32), axis=0).astype(jnp.bfloat16)
    outgoing = jnp.dot(
        select, summed.reshape(blocks, row_count * col_share), preferred_element_type=jnp.float32
    )
    outgoing = outgoing.astype(jnp.bfloat16).reshape(groups, row_count, col_share)
    landed = lax.all_to_all(outgoing, "mp", split_axis=0, concat_axis=0, tiled=True)
    arrived = lax.all_gather(landed, "dp", axis=2, tiled=True)
    gradient = arrived.reshape(groups * row_count, columns)

    def refresh(operands):
        grad_in, left_fac, right_fac, lbasis, rbasis, moment, second = operands
        grad_rows = lax.dynamic_slice_in_dim(grad_in, column, col_share, 0)
        grad_cols = lax.dynamic_slice_in_dim(grad_in, column, col_share, 1)
        new_left = 0.95 * left_fac + 0.05 * contract_last(grad_in, grad_rows)
        new_right = 0.95 * right_fac + 0.05 * contract_first(grad_in, grad_cols)
        new_moment = (0.9 * moment.astype(jnp.float32) + 0.1 * grad_in.astype(jnp.float32)).astype(
            jnp.bfloat16
        )
        turned = contract_first(lbasis, grad_in).astype(jnp.bfloat16)
        rotated = jnp.dot(turned, rbasis, preferred_element_type=jnp.float32)
        turned_mom = contract_first(lbasis, new_moment).astype(jnp.bfloat16)
        rotated_mom = jnp.dot(turned_mom, rbasis, preferred_element_type=jnp.float32)
        new_second = 0.95 * second + 0.05 * rotated * rotated
        scaled = (rotated_mom / (jnp.sqrt(new_second) + 1e-08)).astype(jnp.bfloat16)
        unrotated = jnp.dot(lbasis, scaled, preferred_element_type=jnp.float32).astype(jnp.bfloat16)
        back_rows = lax.dynamic_slice_in_dim(rbasis, column, col_share, 0)
        return (new_left, new_right, new_moment, new_second, contract_last(unrotated, back_rows))

    def keep_old(operands):
        grad_in, left_fac, right_fac, lbasis, rbasis, moment, second = operands
        return (left_fac, right_fac, moment, second, jnp.zeros((columns, col_share), jnp.float32))

    operands = (
        gradient,
        left_factor[0],
        right_factor[0],
        left_basis[0],
        right_basis[0],
        momentum[0],
        second_moment[0],
    )
    new_left, new_right, new_moment, new_second, turned_cols = lax.cond(
        occupied, refresh, keep_old, operands
    )
    outgoing_back = turned_cols.astype(jnp.bfloat16).reshape(groups, row_count, col_share)
    returned = lax.all_to_all(outgoing_back, "mp", split_axis=0, concat_axis=0, tiled=True)
    update = contract_first(select, returned.reshape(groups, row_count * col_share)).astype(
        jnp.bfloat16
    )
    update = update.reshape(blocks, row_count, col_share)
    return (update, new_left[None], new_right[None], new_moment[None], new_second[None])


def solution(mesh):
    placed = (
        P("dp", None, "mp", None),
        P(),
        P(),
        P("mp", None, "dp"),
        P("mp", None, "dp"),
        P("mp", None, None),
        P("mp", None, None),
        P("mp", None, None),
        P("mp", None, None),
    )
    return jax.shard_map(
        per_device,
        mesh=mesh,
        in_specs=placed,
        out_specs=(
            P(None, "mp", "dp"),
            P("mp", None, "dp"),
            P("mp", None, "dp"),
            P("mp", None, None),
            P("mp", None, None),
        ),
        check_vma=False,
    )
```

```python
import jax
import jax.numpy as jnp
from jax import lax
from jax.experimental import pallas as pl
from jax.experimental.pallas import tpu as pltpu
from jax.sharding import PartitionSpec as P

LANES = 128
SUBLANES = 8
VMEM = pl.BlockSpec(memory_space=pltpu.VMEM)
SMEM = pl.BlockSpec(memory_space=pltpu.SMEM)
VMEM_GRANT = 16 * 2**20
CUT = 2 * LANES

def contract_first(matrix_a, matrix_b):
    return lax.dot_general(
        matrix_a, matrix_b, (((0,), (0,)), ((), ())), preferred_element_type=jnp.float32
    )


def contract_last(matrix_a, matrix_b):
    return lax.dot_general(
        matrix_a, matrix_b, (((1,), (1,)), ((), ())), preferred_element_type=jnp.float32
    )


def matmul(matrix_a, matrix_b):
    return jnp.dot(matrix_a, matrix_b, preferred_element_type=jnp.float32)


def tail_start(share):
    return jnp.where(share == 0, 0, 2 * share + 1) if not isinstance(share, int) else (
        0 if share == 0 else 2 * share + 1
    )


def packed_fits(rows, columns, replicas):
    width = columns // replicas - LANES
    return (
        columns == replicas * LANES + LANES // 2
        and rows == (2 * replicas + 1) * SUBLANES
        and width * replicas == LANES // 2
        and width % 16 == 0
        and LANES // width == rows // SUBLANES - 1
    )


def pack_kernel(me_ref, grad_ref, *outs):
    replicas = len(outs)
    blocks, rows, columns = grad_ref.shape
    half = LANES // 2
    for step in range(replicas):
        share = lax.rem(me_ref[0] + step, replicas)
        col = pl.multiple_of(share * LANES, LANES)
        start = tail_start(share)
        row = pl.multiple_of(start * SUBLANES, SUBLANES)
        row_third = pl.multiple_of(
            jnp.minimum(start + 2, rows // SUBLANES - 1) * SUBLANES, SUBLANES
        )
        out = outs[step]
        for b in range(blocks):
            out[b, :rows, :] = grad_ref[b, :, pl.ds(col, LANES)]
            out[b, rows : rows + SUBLANES, :half] = grad_ref[
                b, pl.ds(row, SUBLANES), columns - half :
            ]
            row_next = pl.multiple_of(row + SUBLANES, SUBLANES)
            out[b, rows + SUBLANES :, :half] = grad_ref[
                b, pl.ds(row_next, SUBLANES), columns - half :
            ]
            out[b, rows : rows + SUBLANES, half:] = grad_ref[
                b, pl.ds(row_third, SUBLANES), columns - half :
            ]
            out[b, rows + SUBLANES :, half:] = jnp.zeros((SUBLANES, half), out.dtype)


def slot_of(owner_ref, group):
    found = jnp.int32(0)
    block = jnp.int32(0)
    for b in range(owner_ref.shape[0]):
        hit = owner_ref[b] == group
        block = jnp.where(hit, b, block)
        found = jnp.where(hit, 1, found)
    return block, found


def route_kernel(owner_ref, offset_ref, *refs):
    parts, out, summed = refs[:-2], refs[-2], refs[-1]
    replicas = len(parts)
    groups = out.shape[0] // replicas
    blocks = summed.shape[0]
    for b in range(blocks):
        total = parts[0][b].astype(jnp.float32)
        for part in parts[1:]:
            total = total + part[b].astype(jnp.float32)
        summed[b] = total.astype(jnp.bfloat16)
    for group in range(groups):
        block, _ = slot_of(owner_ref, group)
        piece = summed[offset_ref[block]]
        for r in range(replicas):
            out[r * groups + group] = piece


def prepare_kernel(
    group_ref, share_ref, owner_ref, lbasis, rbasis, moment, lbasis_t, old_part, back_basis
):
    _, found = slot_of(owner_ref, group_ref[0])

    @pl.when(found == 1)
    def _():
        transposed = lbasis[...].T
        lbasis_t[...] = transposed
        turned = matmul(transposed, moment[...]).astype(jnp.bfloat16)
        old_part[...] = 0.9 * matmul(turned, rbasis[...])
        columns = rbasis.shape[0]
        col_share = columns // (columns // LANES)
        tail = col_share - LANES
        first = pl.multiple_of(share_ref[0] * col_share, tail)
        main = rbasis[pl.ds(first, LANES), :]
        last = rbasis[pl.ds(pl.multiple_of(first + LANES, tail), tail), :]
        back_basis[...] = jnp.concatenate([main] + [last] * (LANES // tail), axis=0).T


def assemble(arrived, gradient, groups, rows):
    half = LANES // 2
    tail = gradient.shape[1] - half
    for r in range(arrived.shape[0] // groups):
        start = tail_start(r)
        for m in range(groups):
            piece = r * groups + m
            base = m * rows
            gradient[base : base + rows, r * LANES : (r + 1) * LANES] = arrived[piece, :rows, :]
            for g in range(3 if r == 0 else 2):
                row = base + (start + g) * SUBLANES
                below = rows + (g % 2) * SUBLANES
                beside = (g // 2) * half
                gradient[row : row + SUBLANES, tail:] = arrived[
                    piece, below : below + SUBLANES, beside : beside + half
                ]


def owner_kernel(
    group_ref, owner_ref, arrived, lbasis, rbasis, lbasis_t, old_part, back_basis, second,
    back, gradient, new_second, turned,
):
    _, found = slot_of(owner_ref, group_ref[0])
    groups = back.shape[0]
    columns = gradient.shape[1]
    rows = columns // groups

    @pl.when(found == 1)
    def _():
        assemble(arrived, gradient, groups, rows)
        turned[...] = matmul(lbasis_t[...], gradient[...]).astype(jnp.bfloat16)
        total = None
        for low in range(0, columns, CUT):
            cols = slice(low, min(low + CUT, columns))
            rotated = matmul(turned[...], rbasis[:, cols])
            fresh = 0.95 * second[:, cols] + 0.05 * rotated * rotated
            new_second[:, cols] = fresh
            rotated_mom = old_part[:, cols] + 0.1 * rotated
            scaled = (rotated_mom / (jnp.sqrt(fresh) + 1e-08)).astype(jnp.bfloat16)
            term = matmul(scaled, back_basis[cols, :])
            total = term if total is None else total + term
        result = matmul(lbasis[...], total.astype(jnp.bfloat16))
        lane = lax.broadcasted_iota(jnp.int32, (SUBLANES, LANES), 1)
        tail_groups = rows // SUBLANES - 1
        width = LANES // tail_groups
        for m in range(groups):
            base = m * rows
            back[m, :rows, :] = result[base : base + rows, :LANES].astype(jnp.bfloat16)
            mixed = result[base : base + SUBLANES, LANES:]
            for g in range(1, tail_groups):
                row = base + g * SUBLANES
                mixed = jnp.where(
                    lane < g * width, mixed, result[row : row + SUBLANES, LANES:]
                )
            back[m, rows : rows + SUBLANES, :] = mixed.astype(jnp.bfloat16)
            back[m, rows + SUBLANES :, :] = result[
                base + rows - SUBLANES : base + rows, LANES:
            ].astype(jnp.bfloat16)

    @pl.when(found == 0)
    def _():
        new_second[...] = second[...]


def factor_kernel(
    group_ref, share_ref, owner_ref, gradient, left_t, right_t, moment, new_left_t, new_right_t,
    new_moment,
):
    _, found = slot_of(owner_ref, group_ref[0])
    col_share, columns = left_t.shape

    @pl.when(found == 1)
    def _():
        first = pl.multiple_of(share_ref[0] * col_share, 16)
        grad = gradient[...]
        new_left_t[...] = 0.95 * left_t[...] + 0.05 * contract_last(
            gradient[pl.ds(first, col_share), :], grad
        )
        picked = lax.broadcasted_iota(jnp.int32, (col_share, columns), 0) + first
        places = lax.broadcasted_iota(jnp.int32, (col_share, columns), 1)
        pick = jnp.where(picked == places, 1.0, 0.0).astype(jnp.bfloat16)
        grad_cols_t = contract_last(pick, grad).astype(jnp.bfloat16)
        new_right_t[...] = 0.95 * right_t[...] + 0.05 * matmul(grad_cols_t, grad)
        new_moment[...] = (
            0.9 * moment[...].astype(jnp.float32) + 0.1 * grad.astype(jnp.float32)
        ).astype(jnp.bfloat16)

    @pl.when(found == 0)
    def _():
        new_left_t[...] = left_t[...]
        new_right_t[...] = right_t[...]
        new_moment[...] = moment[...]


def place_kernel(owner_ref, offset_ref, returned, update):
    blocks, rows, col_share = update.shape
    tail_groups = rows // SUBLANES - 1
    width = col_share - LANES
    for b in range(blocks):
        place, slot = offset_ref[b], owner_ref[b]
        update[place, :, :LANES] = returned[slot, :rows, :]
        for g in range(tail_groups):
            update[place, g * SUBLANES : (g + 1) * SUBLANES, LANES:] = returned[
                slot, rows : rows + SUBLANES, g * width : (g + 1) * width
            ]
        update[place, rows - SUBLANES :, LANES:] = returned[slot, rows + SUBLANES :, :width]


def run(name, kernel, scalars, arrays, outs, scratch=(), flops=0, keep=True):
    moved = sum(a.size * a.dtype.itemsize for a in list(arrays) + list(outs))
    return pl.pallas_call(
        kernel,
        out_shape=[pltpu.VMEM(o.shape, o.dtype) for o in outs] if keep else list(outs),
        in_specs=[SMEM] * len(scalars) + [VMEM] * len(arrays),
        out_specs=[VMEM] * len(outs),
        scratch_shapes=[pltpu.VMEM(o.shape, o.dtype) for o in scratch],
        compiler_params=pltpu.CompilerParams(vmem_limit_bytes=VMEM_GRANT),
        cost_estimate=pl.CostEstimate(flops=flops, bytes_accessed=moved, transcendentals=0),
        name=name,
    )(*scalars, *(pltpu.with_memory_space_constraint(a, pltpu.VMEM) for a in arrays))


def per_device_packed(
    grad_partial,
    owner,
    offset,
    left_factor,
    right_factor,
    left_basis,
    right_basis,
    momentum,
    second_moment,
):
    pieces = grad_partial[0]
    blocks, rows, columns = pieces.shape
    groups = lax.axis_size("mp")
    replicas = lax.axis_size("dp")
    col_share = columns // replicas
    share = lax.axis_index("dp").astype(jnp.int32).reshape(1)
    group = lax.axis_index("mp").astype(jnp.int32).reshape(1)
    bf16, f32 = jnp.bfloat16, jnp.float32
    shape = jax.ShapeDtypeStruct
    packed = shape((blocks, rows + 2 * SUBLANES, LANES), bf16)
    square = (columns, columns)
    lbasis, rbasis, moment, second = left_basis[0], right_basis[0], momentum[0], second_moment[0]
    left_t, right_t = left_factor[0].T, right_factor[0].T
    product = 2 * columns**3

    parts = run("pack", pack_kernel, [share], [pieces], [packed] * replicas)
    parts = [parts[0]] + [
        lax.ppermute(parts[s], "dp", [(i, (i + s) % replicas) for i in range(replicas)])
        for s in range(1, replicas)
    ]
    lbasis_t, old_part, back_basis = run(
        "prepare",
        prepare_kernel,
        [group, share, owner],
        [lbasis, rbasis, moment],
        [shape(square, bf16), shape(square, f32), shape((columns, 2 * LANES), bf16)],
        flops=2 * product,
    )
    parts, lbasis_t, old_part, back_basis = lax.optimization_barrier(
        (parts, lbasis_t, old_part, back_basis)
    )
    (outgoing,) = run(
        "route",
        route_kernel,
        [owner, offset],
        parts,
        [shape((replicas * groups,) + packed.shape[1:], bf16)],
        scratch=[packed],
    )
    arrived = lax.all_to_all(outgoing, ("dp", "mp"), split_axis=0, concat_axis=0, tiled=True)
    back, gradient, new_second = run(
        "owner_step",
        owner_kernel,
        [group, owner],
        [arrived, lbasis, rbasis, lbasis_t, old_part, back_basis, second],
        [
            shape((groups, rows + 2 * SUBLANES, LANES), bf16),
            shape(square, bf16),
            shape(square, f32),
        ],
        scratch=[shape(square, bf16)],
        flops=3 * product,
    )
    returned = lax.all_to_all(back, "mp", split_axis=0, concat_axis=0, tiled=True)
    new_left_t, new_right_t, new_moment = run(
        "factors",
        factor_kernel,
        [group, share, owner],
        [gradient, left_t, right_t, moment],
        [shape(left_t.shape, f32), shape(right_t.shape, f32), shape(square, bf16)],
        flops=product,
        keep=False,
    )
    (update,) = run(
        "place",
        place_kernel,
        [owner, offset],
        [returned],
        [shape((blocks, rows, col_share), bf16)],
        keep=False,
    )
    return (
        update,
        new_left_t.T[None],
        new_right_t.T[None],
        new_moment[None],
        new_second[None],
    )


def per_device(grad_partial, *rest):
    _, _, rows, columns = grad_partial.shape
    fits = packed_fits(rows, columns, lax.axis_size("dp"))
    return (per_device_packed if fits else per_device_general)(grad_partial, *rest)


def per_device_general(
    grad_partial,
    owner,
    offset,
    left_factor,
    right_factor,
    left_basis,
    right_basis,
    momentum,
    second_moment,
):
    pieces = grad_partial[0]
    blocks, row_count, columns = pieces.shape
    groups = lax.axis_size("mp")
    replicas = lax.axis_size("dp")
    col_share = columns // replicas
    column = lax.axis_index("dp") * col_share
    my_group = lax.axis_index("mp")
    targets = lax.broadcasted_iota(jnp.int32, (groups, blocks), 0)
    positions = lax.broadcasted_iota(jnp.int32, (blocks, blocks), 0)
    routing = (owner[None, :] == targets).astype(jnp.float32)
    where_at = (offset[None, :] == positions).astype(jnp.float32)
    select = contract_last(routing, where_at).astype(jnp.bfloat16)
    occupied = jnp.any(owner == my_group)
    swapped = lax.all_to_all(grad_partial, "dp", split_axis=3, concat_axis=0, tiled=True)
    summed = jnp.sum(swapped.astype(jnp.float32), axis=0).astype(jnp.bfloat16)
    outgoing = jnp.dot(
        select, summed.reshape(blocks, row_count * col_share), preferred_element_type=jnp.float32
    )
    outgoing = outgoing.astype(jnp.bfloat16).reshape(groups, row_count, col_share)
    landed = lax.all_to_all(outgoing, "mp", split_axis=0, concat_axis=0, tiled=True)
    arrived = lax.all_gather(landed, "dp", axis=2, tiled=True)
    gradient = arrived.reshape(groups * row_count, columns)

    def refresh(operands):
        grad_in, left_fac, right_fac, lbasis, rbasis, moment, second = operands
        grad_rows = lax.dynamic_slice_in_dim(grad_in, column, col_share, 0)
        grad_cols = lax.dynamic_slice_in_dim(grad_in, column, col_share, 1)
        new_left = 0.95 * left_fac + 0.05 * contract_last(grad_in, grad_rows)
        new_right = 0.95 * right_fac + 0.05 * contract_first(grad_in, grad_cols)
        new_moment = (0.9 * moment.astype(jnp.float32) + 0.1 * grad_in.astype(jnp.float32)).astype(
            jnp.bfloat16
        )
        turned = contract_first(lbasis, grad_in).astype(jnp.bfloat16)
        rotated = jnp.dot(turned, rbasis, preferred_element_type=jnp.float32)
        turned_mom = contract_first(lbasis, new_moment).astype(jnp.bfloat16)
        rotated_mom = jnp.dot(turned_mom, rbasis, preferred_element_type=jnp.float32)
        new_second = 0.95 * second + 0.05 * rotated * rotated
        scaled = (rotated_mom / (jnp.sqrt(new_second) + 1e-08)).astype(jnp.bfloat16)
        unrotated = jnp.dot(lbasis, scaled, preferred_element_type=jnp.float32).astype(jnp.bfloat16)
        back_rows = lax.dynamic_slice_in_dim(rbasis, column, col_share, 0)
        return (new_left, new_right, new_moment, new_second, contract_last(unrotated, back_rows))

    def keep_old(operands):
        grad_in, left_fac, right_fac, lbasis, rbasis, moment, second = operands
        return (left_fac, right_fac, moment, second, jnp.zeros((columns, col_share), jnp.float32))

    operands = (
        gradient,
        left_factor[0],
        right_factor[0],
        left_basis[0],
        right_basis[0],
        momentum[0],
        second_moment[0],
    )
    new_left, new_right, new_moment, new_second, turned_cols = lax.cond(
        occupied, refresh, keep_old, operands
    )
    outgoing_back = turned_cols.astype(jnp.bfloat16).reshape(groups, row_count, col_share)
    returned = lax.all_to_all(outgoing_back, "mp", split_axis=0, concat_axis=0, tiled=True)
    update = contract_first(select, returned.reshape(groups, row_count * col_share)).astype(
        jnp.bfloat16
    )
    update = update.reshape(blocks, row_count, col_share)
    return (update, new_left[None], new_right[None], new_moment[None], new_second[None])


def solution(mesh):
    placed = (
        P("dp", None, "mp", None),
        P(),
        P(),
        P("mp", None, "dp"),
        P("mp", None, "dp"),
        P("mp", None, None),
        P("mp", None, None),
        P("mp", None, None),
        P("mp", None, None),
    )
    return jax.shard_map(
        per_device,
        mesh=mesh,
        in_specs=placed,
        out_specs=(
            P(None, "mp", "dp"),
            P("mp", None, "dp"),
            P("mp", None, "dp"),
            P("mp", None, None),
            P("mp", None, None),
        ),
        check_vma=False,
    )
```

```python
import jax
import jax.numpy as jnp
from jax import lax
from jax.experimental import pallas as pl
from jax.experimental.pallas import tpu as pltpu
from jax.sharding import PartitionSpec as P

LANES = 128
SUBLANES = 8
VMEM = pl.BlockSpec(memory_space=pltpu.VMEM)
SMEM = pl.BlockSpec(memory_space=pltpu.SMEM)
FAR = pl.BlockSpec(memory_space=pltpu.HBM)
VMEM_GRANT = 16 * 2**20
CUT = 2 * LANES
STRIP = 48

def contract_first(matrix_a, matrix_b):
    return lax.dot_general(
        matrix_a, matrix_b, (((0,), (0,)), ((), ())), preferred_element_type=jnp.float32
    )


def contract_last(matrix_a, matrix_b):
    return lax.dot_general(
        matrix_a, matrix_b, (((1,), (1,)), ((), ())), preferred_element_type=jnp.float32
    )


def matmul(matrix_a, matrix_b):
    return jnp.dot(matrix_a, matrix_b, preferred_element_type=jnp.float32)


def tail_start(share):
    return jnp.where(share == 0, 0, 2 * share + 1) if not isinstance(share, int) else (
        0 if share == 0 else 2 * share + 1
    )


def packed_fits(rows, columns, replicas):
    width = columns // replicas - LANES
    return (
        columns == replicas * LANES + LANES // 2
        and rows == (2 * replicas + 1) * SUBLANES
        and width * replicas == LANES // 2
        and width % 16 == 0
        and LANES // width == rows // SUBLANES - 1
    )


def pack_kernel(me_ref, grad_ref, *outs):
    replicas = len(outs)
    blocks, rows, columns = grad_ref.shape
    half = LANES // 2
    for step in range(replicas):
        share = lax.rem(me_ref[0] + step, replicas)
        col = pl.multiple_of(share * LANES, LANES)
        start = tail_start(share)
        row = pl.multiple_of(start * SUBLANES, SUBLANES)
        row_third = pl.multiple_of(
            jnp.minimum(start + 2, rows // SUBLANES - 1) * SUBLANES, SUBLANES
        )
        out = outs[step]
        for b in range(blocks):
            out[b, :rows, :] = grad_ref[b, :, pl.ds(col, LANES)]
            out[b, rows : rows + SUBLANES, :half] = grad_ref[
                b, pl.ds(row, SUBLANES), columns - half :
            ]
            row_next = pl.multiple_of(row + SUBLANES, SUBLANES)
            out[b, rows + SUBLANES :, :half] = grad_ref[
                b, pl.ds(row_next, SUBLANES), columns - half :
            ]
            out[b, rows : rows + SUBLANES, half:] = grad_ref[
                b, pl.ds(row_third, SUBLANES), columns - half :
            ]
            out[b, rows + SUBLANES :, half:] = jnp.zeros((SUBLANES, half), out.dtype)


def slot_of(owner_ref, group):
    found = jnp.int32(0)
    block = jnp.int32(0)
    for b in range(owner_ref.shape[0]):
        hit = owner_ref[b] == group
        block = jnp.where(hit, b, block)
        found = jnp.where(hit, 1, found)
    return block, found


def route_kernel(owner_ref, offset_ref, *refs):
    parts, out, summed = refs[:-2], refs[-2], refs[-1]
    replicas = len(parts)
    groups = out.shape[0] // replicas
    blocks = summed.shape[0]
    for b in range(blocks):
        total = parts[0][b].astype(jnp.float32)
        for part in parts[1:]:
            total = total + part[b].astype(jnp.float32)
        summed[b] = total.astype(jnp.bfloat16)
    for group in range(groups):
        block, _ = slot_of(owner_ref, group)
        piece = summed[offset_ref[block]]
        for r in range(replicas):
            out[r * groups + group] = piece


def prepare_kernel(
    group_ref, share_ref, owner_ref, lbasis_hbm, rbasis_hbm, moment_hbm,
    lbasis_t, old_part, back_basis, lbasis, rbasis, moment, sems,
):
    _, found = slot_of(owner_ref, group_ref[0])

    @pl.when(found == 1)
    def _():
        copies = [
            pltpu.make_async_copy(source, target, sems.at[n])
            for n, (source, target) in enumerate(
                ((lbasis_hbm, lbasis), (moment_hbm, moment), (rbasis_hbm, rbasis))
            )
        ]
        for copy in copies:
            copy.start()
        copies[0].wait()
        transposed = lbasis[...].T
        lbasis_t[...] = transposed
        copies[1].wait()
        turned = matmul(transposed, moment[...]).astype(jnp.bfloat16)
        copies[2].wait()
        old_part[...] = 0.9 * matmul(turned, rbasis[...])
        columns = rbasis.shape[0]
        col_share = columns // (columns // LANES)
        tail = col_share - LANES
        first = pl.multiple_of(share_ref[0] * col_share, tail)
        main = rbasis[pl.ds(first, LANES), :]
        last = rbasis[pl.ds(pl.multiple_of(first + LANES, tail), tail), :]
        back_basis[...] = jnp.concatenate([main] + [last] * (LANES // tail), axis=0).T


def assemble(arrived, gradient, groups, rows):
    half = LANES // 2
    tail = gradient.shape[1] - half
    for r in range(arrived.shape[0] // groups):
        start = tail_start(r)
        for m in range(groups):
            piece = r * groups + m
            base = m * rows
            gradient[base : base + rows, r * LANES : (r + 1) * LANES] = arrived[piece, :rows, :]
            for g in range(3 if r == 0 else 2):
                row = base + (start + g) * SUBLANES
                below = rows + (g % 2) * SUBLANES
                beside = (g // 2) * half
                gradient[row : row + SUBLANES, tail:] = arrived[
                    piece, below : below + SUBLANES, beside : beside + half
                ]


def owner_kernel(
    group_ref, owner_ref, arrived, lbasis, rbasis, lbasis_t, old_part, back_basis, second,
    gradient, new_second, back_out, turned, back, sems,
):
    _, found = slot_of(owner_ref, group_ref[0])
    groups = back.shape[0]
    copies = [
        pltpu.make_async_copy(back.at[n], back_out.at[n], sems.at[n]) for n in range(groups)
    ]
    columns = gradient.shape[1]
    rows = columns // groups

    @pl.when(found == 1)
    def _():
        assemble(arrived, gradient, groups, rows)
        turned[...] = matmul(lbasis_t[...], gradient[...]).astype(jnp.bfloat16)
        total = None
        for low in range(0, columns, CUT):
            cols = slice(low, min(low + CUT, columns))
            rotated = matmul(turned[...], rbasis[:, cols])
            fresh = 0.95 * second[:, cols] + 0.05 * rotated * rotated
            new_second[:, cols] = fresh
            rotated_mom = old_part[:, cols] + 0.1 * rotated
            spread = fresh * lax.rsqrt(fresh) + 1e-08
            scaled = (rotated_mom * lax.rsqrt(spread * spread)).astype(jnp.bfloat16)
            term = matmul(scaled, back_basis[cols, :])
            total = term if total is None else total + term
        result = matmul(lbasis[...], total.astype(jnp.bfloat16))
        lane = lax.broadcasted_iota(jnp.int32, (SUBLANES, LANES), 1)
        tail_groups = rows // SUBLANES - 1
        width = LANES // tail_groups
        for m in range(groups):
            base = m * rows
            back[groups - 1 - m, :rows, :] = result[base : base + rows, :LANES].astype(jnp.bfloat16)
            mixed = result[base : base + SUBLANES, LANES:]
            for g in range(1, tail_groups):
                row = base + g * SUBLANES
                mixed = jnp.where(
                    lane < g * width, mixed, result[row : row + SUBLANES, LANES:]
                )
            back[groups - 1 - m, rows : rows + SUBLANES, :] = mixed.astype(jnp.bfloat16)
            back[groups - 1 - m, rows + SUBLANES :, :] = result[
                base + rows - SUBLANES : base + rows, LANES:
            ].astype(jnp.bfloat16)
        for copy in copies:
            copy.start()
        for copy in copies:
            copy.wait()

    @pl.when(found == 0)
    def _():
        new_second[...] = second[...]


def factor_kernel(
    group_ref, share_ref, owner_ref, gradient, second, left_hbm, right_hbm, moment_hbm,
    second_out, left_out, right_out, moment_out,
    left_t, right_t, moment, new_left_t, new_right_t, new_moment, sems,
):
    _, found = slot_of(owner_ref, group_ref[0])
    col_share, columns = left_t.shape
    pairs = (
        (moment_hbm, moment),
        (left_hbm, left_t),
        (right_hbm, right_t),
        (second, second_out),
        (new_moment, moment_out),
        (new_left_t, left_out),
        (new_right_t, right_out),
        (moment, moment_out),
        (left_t, left_out),
        (right_t, right_out),
    )
    copies = [pltpu.make_async_copy(a, b, sems.at[n]) for n, (a, b) in enumerate(pairs)]
    for copy in copies[:4]:
        copy.start()

    @pl.when(found == 1)
    def _():
        first = pl.multiple_of(share_ref[0] * col_share, 16)
        grad = gradient[...]
        copies[0].wait()
        for low in range(0, columns, STRIP):
            strip = slice(low, min(low + STRIP, columns))
            new_moment[strip, :] = (
                0.9 * moment[strip, :].astype(jnp.float32)
                + 0.1 * gradient[strip, :].astype(jnp.float32)
            ).astype(jnp.bfloat16)
        copies[4].start()
        copies[1].wait()
        new_left_t[...] = 0.95 * left_t[...] + 0.05 * contract_last(
            gradient[pl.ds(first, col_share), :], grad
        )
        copies[5].start()
        picked = lax.broadcasted_iota(jnp.int32, (col_share, columns), 0) + first
        places = lax.broadcasted_iota(jnp.int32, (col_share, columns), 1)
        pick = jnp.where(picked == places, 1.0, 0.0).astype(jnp.bfloat16)
        grad_cols_t = contract_last(pick, grad).astype(jnp.bfloat16)
        copies[2].wait()
        new_right_t[...] = 0.95 * right_t[...] + 0.05 * matmul(grad_cols_t, grad)
        copies[6].start()
        for copy in copies[3:7]:
            copy.wait()

    @pl.when(found == 0)
    def _():
        for n in range(3):
            copies[n].wait()
            copies[7 + n].start()
        copies[3].wait()
        for copy in copies[7:]:
            copy.wait()


def place_kernel(owner_ref, offset_ref, returned, update):
    blocks, rows, col_share = update.shape
    tail_groups = rows // SUBLANES - 1
    width = col_share - LANES
    for b in range(blocks):
        place, slot = offset_ref[b], returned.shape[0] - 1 - owner_ref[b]
        update[place, :, :LANES] = returned[slot, :rows, :]
        for g in range(tail_groups):
            update[place, g * SUBLANES : (g + 1) * SUBLANES, LANES:] = returned[
                slot, rows : rows + SUBLANES, g * width : (g + 1) * width
            ]
        update[place, rows - SUBLANES :, LANES:] = returned[slot, rows + SUBLANES :, :width]


def run(name, kernel, scalars, arrays, outs, scratch=(), flops=0, sems=0, far=0, far_outs=0):
    moved = sum(a.size * a.dtype.itemsize for a in list(arrays) + list(outs))
    near = len(arrays) - far
    near_outs = len(outs) - max(far_outs, 0)
    near_shape = (lambda o: o) if far_outs < 0 else (lambda o: pltpu.VMEM(o.shape, o.dtype))
    return pl.pallas_call(
        kernel,
        out_shape=[near_shape(o) for o in outs[:near_outs]]
        + [pltpu.HBM(o.shape, o.dtype) for o in outs[near_outs:]],
        in_specs=[SMEM] * len(scalars) + [VMEM] * near + [FAR] * far,
        out_specs=[VMEM] * near_outs + [FAR] * max(far_outs, 0),
        scratch_shapes=[pltpu.VMEM(o.shape, o.dtype) for o in scratch]
        + [pltpu.SemaphoreType.DMA((sems,))] * (sems > 0),
        compiler_params=pltpu.CompilerParams(vmem_limit_bytes=VMEM_GRANT),
        cost_estimate=pl.CostEstimate(flops=flops, bytes_accessed=moved, transcendentals=0),
        name=name,
    )(
        *scalars,
        *(pltpu.with_memory_space_constraint(a, pltpu.VMEM) for a in arrays[:near]),
        *(pltpu.with_memory_space_constraint(a, pltpu.HBM) for a in arrays[near:]),
    )


def per_device_packed(
    grad_partial,
    owner,
    offset,
    left_factor,
    right_factor,
    left_basis,
    right_basis,
    momentum,
    second_moment,
):
    pieces = grad_partial[0]
    blocks, rows, columns = pieces.shape
    groups = lax.axis_size("mp")
    replicas = lax.axis_size("dp")
    col_share = columns // replicas
    share = lax.axis_index("dp").astype(jnp.int32).reshape(1)
    group = lax.axis_index("mp").astype(jnp.int32).reshape(1)
    bf16, f32 = jnp.bfloat16, jnp.float32
    shape = jax.ShapeDtypeStruct
    packed = shape((blocks, rows + 2 * SUBLANES, LANES), bf16)
    square = (columns, columns)
    lbasis, rbasis, moment, second = left_basis[0], right_basis[0], momentum[0], second_moment[0]
    left_t, right_t = left_factor[0].T, right_factor[0].T
    product = 2 * columns**3

    parts = run("pack", pack_kernel, [share], [pieces], [packed] * replicas)
    parts = [parts[0]] + [
        lax.ppermute(parts[s], "dp", [(i, (i + s) % replicas) for i in range(replicas)])
        for s in range(1, replicas)
    ]
    lbasis_t, old_part, back_basis = run(
        "prepare",
        prepare_kernel,
        [group, share, owner],
        [lbasis, rbasis, moment],
        [shape(square, bf16), shape(square, f32), shape((columns, 2 * LANES), bf16)],
        scratch=[shape(square, bf16)] * 3,
        sems=3,
        far=3,
        flops=2 * product,
    )
    parts, lbasis_t, old_part, back_basis = lax.optimization_barrier(
        (parts, lbasis_t, old_part, back_basis)
    )
    (outgoing,) = run(
        "route",
        route_kernel,
        [owner, offset],
        parts,
        [shape((replicas * groups,) + packed.shape[1:], bf16)],
        scratch=[packed],
    )
    arrived = lax.all_to_all(outgoing, ("dp", "mp"), split_axis=0, concat_axis=0, tiled=True)
    chunks = shape((groups, rows + 2 * SUBLANES, LANES), bf16)
    gradient, new_second, back = run(
        "owner_step",
        owner_kernel,
        [group, owner],
        [arrived, lbasis, rbasis, lbasis_t, old_part, back_basis, second],
        [shape(square, bf16), shape(square, f32), chunks],
        scratch=[shape(square, bf16), chunks],
        sems=groups,
        far_outs=1,
        flops=3 * product,
    )
    returned = lax.all_to_all(
        back,
        "mp",
        split_axis=0,
        concat_axis=0,
        tiled=True,
        axis_index_groups=[list(range(groups))[::-1]],
    )
    factor_t = shape(left_t.shape, f32)
    new_second, new_left_t, new_right_t, new_moment = run(
        "factors",
        factor_kernel,
        [group, share, owner],
        [gradient, new_second, left_t, right_t, moment],
        [shape(square, f32), factor_t, factor_t, shape(square, bf16)],
        scratch=[factor_t, factor_t, shape(square, bf16)] * 2,
        sems=10,
        far=3,
        far_outs=4,
        flops=product,
    )
    (update,) = run(
        "place",
        place_kernel,
        [owner, offset],
        [returned],
        [shape((blocks, rows, col_share), bf16)],
        far_outs=-1,
    )
    return (
        update,
        new_left_t.T[None],
        new_right_t.T[None],
        new_moment[None],
        new_second[None],
    )


def per_device(grad_partial, *rest):
    _, _, rows, columns = grad_partial.shape
    fits = packed_fits(rows, columns, lax.axis_size("dp"))
    return (per_device_packed if fits else per_device_general)(grad_partial, *rest)


def per_device_general(
    grad_partial,
    owner,
    offset,
    left_factor,
    right_factor,
    left_basis,
    right_basis,
    momentum,
    second_moment,
):
    pieces = grad_partial[0]
    blocks, row_count, columns = pieces.shape
    groups = lax.axis_size("mp")
    replicas = lax.axis_size("dp")
    col_share = columns // replicas
    column = lax.axis_index("dp") * col_share
    my_group = lax.axis_index("mp")
    targets = lax.broadcasted_iota(jnp.int32, (groups, blocks), 0)
    positions = lax.broadcasted_iota(jnp.int32, (blocks, blocks), 0)
    routing = (owner[None, :] == targets).astype(jnp.float32)
    where_at = (offset[None, :] == positions).astype(jnp.float32)
    select = contract_last(routing, where_at).astype(jnp.bfloat16)
    occupied = jnp.any(owner == my_group)
    swapped = lax.all_to_all(grad_partial, "dp", split_axis=3, concat_axis=0, tiled=True)
    summed = jnp.sum(swapped.astype(jnp.float32), axis=0).astype(jnp.bfloat16)
    outgoing = jnp.dot(
        select, summed.reshape(blocks, row_count * col_share), preferred_element_type=jnp.float32
    )
    outgoing = outgoing.astype(jnp.bfloat16).reshape(groups, row_count, col_share)
    landed = lax.all_to_all(outgoing, "mp", split_axis=0, concat_axis=0, tiled=True)
    arrived = lax.all_gather(landed, "dp", axis=2, tiled=True)
    gradient = arrived.reshape(groups * row_count, columns)

    def refresh(operands):
        grad_in, left_fac, right_fac, lbasis, rbasis, moment, second = operands
        grad_rows = lax.dynamic_slice_in_dim(grad_in, column, col_share, 0)
        grad_cols = lax.dynamic_slice_in_dim(grad_in, column, col_share, 1)
        new_left = 0.95 * left_fac + 0.05 * contract_last(grad_in, grad_rows)
        new_right = 0.95 * right_fac + 0.05 * contract_first(grad_in, grad_cols)
        new_moment = (0.9 * moment.astype(jnp.float32) + 0.1 * grad_in.astype(jnp.float32)).astype(
            jnp.bfloat16
        )
        turned = contract_first(lbasis, grad_in).astype(jnp.bfloat16)
        rotated = jnp.dot(turned, rbasis, preferred_element_type=jnp.float32)
        turned_mom = contract_first(lbasis, new_moment).astype(jnp.bfloat16)
        rotated_mom = jnp.dot(turned_mom, rbasis, preferred_element_type=jnp.float32)
        new_second = 0.95 * second + 0.05 * rotated * rotated
        scaled = (rotated_mom / (jnp.sqrt(new_second) + 1e-08)).astype(jnp.bfloat16)
        unrotated = jnp.dot(lbasis, scaled, preferred_element_type=jnp.float32).astype(jnp.bfloat16)
        back_rows = lax.dynamic_slice_in_dim(rbasis, column, col_share, 0)
        return (new_left, new_right, new_moment, new_second, contract_last(unrotated, back_rows))

    def keep_old(operands):
        grad_in, left_fac, right_fac, lbasis, rbasis, moment, second = operands
        return (left_fac, right_fac, moment, second, jnp.zeros((columns, col_share), jnp.float32))

    operands = (
        gradient,
        left_factor[0],
        right_factor[0],
        left_basis[0],
        right_basis[0],
        momentum[0],
        second_moment[0],
    )
    new_left, new_right, new_moment, new_second, turned_cols = lax.cond(
        occupied, refresh, keep_old, operands
    )
    outgoing_back = turned_cols.astype(jnp.bfloat16).reshape(groups, row_count, col_share)
    returned = lax.all_to_all(outgoing_back, "mp", split_axis=0, concat_axis=0, tiled=True)
    update = contract_first(select, returned.reshape(groups, row_count * col_share)).astype(
        jnp.bfloat16
    )
    update = update.reshape(blocks, row_count, col_share)
    return (update, new_left[None], new_right[None], new_moment[None], new_second[None])


def solution(mesh):
    placed = (
        P("dp", None, "mp", None),
        P(),
        P(),
        P("mp", None, "dp"),
        P("mp", None, "dp"),
        P("mp", None, None),
        P("mp", None, None),
        P("mp", None, None),
        P("mp", None, None),
    )
    return jax.shard_map(
        per_device,
        mesh=mesh,
        in_specs=placed,
        out_specs=(
            P(None, "mp", "dp"),
            P("mp", None, "dp"),
            P("mp", None, "dp"),
            P("mp", None, None),
            P("mp", None, None),
        ),
        check_vma=False,
    )
```

```python
import jax
import jax.numpy as jnp
from jax import lax
from jax.experimental import pallas as pl
from jax.experimental.pallas import tpu as pltpu
from jax.sharding import PartitionSpec as P

LANES = 128
SUBLANES = 8
VMEM = pl.BlockSpec(memory_space=pltpu.VMEM)
SMEM = pl.BlockSpec(memory_space=pltpu.SMEM)
FAR = pl.BlockSpec(memory_space=pltpu.HBM)
VMEM_GRANT = 16 * 2**20
CUT = 2 * LANES
STRIP = 48

def contract_first(matrix_a, matrix_b):
    return lax.dot_general(
        matrix_a, matrix_b, (((0,), (0,)), ((), ())), preferred_element_type=jnp.float32
    )


def contract_last(matrix_a, matrix_b):
    return lax.dot_general(
        matrix_a, matrix_b, (((1,), (1,)), ((), ())), preferred_element_type=jnp.float32
    )


def matmul(matrix_a, matrix_b):
    return jnp.dot(matrix_a, matrix_b, preferred_element_type=jnp.float32)


def tail_start(share):
    return jnp.where(share == 0, 0, 2 * share + 1) if not isinstance(share, int) else (
        0 if share == 0 else 2 * share + 1
    )


def packed_fits(rows, columns, replicas):
    width = columns // replicas - LANES
    return (
        columns == replicas * LANES + LANES // 2
        and rows == (2 * replicas + 1) * SUBLANES
        and width * replicas == LANES // 2
        and width % 16 == 0
        and LANES // width == rows // SUBLANES - 1
    )


def pack_kernel(me_ref, grad_hbm, *refs):
    outs, last, sems = refs[:-2], refs[-2], refs[-1]
    replicas = len(outs)
    blocks, rows, columns = grad_hbm.shape
    half = LANES // 2
    copies = [pltpu.make_async_copy(grad_hbm.at[:, :, columns - half :], last, sems.at[replicas])]
    for step in range(replicas):
        share = lax.rem(me_ref[0] + step, replicas)
        col = pl.multiple_of(share * LANES, LANES)
        copies.append(
            pltpu.make_async_copy(
                grad_hbm.at[:, :, pl.ds(col, LANES)], outs[step].at[:, :rows, :], sems.at[step]
            )
        )
    for copy in copies:
        copy.start()
    copies[0].wait()
    for step in range(replicas):
        share = lax.rem(me_ref[0] + step, replicas)
        start = tail_start(share)
        row = pl.multiple_of(start * SUBLANES, SUBLANES)
        row_next = pl.multiple_of(row + SUBLANES, SUBLANES)
        row_third = pl.multiple_of(
            jnp.minimum(start + 2, rows // SUBLANES - 1) * SUBLANES, SUBLANES
        )
        out = outs[step]
        for b in range(blocks):
            out[b, rows : rows + SUBLANES, :half] = last[b, pl.ds(row, SUBLANES), :]
            out[b, rows + SUBLANES :, :half] = last[b, pl.ds(row_next, SUBLANES), :]
            out[b, rows : rows + SUBLANES, half:] = last[b, pl.ds(row_third, SUBLANES), :]
            out[b, rows + SUBLANES :, half:] = jnp.zeros((SUBLANES, half), out.dtype)
    for copy in copies[1:]:
        copy.wait()


def slot_of(owner_ref, group):
    found = jnp.int32(0)
    block = jnp.int32(0)
    for b in range(owner_ref.shape[0]):
        hit = owner_ref[b] == group
        block = jnp.where(hit, b, block)
        found = jnp.where(hit, 1, found)
    return block, found


def route_kernel(owner_ref, offset_ref, *refs):
    parts, out, summed = refs[:-2], refs[-2], refs[-1]
    replicas = len(parts)
    groups = out.shape[0] // replicas
    blocks = summed.shape[0]
    for b in range(blocks):
        total = parts[0][b].astype(jnp.float32)
        for part in parts[1:]:
            total = total + part[b].astype(jnp.float32)
        summed[b] = total.astype(jnp.bfloat16)
    for group in range(groups):
        block, _ = slot_of(owner_ref, group)
        piece = summed[offset_ref[block]]
        for r in range(replicas):
            out[r * groups + group] = piece


def prepare_kernel(
    group_ref, share_ref, owner_ref, lbasis_hbm, rbasis_hbm, moment_hbm,
    lbasis_t, old_part, back_basis, lbasis, rbasis, moment, sems,
):
    _, found = slot_of(owner_ref, group_ref[0])

    @pl.when(found == 1)
    def _():
        copies = [
            pltpu.make_async_copy(source, target, sems.at[n])
            for n, (source, target) in enumerate(
                ((lbasis_hbm, lbasis), (moment_hbm, moment), (rbasis_hbm, rbasis))
            )
        ]
        for copy in copies:
            copy.start()
        copies[0].wait()
        transposed = lbasis[...].T
        lbasis_t[...] = transposed
        copies[1].wait()
        turned = matmul(transposed, moment[...]).astype(jnp.bfloat16)
        copies[2].wait()
        old_part[...] = 0.9 * matmul(turned, rbasis[...])
        columns = rbasis.shape[0]
        col_share = columns // (columns // LANES)
        tail = col_share - LANES
        first = pl.multiple_of(share_ref[0] * col_share, tail)
        main = rbasis[pl.ds(first, LANES), :]
        last = rbasis[pl.ds(pl.multiple_of(first + LANES, tail), tail), :]
        back_basis[...] = jnp.concatenate([main] + [last] * (LANES // tail), axis=0).T


def assemble(arrived, gradient, groups, rows):
    half = LANES // 2
    tail = gradient.shape[1] - half
    for r in range(arrived.shape[0] // groups):
        start = tail_start(r)
        for m in range(groups):
            piece = r * groups + m
            base = m * rows
            gradient[base : base + rows, r * LANES : (r + 1) * LANES] = arrived[piece, :rows, :]
            for g in range(3 if r == 0 else 2):
                row = base + (start + g) * SUBLANES
                below = rows + (g % 2) * SUBLANES
                beside = (g // 2) * half
                gradient[row : row + SUBLANES, tail:] = arrived[
                    piece, below : below + SUBLANES, beside : beside + half
                ]


def owner_kernel(
    group_ref, owner_ref, arrived, lbasis, rbasis, lbasis_t, old_part, back_basis, second,
    moment_hbm, left_hbm, right_hbm,
    gradient, moment, left_t, right_t, second_out, back_out,
    turned, back, new_second, sems,
):
    _, found = slot_of(owner_ref, group_ref[0])
    groups = back.shape[0]
    copies = [
        pltpu.make_async_copy(back.at[n], back_out.at[n], sems.at[n]) for n in range(groups)
    ]
    loads = [
        pltpu.make_async_copy(source, target, sems.at[groups + n])
        for n, (source, target) in enumerate(
            ((moment_hbm, moment), (left_hbm, left_t), (right_hbm, right_t))
        )
    ]
    fresh_copy = pltpu.make_async_copy(new_second, second_out, sems.at[groups + 3])
    kept_copy = pltpu.make_async_copy(second, second_out, sems.at[groups + 4])
    for load in loads:
        load.start()
    columns = gradient.shape[1]
    rows = columns // groups

    @pl.when(found == 1)
    def _():
        assemble(arrived, gradient, groups, rows)
        turned[...] = matmul(lbasis_t[...], gradient[...]).astype(jnp.bfloat16)
        total = None
        for low in range(0, columns, CUT):
            cols = slice(low, min(low + CUT, columns))
            rotated = matmul(turned[...], rbasis[:, cols])
            fresh = 0.95 * second[:, cols] + 0.05 * rotated * rotated
            new_second[:, cols] = fresh
            rotated_mom = old_part[:, cols] + 0.1 * rotated
            spread = fresh * lax.rsqrt(fresh) + 1e-08
            scaled = (rotated_mom * lax.rsqrt(spread * spread)).astype(jnp.bfloat16)
            term = matmul(scaled, back_basis[cols, :])
            total = term if total is None else total + term
        fresh_copy.start()
        result = matmul(lbasis[...], total.astype(jnp.bfloat16))
        lane = lax.broadcasted_iota(jnp.int32, (SUBLANES, LANES), 1)
        tail_groups = rows // SUBLANES - 1
        width = LANES // tail_groups
        for m in range(groups):
            base = m * rows
            back[groups - 1 - m, :rows, :] = result[base : base + rows, :LANES].astype(jnp.bfloat16)
            mixed = result[base : base + SUBLANES, LANES:]
            for g in range(1, tail_groups):
                row = base + g * SUBLANES
                mixed = jnp.where(
                    lane < g * width, mixed, result[row : row + SUBLANES, LANES:]
                )
            back[groups - 1 - m, rows : rows + SUBLANES, :] = mixed.astype(jnp.bfloat16)
            back[groups - 1 - m, rows + SUBLANES :, :] = result[
                base + rows - SUBLANES : base + rows, LANES:
            ].astype(jnp.bfloat16)
        for copy in copies:
            copy.start()
        for copy in copies + [fresh_copy]:
            copy.wait()

    @pl.when(found == 0)
    def _():
        kept_copy.start()
        kept_copy.wait()

    for load in loads:
        load.wait()


def factor_kernel(
    group_ref, share_ref, owner_ref, gradient, moment, left_t, right_t,
    moment_out, left_out, right_out, new_moment, new_left_t, new_right_t, sems,
):
    _, found = slot_of(owner_ref, group_ref[0])
    col_share, columns = left_t.shape
    outs = (moment_out, left_out, right_out)
    fresh, kept = (
        [pltpu.make_async_copy(a, b, sems.at[n]) for n, (a, b) in enumerate(zip(sources, outs))]
        for sources in ((new_moment, new_left_t, new_right_t), (moment, left_t, right_t))
    )

    @pl.when(found == 1)
    def _():
        for low in range(0, columns, STRIP):
            strip = slice(low, min(low + STRIP, columns))
            new_moment[strip, :] = (
                0.9 * moment[strip, :].astype(jnp.float32)
                + 0.1 * gradient[strip, :].astype(jnp.float32)
            ).astype(jnp.bfloat16)
        fresh[0].start()
        first = pl.multiple_of(share_ref[0] * col_share, 16)
        grad = gradient[...]
        new_left_t[...] = 0.95 * left_t[...] + 0.05 * contract_last(
            gradient[pl.ds(first, col_share), :], grad
        )
        picked = lax.broadcasted_iota(jnp.int32, (col_share, columns), 0) + first
        places = lax.broadcasted_iota(jnp.int32, (col_share, columns), 1)
        pick = jnp.where(picked == places, 1.0, 0.0).astype(jnp.bfloat16)
        grad_cols_t = contract_last(pick, grad).astype(jnp.bfloat16)
        new_right_t[...] = 0.95 * right_t[...] + 0.05 * matmul(grad_cols_t, grad)
        for copy in fresh[1:]:
            copy.start()
        for copy in fresh:
            copy.wait()

    @pl.when(found == 0)
    def _():
        for copy in kept:
            copy.start()
        for copy in kept:
            copy.wait()


def place_kernel(owner_ref, offset_ref, returned, update, tails, sems):
    blocks, rows, col_share = update.shape
    tail_groups = rows // SUBLANES - 1
    width = col_share - LANES
    copies = []
    for b in range(blocks):
        place, slot = offset_ref[b], returned.shape[0] - 1 - owner_ref[b]
        copies.append(
            pltpu.make_async_copy(
                returned.at[slot, :rows], update.at[place, :, :LANES], sems.at[b]
            )
        )
        copies[-1].start()
    for b in range(blocks):
        place, slot = offset_ref[b], returned.shape[0] - 1 - owner_ref[b]
        for g in range(tail_groups):
            tails[b, g * SUBLANES : (g + 1) * SUBLANES, :] = returned[
                slot, rows : rows + SUBLANES, g * width : (g + 1) * width
            ]
        tails[b, rows - SUBLANES :, :] = returned[slot, rows + SUBLANES :, :width]
        copies.append(
            pltpu.make_async_copy(
                tails.at[b], update.at[place, :, LANES:], sems.at[blocks + b]
            )
        )
        copies[-1].start()
    for copy in copies:
        copy.wait()


def run(name, kernel, scalars, arrays, outs, scratch=(), flops=0, sems=0, far=0, far_outs=0):
    moved = sum(a.size * a.dtype.itemsize for a in list(arrays) + list(outs))
    near = len(arrays) - far
    near_outs = len(outs) - far_outs
    return pl.pallas_call(
        kernel,
        out_shape=[pltpu.VMEM(o.shape, o.dtype) for o in outs[:near_outs]]
        + [pltpu.HBM(o.shape, o.dtype) for o in outs[near_outs:]],
        in_specs=[SMEM] * len(scalars) + [VMEM] * near + [FAR] * far,
        out_specs=[VMEM] * near_outs + [FAR] * far_outs,
        scratch_shapes=[pltpu.VMEM(o.shape, o.dtype) for o in scratch]
        + [pltpu.SemaphoreType.DMA((sems,))] * (sems > 0),
        compiler_params=pltpu.CompilerParams(vmem_limit_bytes=VMEM_GRANT),
        cost_estimate=pl.CostEstimate(flops=flops, bytes_accessed=moved, transcendentals=0),
        name=name,
    )(
        *scalars,
        *(pltpu.with_memory_space_constraint(a, pltpu.VMEM) for a in arrays[:near]),
        *(pltpu.with_memory_space_constraint(a, pltpu.HBM) for a in arrays[near:]),
    )


def per_device_packed(
    grad_partial,
    owner,
    offset,
    left_factor,
    right_factor,
    left_basis,
    right_basis,
    momentum,
    second_moment,
):
    pieces = grad_partial[0]
    blocks, rows, columns = pieces.shape
    groups = lax.axis_size("mp")
    replicas = lax.axis_size("dp")
    col_share = columns // replicas
    share = lax.axis_index("dp").astype(jnp.int32).reshape(1)
    group = lax.axis_index("mp").astype(jnp.int32).reshape(1)
    bf16, f32 = jnp.bfloat16, jnp.float32
    shape = jax.ShapeDtypeStruct
    packed = shape((blocks, rows + 2 * SUBLANES, LANES), bf16)
    square = (columns, columns)
    lbasis, rbasis, moment, second = left_basis[0], right_basis[0], momentum[0], second_moment[0]
    left_t, right_t = left_factor[0].T, right_factor[0].T
    product = 2 * columns**3

    parts = run(
        "pack",
        pack_kernel,
        [share],
        [pieces],
        [packed] * replicas,
        scratch=[shape((blocks, rows, LANES // 2), bf16)],
        sems=replicas + 1,
        far=1,
    )
    parts = [parts[0]] + [
        lax.ppermute(parts[s], "dp", [(i, (i + s) % replicas) for i in range(replicas)])
        for s in range(1, replicas)
    ]
    lbasis_t, old_part, back_basis = run(
        "prepare",
        prepare_kernel,
        [group, share, owner],
        [lbasis, rbasis, moment],
        [shape(square, bf16), shape(square, f32), shape((columns, 2 * LANES), bf16)],
        scratch=[shape(square, bf16)] * 3,
        sems=3,
        far=3,
        flops=2 * product,
    )
    parts, lbasis_t, old_part, back_basis = lax.optimization_barrier(
        (parts, lbasis_t, old_part, back_basis)
    )
    (outgoing,) = run(
        "route",
        route_kernel,
        [owner, offset],
        parts,
        [shape((replicas * groups,) + packed.shape[1:], bf16)],
        scratch=[packed],
    )
    arrived = lax.all_to_all(outgoing, ("dp", "mp"), split_axis=0, concat_axis=0, tiled=True)
    chunks = shape((groups, rows + 2 * SUBLANES, LANES), bf16)
    factor_t = shape(left_t.shape, f32)
    gradient, moment, left_t, right_t, new_second, back = run(
        "owner_step",
        owner_kernel,
        [group, owner],
        [
            arrived, lbasis, rbasis, lbasis_t, old_part, back_basis, second, moment, left_t,
            right_t,
        ],
        [shape(square, bf16)] * 2 + [factor_t] * 2 + [shape(square, f32), chunks],
        scratch=[shape(square, bf16), chunks, shape(square, f32)],
        sems=groups + 5,
        far=3,
        far_outs=2,
        flops=3 * product,
    )
    returned = lax.all_to_all(
        back,
        "mp",
        split_axis=0,
        concat_axis=0,
        tiled=True,
        axis_index_groups=[list(range(groups))[::-1]],
    )
    new_moment, new_left_t, new_right_t = run(
        "factors",
        factor_kernel,
        [group, share, owner],
        [gradient, moment, left_t, right_t],
        [shape(square, bf16), factor_t, factor_t],
        scratch=[shape(square, bf16), factor_t, factor_t],
        sems=3,
        far_outs=3,
        flops=product,
    )
    (update,) = run(
        "place",
        place_kernel,
        [owner, offset],
        [returned],
        [shape((blocks, rows, col_share), bf16)],
        scratch=[shape((blocks, rows, col_share - LANES), bf16)],
        sems=2 * blocks,
        far_outs=1,
    )
    return (
        update,
        new_left_t.T[None],
        new_right_t.T[None],
        new_moment[None],
        new_second[None],
    )


def per_device(grad_partial, *rest):
    _, _, rows, columns = grad_partial.shape
    fits = packed_fits(rows, columns, lax.axis_size("dp"))
    return (per_device_packed if fits else per_device_general)(grad_partial, *rest)


def per_device_general(
    grad_partial,
    owner,
    offset,
    left_factor,
    right_factor,
    left_basis,
    right_basis,
    momentum,
    second_moment,
):
    pieces = grad_partial[0]
    blocks, row_count, columns = pieces.shape
    groups = lax.axis_size("mp")
    replicas = lax.axis_size("dp")
    col_share = columns // replicas
    column = lax.axis_index("dp") * col_share
    my_group = lax.axis_index("mp")
    targets = lax.broadcasted_iota(jnp.int32, (groups, blocks), 0)
    positions = lax.broadcasted_iota(jnp.int32, (blocks, blocks), 0)
    routing = (owner[None, :] == targets).astype(jnp.float32)
    where_at = (offset[None, :] == positions).astype(jnp.float32)
    select = contract_last(routing, where_at).astype(jnp.bfloat16)
    occupied = jnp.any(owner == my_group)
    swapped = lax.all_to_all(grad_partial, "dp", split_axis=3, concat_axis=0, tiled=True)
    summed = jnp.sum(swapped.astype(jnp.float32), axis=0).astype(jnp.bfloat16)
    outgoing = jnp.dot(
        select, summed.reshape(blocks, row_count * col_share), preferred_element_type=jnp.float32
    )
    outgoing = outgoing.astype(jnp.bfloat16).reshape(groups, row_count, col_share)
    landed = lax.all_to_all(outgoing, "mp", split_axis=0, concat_axis=0, tiled=True)
    arrived = lax.all_gather(landed, "dp", axis=2, tiled=True)
    gradient = arrived.reshape(groups * row_count, columns)

    def refresh(operands):
        grad_in, left_fac, right_fac, lbasis, rbasis, moment, second = operands
        grad_rows = lax.dynamic_slice_in_dim(grad_in, column, col_share, 0)
        grad_cols = lax.dynamic_slice_in_dim(grad_in, column, col_share, 1)
        new_left = 0.95 * left_fac + 0.05 * contract_last(grad_in, grad_rows)
        new_right = 0.95 * right_fac + 0.05 * contract_first(grad_in, grad_cols)
        new_moment = (0.9 * moment.astype(jnp.float32) + 0.1 * grad_in.astype(jnp.float32)).astype(
            jnp.bfloat16
        )
        turned = contract_first(lbasis, grad_in).astype(jnp.bfloat16)
        rotated = jnp.dot(turned, rbasis, preferred_element_type=jnp.float32)
        turned_mom = contract_first(lbasis, new_moment).astype(jnp.bfloat16)
        rotated_mom = jnp.dot(turned_mom, rbasis, preferred_element_type=jnp.float32)
        new_second = 0.95 * second + 0.05 * rotated * rotated
        scaled = (rotated_mom / (jnp.sqrt(new_second) + 1e-08)).astype(jnp.bfloat16)
        unrotated = jnp.dot(lbasis, scaled, preferred_element_type=jnp.float32).astype(jnp.bfloat16)
        back_rows = lax.dynamic_slice_in_dim(rbasis, column, col_share, 0)
        return (new_left, new_right, new_moment, new_second, contract_last(unrotated, back_rows))

    def keep_old(operands):
        grad_in, left_fac, right_fac, lbasis, rbasis, moment, second = operands
        return (left_fac, right_fac, moment, second, jnp.zeros((columns, col_share), jnp.float32))

    operands = (
        gradient,
        left_factor[0],
        right_factor[0],
        left_basis[0],
        right_basis[0],
        momentum[0],
        second_moment[0],
    )
    new_left, new_right, new_moment, new_second, turned_cols = lax.cond(
        occupied, refresh, keep_old, operands
    )
    outgoing_back = turned_cols.astype(jnp.bfloat16).reshape(groups, row_count, col_share)
    returned = lax.all_to_all(outgoing_back, "mp", split_axis=0, concat_axis=0, tiled=True)
    update = contract_first(select, returned.reshape(groups, row_count * col_share)).astype(
        jnp.bfloat16
    )
    update = update.reshape(blocks, row_count, col_share)
    return (update, new_left[None], new_right[None], new_moment[None], new_second[None])


def solution(mesh):
    placed = (
        P("dp", None, "mp", None),
        P(),
        P(),
        P("mp", None, "dp"),
        P("mp", None, "dp"),
        P("mp", None, None),
        P("mp", None, None),
        P("mp", None, None),
        P("mp", None, None),
    )
    return jax.shard_map(
        per_device,
        mesh=mesh,
        in_specs=placed,
        out_specs=(
            P(None, "mp", "dp"),
            P("mp", None, "dp"),
            P("mp", None, "dp"),
            P("mp", None, None),
            P("mp", None, None),
        ),
        check_vma=False,
    )
```

```python
import jax
import jax.numpy as jnp
from jax import lax
from jax.experimental import pallas as pl
from jax.experimental.pallas import tpu as pltpu
from jax.sharding import PartitionSpec as P

LANES = 128
SUBLANES = 8
VMEM = pl.BlockSpec(memory_space=pltpu.VMEM)
SMEM = pl.BlockSpec(memory_space=pltpu.SMEM)
FAR = pl.BlockSpec(memory_space=pltpu.HBM)
VMEM_GRANT = 16 * 2**20
CUT = 2 * LANES
STRIP = 48

def contract_first(matrix_a, matrix_b):
    return lax.dot_general(
        matrix_a, matrix_b, (((0,), (0,)), ((), ())), preferred_element_type=jnp.float32
    )


def contract_last(matrix_a, matrix_b):
    return lax.dot_general(
        matrix_a, matrix_b, (((1,), (1,)), ((), ())), preferred_element_type=jnp.float32
    )


def matmul(matrix_a, matrix_b):
    return jnp.dot(matrix_a, matrix_b, preferred_element_type=jnp.float32)


def tail_start(share):
    return jnp.where(share == 0, 0, 2 * share + 1) if not isinstance(share, int) else (
        0 if share == 0 else 2 * share + 1
    )


def packed_fits(rows, columns, replicas):
    width = columns // replicas - LANES
    return (
        columns == replicas * LANES + LANES // 2
        and rows == (2 * replicas + 1) * SUBLANES
        and width * replicas == LANES // 2
        and width % 16 == 0
        and LANES // width == rows // SUBLANES - 1
    )


def pack_kernel(me_ref, grad_hbm, *refs):
    outs, last, sems = refs[:-2], refs[-2], refs[-1]
    replicas = len(outs)
    blocks, rows, columns = grad_hbm.shape
    half = LANES // 2
    copies = [pltpu.make_async_copy(grad_hbm.at[:, :, columns - half :], last, sems.at[replicas])]
    for step in range(replicas):
        share = lax.rem(me_ref[0] + step, replicas)
        col = pl.multiple_of(share * LANES, LANES)
        copies.append(
            pltpu.make_async_copy(
                grad_hbm.at[:, :, pl.ds(col, LANES)], outs[step].at[:, :rows, :], sems.at[step]
            )
        )
    for copy in copies:
        copy.start()
    copies[0].wait()
    for step in range(replicas):
        share = lax.rem(me_ref[0] + step, replicas)
        start = tail_start(share)
        row = pl.multiple_of(start * SUBLANES, SUBLANES)
        row_next = pl.multiple_of(row + SUBLANES, SUBLANES)
        row_third = pl.multiple_of(
            jnp.minimum(start + 2, rows // SUBLANES - 1) * SUBLANES, SUBLANES
        )
        out = outs[step]
        for b in range(blocks):
            out[b, rows : rows + SUBLANES, :half] = last[b, pl.ds(row, SUBLANES), :]
            out[b, rows + SUBLANES :, :half] = last[b, pl.ds(row_next, SUBLANES), :]
            out[b, rows : rows + SUBLANES, half:] = last[b, pl.ds(row_third, SUBLANES), :]
            out[b, rows + SUBLANES :, half:] = jnp.zeros((SUBLANES, half), out.dtype)
    for copy in copies[1:]:
        copy.wait()


SHARE, GROUP, FOUND, SLOTS = 0, 1, 2, 3


def table_kernel(share_ref, group_ref, owner_ref, offset_ref, table):
    blocks = owner_ref.shape[0]
    groups = table.shape[0] - SLOTS - blocks
    table[SHARE] = share_ref[0]
    table[GROUP] = group_ref[0]
    found = jnp.int32(0)
    for b in range(blocks):
        found = jnp.where(owner_ref[b] == group_ref[0], 1, found)
    table[FOUND] = found
    for group in range(groups):
        table[SLOTS + group] = jnp.int32(0)
    for b in range(blocks):
        table[SLOTS + owner_ref[b]] = offset_ref[b]
        table[SLOTS + groups + offset_ref[b]] = groups - 1 - owner_ref[b]


def route_kernel(table, *refs):
    parts, out, summed = refs[:-2], refs[-2], refs[-1]
    replicas = len(parts)
    groups = out.shape[0] // replicas
    blocks = summed.shape[0]
    for b in range(blocks):
        total = parts[0][b].astype(jnp.float32)
        for part in parts[1:]:
            total = total + part[b].astype(jnp.float32)
        summed[b] = total.astype(jnp.bfloat16)
    for group in range(groups):
        piece = summed[table[SLOTS + group]]
        for r in range(replicas):
            out[r * groups + group] = piece


def prepare_kernel(
    table, lbasis_hbm, rbasis_hbm, moment_hbm,
    lbasis_t, old_part, back_basis, lbasis, rbasis, moment, sems,
):
    found = table[FOUND]

    @pl.when(found == 1)
    def _():
        copies = [
            pltpu.make_async_copy(source, target, sems.at[n])
            for n, (source, target) in enumerate(
                ((lbasis_hbm, lbasis), (moment_hbm, moment), (rbasis_hbm, rbasis))
            )
        ]
        for copy in copies:
            copy.start()
        copies[0].wait()
        transposed = lbasis[...].T
        lbasis_t[...] = transposed
        copies[1].wait()
        turned = matmul(transposed, moment[...]).astype(jnp.bfloat16)
        copies[2].wait()
        old_part[...] = 0.9 * matmul(turned, rbasis[...])
        columns = rbasis.shape[0]
        col_share = columns // (columns // LANES)
        tail = col_share - LANES
        first = pl.multiple_of(table[SHARE] * col_share, tail)
        main = rbasis[pl.ds(first, LANES), :]
        last = rbasis[pl.ds(pl.multiple_of(first + LANES, tail), tail), :]
        back_basis[...] = jnp.concatenate([main] + [last] * (LANES // tail), axis=0).T


def assemble(arrived, gradient, groups, rows):
    half = LANES // 2
    tail = gradient.shape[1] - half
    for r in range(arrived.shape[0] // groups):
        start = tail_start(r)
        for m in range(groups):
            piece = r * groups + m
            base = m * rows
            gradient[base : base + rows, r * LANES : (r + 1) * LANES] = arrived[piece, :rows, :]
            for g in range(3 if r == 0 else 2):
                row = base + (start + g) * SUBLANES
                below = rows + (g % 2) * SUBLANES
                beside = (g // 2) * half
                gradient[row : row + SUBLANES, tail:] = arrived[
                    piece, below : below + SUBLANES, beside : beside + half
                ]


def owner_kernel(
    table, arrived, lbasis, rbasis, lbasis_t, old_part, back_basis, second,
    moment_hbm, left_hbm, right_hbm,
    gradient, moment, left_t, right_t, second_out, back_out,
    turned, back, new_second, sems,
):
    found = table[FOUND]
    groups = back.shape[0]
    copies = [
        pltpu.make_async_copy(back.at[n], back_out.at[n], sems.at[n]) for n in range(groups)
    ]
    loads = [
        pltpu.make_async_copy(source, target, sems.at[groups + n])
        for n, (source, target) in enumerate(
            ((moment_hbm, moment), (left_hbm, left_t), (right_hbm, right_t))
        )
    ]
    fresh_copy = pltpu.make_async_copy(new_second, second_out, sems.at[groups + 3])
    kept_copy = pltpu.make_async_copy(second, second_out, sems.at[groups + 4])
    for load in loads:
        load.start()
    columns = gradient.shape[1]
    rows = columns // groups

    @pl.when(found == 1)
    def _():
        assemble(arrived, gradient, groups, rows)
        turned[...] = matmul(lbasis_t[...], gradient[...]).astype(jnp.bfloat16)
        total = None
        for low in range(0, columns, CUT):
            cols = slice(low, min(low + CUT, columns))
            rotated = matmul(turned[...], rbasis[:, cols])
            fresh = 0.95 * second[:, cols] + 0.05 * rotated * rotated
            new_second[:, cols] = fresh
            rotated_mom = old_part[:, cols] + 0.1 * rotated
            spread = fresh * lax.rsqrt(fresh) + 1e-08
            scaled = (rotated_mom * lax.rsqrt(spread * spread)).astype(jnp.bfloat16)
            term = matmul(scaled, back_basis[cols, :])
            total = term if total is None else total + term
        fresh_copy.start()
        result = matmul(lbasis[...], total.astype(jnp.bfloat16))
        lane = lax.broadcasted_iota(jnp.int32, (SUBLANES, LANES), 1)
        tail_groups = rows // SUBLANES - 1
        width = LANES // tail_groups
        for m in range(groups):
            base = m * rows
            back[groups - 1 - m, :rows, :] = result[base : base + rows, :LANES].astype(jnp.bfloat16)
            mixed = result[base : base + SUBLANES, LANES:]
            for g in range(1, tail_groups):
                row = base + g * SUBLANES
                mixed = jnp.where(
                    lane < g * width, mixed, result[row : row + SUBLANES, LANES:]
                )
            back[groups - 1 - m, rows : rows + SUBLANES, :] = mixed.astype(jnp.bfloat16)
            back[groups - 1 - m, rows + SUBLANES :, :] = result[
                base + rows - SUBLANES : base + rows, LANES:
            ].astype(jnp.bfloat16)
        for copy in copies:
            copy.start()
        for copy in copies + [fresh_copy]:
            copy.wait()

    @pl.when(found == 0)
    def _():
        kept_copy.start()
        kept_copy.wait()

    for load in loads:
        load.wait()


def factor_kernel(
    table, gradient, moment, left_t, right_t,
    moment_out, left_out, right_out, new_moment, new_left_t, new_right_t, sems,
):
    found = table[FOUND]
    col_share, columns = left_t.shape
    outs = (moment_out, left_out, right_out)
    fresh, kept = (
        [pltpu.make_async_copy(a, b, sems.at[n]) for n, (a, b) in enumerate(zip(sources, outs))]
        for sources in ((new_moment, new_left_t, new_right_t), (moment, left_t, right_t))
    )

    @pl.when(found == 1)
    def _():
        for low in range(0, columns, STRIP):
            strip = slice(low, min(low + STRIP, columns))
            new_moment[strip, :] = (
                0.9 * moment[strip, :].astype(jnp.float32)
                + 0.1 * gradient[strip, :].astype(jnp.float32)
            ).astype(jnp.bfloat16)
        fresh[0].start()
        first = pl.multiple_of(table[SHARE] * col_share, 16)
        grad = gradient[...]
        new_left_t[...] = 0.95 * left_t[...] + 0.05 * contract_last(
            gradient[pl.ds(first, col_share), :], grad
        )
        picked = lax.broadcasted_iota(jnp.int32, (col_share, columns), 0) + first
        places = lax.broadcasted_iota(jnp.int32, (col_share, columns), 1)
        pick = jnp.where(picked == places, 1.0, 0.0).astype(jnp.bfloat16)
        grad_cols_t = contract_last(pick, grad).astype(jnp.bfloat16)
        new_right_t[...] = 0.95 * right_t[...] + 0.05 * matmul(grad_cols_t, grad)
        for copy in fresh[1:]:
            copy.start()
        for copy in fresh:
            copy.wait()

    @pl.when(found == 0)
    def _():
        for copy in kept:
            copy.start()
        for copy in kept:
            copy.wait()


def place_kernel(table, returned, update, tails, sems):
    blocks, rows, col_share = update.shape
    groups = returned.shape[0]
    tail_groups = rows // SUBLANES - 1
    width = col_share - LANES
    copies = []
    for place in range(blocks):
        slot = table[SLOTS + groups + place]
        copies.append(
            pltpu.make_async_copy(
                returned.at[slot, :rows], update.at[place, :, :LANES], sems.at[place]
            )
        )
        copies[-1].start()
    for place in range(blocks):
        slot = table[SLOTS + groups + place]
        for g in range(tail_groups):
            tails[place, g * SUBLANES : (g + 1) * SUBLANES, :] = returned[
                slot, rows : rows + SUBLANES, g * width : (g + 1) * width
            ]
        tails[place, rows - SUBLANES :, :] = returned[slot, rows + SUBLANES :, :width]
        copies.append(
            pltpu.make_async_copy(
                tails.at[place], update.at[place, :, LANES:], sems.at[blocks + place]
            )
        )
        copies[-1].start()
    for copy in copies:
        copy.wait()


def run(name, kernel, scalars, arrays, outs, scratch=(), flops=0, sems=0, far=0, far_outs=0):
    moved = sum(a.size * a.dtype.itemsize for a in list(arrays) + list(outs))
    near = len(arrays) - far
    near_outs = len(outs) - far_outs
    return pl.pallas_call(
        kernel,
        out_shape=[pltpu.VMEM(o.shape, o.dtype) for o in outs[:near_outs]]
        + [pltpu.HBM(o.shape, o.dtype) for o in outs[near_outs:]],
        in_specs=[SMEM] * len(scalars) + [VMEM] * near + [FAR] * far,
        out_specs=[VMEM] * near_outs + [FAR] * far_outs,
        scratch_shapes=[pltpu.VMEM(o.shape, o.dtype) for o in scratch]
        + [pltpu.SemaphoreType.DMA((sems,))] * (sems > 0),
        compiler_params=pltpu.CompilerParams(vmem_limit_bytes=VMEM_GRANT),
        cost_estimate=pl.CostEstimate(flops=flops, bytes_accessed=moved, transcendentals=0),
        name=name,
    )(
        *scalars,
        *(pltpu.with_memory_space_constraint(a, pltpu.VMEM) for a in arrays[:near]),
        *(pltpu.with_memory_space_constraint(a, pltpu.HBM) for a in arrays[near:]),
    )


def per_device_packed(
    grad_partial,
    owner,
    offset,
    left_factor,
    right_factor,
    left_basis,
    right_basis,
    momentum,
    second_moment,
):
    pieces = grad_partial[0]
    blocks, rows, columns = pieces.shape
    groups = lax.axis_size("mp")
    replicas = lax.axis_size("dp")
    col_share = columns // replicas
    share = lax.axis_index("dp").astype(jnp.int32).reshape(1)
    group = lax.axis_index("mp").astype(jnp.int32).reshape(1)
    bf16, f32 = jnp.bfloat16, jnp.float32
    shape = jax.ShapeDtypeStruct
    packed = shape((blocks, rows + 2 * SUBLANES, LANES), bf16)
    square = (columns, columns)
    lbasis, rbasis, moment, second = left_basis[0], right_basis[0], momentum[0], second_moment[0]
    left_t, right_t = left_factor[0].T, right_factor[0].T
    product = 2 * columns**3

    parts = run(
        "pack",
        pack_kernel,
        [share],
        [pieces],
        [packed] * replicas,
        scratch=[shape((blocks, rows, LANES // 2), bf16)],
        sems=replicas + 1,
        far=1,
    )
    parts = [parts[0]] + [
        lax.ppermute(parts[s], "dp", [(i, (i + s) % replicas) for i in range(replicas)])
        for s in range(1, replicas)
    ]
    table = pl.pallas_call(
        table_kernel,
        out_shape=pltpu.SMEM((SLOTS + groups + blocks,), jnp.int32),
        in_specs=[SMEM] * 4,
        out_specs=SMEM,
        name="table",
    )(share, group, owner, offset)
    lbasis_t, old_part, back_basis = run(
        "prepare",
        prepare_kernel,
        [table],
        [lbasis, rbasis, moment],
        [shape(square, bf16), shape(square, f32), shape((columns, 2 * LANES), bf16)],
        scratch=[shape(square, bf16)] * 3,
        sems=3,
        far=3,
        flops=2 * product,
    )
    parts, lbasis_t, old_part, back_basis = lax.optimization_barrier(
        (parts, lbasis_t, old_part, back_basis)
    )
    (outgoing,) = run(
        "route",
        route_kernel,
        [table],
        parts,
        [shape((replicas * groups,) + packed.shape[1:], bf16)],
        scratch=[packed],
    )
    arrived = lax.all_to_all(outgoing, ("dp", "mp"), split_axis=0, concat_axis=0, tiled=True)
    chunks = shape((groups, rows + 2 * SUBLANES, LANES), bf16)
    factor_t = shape(left_t.shape, f32)
    gradient, moment, left_t, right_t, new_second, back = run(
        "owner_step",
        owner_kernel,
        [table],
        [
            arrived, lbasis, rbasis, lbasis_t, old_part, back_basis, second, moment, left_t,
            right_t,
        ],
        [shape(square, bf16)] * 2 + [factor_t] * 2 + [shape(square, f32), chunks],
        scratch=[shape(square, bf16), chunks, shape(square, f32)],
        sems=groups + 5,
        far=3,
        far_outs=2,
        flops=3 * product,
    )
    returned = lax.all_to_all(
        back,
        "mp",
        split_axis=0,
        concat_axis=0,
        tiled=True,
        axis_index_groups=[list(range(groups))[::-1]],
    )
    new_moment, new_left_t, new_right_t = run(
        "factors",
        factor_kernel,
        [table],
        [gradient, moment, left_t, right_t],
        [shape(square, bf16), factor_t, factor_t],
        scratch=[shape(square, bf16), factor_t, factor_t],
        sems=3,
        far_outs=3,
        flops=product,
    )
    (update,) = run(
        "place",
        place_kernel,
        [table],
        [returned],
        [shape((blocks, rows, col_share), bf16)],
        scratch=[shape((blocks, rows, col_share - LANES), bf16)],
        sems=2 * blocks,
        far_outs=1,
    )
    return (
        update,
        new_left_t.T[None],
        new_right_t.T[None],
        new_moment[None],
        new_second[None],
    )


def per_device(grad_partial, *rest):
    _, _, rows, columns = grad_partial.shape
    fits = packed_fits(rows, columns, lax.axis_size("dp"))
    return (per_device_packed if fits else per_device_general)(grad_partial, *rest)


def per_device_general(
    grad_partial,
    owner,
    offset,
    left_factor,
    right_factor,
    left_basis,
    right_basis,
    momentum,
    second_moment,
):
    pieces = grad_partial[0]
    blocks, row_count, columns = pieces.shape
    groups = lax.axis_size("mp")
    replicas = lax.axis_size("dp")
    col_share = columns // replicas
    column = lax.axis_index("dp") * col_share
    my_group = lax.axis_index("mp")
    targets = lax.broadcasted_iota(jnp.int32, (groups, blocks), 0)
    positions = lax.broadcasted_iota(jnp.int32, (blocks, blocks), 0)
    routing = (owner[None, :] == targets).astype(jnp.float32)
    where_at = (offset[None, :] == positions).astype(jnp.float32)
    select = contract_last(routing, where_at).astype(jnp.bfloat16)
    occupied = jnp.any(owner == my_group)
    swapped = lax.all_to_all(grad_partial, "dp", split_axis=3, concat_axis=0, tiled=True)
    summed = jnp.sum(swapped.astype(jnp.float32), axis=0).astype(jnp.bfloat16)
    outgoing = jnp.dot(
        select, summed.reshape(blocks, row_count * col_share), preferred_element_type=jnp.float32
    )
    outgoing = outgoing.astype(jnp.bfloat16).reshape(groups, row_count, col_share)
    landed = lax.all_to_all(outgoing, "mp", split_axis=0, concat_axis=0, tiled=True)
    arrived = lax.all_gather(landed, "dp", axis=2, tiled=True)
    gradient = arrived.reshape(groups * row_count, columns)

    def refresh(operands):
        grad_in, left_fac, right_fac, lbasis, rbasis, moment, second = operands
        grad_rows = lax.dynamic_slice_in_dim(grad_in, column, col_share, 0)
        grad_cols = lax.dynamic_slice_in_dim(grad_in, column, col_share, 1)
        new_left = 0.95 * left_fac + 0.05 * contract_last(grad_in, grad_rows)
        new_right = 0.95 * right_fac + 0.05 * contract_first(grad_in, grad_cols)
        new_moment = (0.9 * moment.astype(jnp.float32) + 0.1 * grad_in.astype(jnp.float32)).astype(
            jnp.bfloat16
        )
        turned = contract_first(lbasis, grad_in).astype(jnp.bfloat16)
        rotated = jnp.dot(turned, rbasis, preferred_element_type=jnp.float32)
        turned_mom = contract_first(lbasis, new_moment).astype(jnp.bfloat16)
        rotated_mom = jnp.dot(turned_mom, rbasis, preferred_element_type=jnp.float32)
        new_second = 0.95 * second + 0.05 * rotated * rotated
        scaled = (rotated_mom / (jnp.sqrt(new_second) + 1e-08)).astype(jnp.bfloat16)
        unrotated = jnp.dot(lbasis, scaled, preferred_element_type=jnp.float32).astype(jnp.bfloat16)
        back_rows = lax.dynamic_slice_in_dim(rbasis, column, col_share, 0)
        return (new_left, new_right, new_moment, new_second, contract_last(unrotated, back_rows))

    def keep_old(operands):
        grad_in, left_fac, right_fac, lbasis, rbasis, moment, second = operands
        return (left_fac, right_fac, moment, second, jnp.zeros((columns, col_share), jnp.float32))

    operands = (
        gradient,
        left_factor[0],
        right_factor[0],
        left_basis[0],
        right_basis[0],
        momentum[0],
        second_moment[0],
    )
    new_left, new_right, new_moment, new_second, turned_cols = lax.cond(
        occupied, refresh, keep_old, operands
    )
    outgoing_back = turned_cols.astype(jnp.bfloat16).reshape(groups, row_count, col_share)
    returned = lax.all_to_all(outgoing_back, "mp", split_axis=0, concat_axis=0, tiled=True)
    update = contract_first(select, returned.reshape(groups, row_count * col_share)).astype(
        jnp.bfloat16
    )
    update = update.reshape(blocks, row_count, col_share)
    return (update, new_left[None], new_right[None], new_moment[None], new_second[None])


def solution(mesh):
    placed = (
        P("dp", None, "mp", None),
        P(),
        P(),
        P("mp", None, "dp"),
        P("mp", None, "dp"),
        P("mp", None, None),
        P("mp", None, None),
        P("mp", None, None),
        P("mp", None, None),
    )
    return jax.shard_map(
        per_device,
        mesh=mesh,
        in_specs=placed,
        out_specs=(
            P(None, "mp", "dp"),
            P("mp", None, "dp"),
            P("mp", None, "dp"),
            P("mp", None, None),
            P("mp", None, None),
        ),
        check_vma=False,
    )
```

```python
import jax
import jax.numpy as jnp
from jax import lax
from jax.experimental import pallas as pl
from jax.experimental.pallas import tpu as pltpu
from jax.sharding import PartitionSpec as P

LANES = 128
SUBLANES = 8
VMEM = pl.BlockSpec(memory_space=pltpu.VMEM)
SMEM = pl.BlockSpec(memory_space=pltpu.SMEM)
FAR = pl.BlockSpec(memory_space=pltpu.HBM)
VMEM_GRANT = 16 * 2**20
CUT = 2 * LANES
STRIP = 48

def contract_first(matrix_a, matrix_b):
    return lax.dot_general(
        matrix_a, matrix_b, (((0,), (0,)), ((), ())), preferred_element_type=jnp.float32
    )


def contract_last(matrix_a, matrix_b):
    return lax.dot_general(
        matrix_a, matrix_b, (((1,), (1,)), ((), ())), preferred_element_type=jnp.float32
    )


def matmul(matrix_a, matrix_b):
    return jnp.dot(matrix_a, matrix_b, preferred_element_type=jnp.float32)


def tail_start(share):
    return jnp.where(share == 0, 0, 2 * share + 1) if not isinstance(share, int) else (
        0 if share == 0 else 2 * share + 1
    )


def packed_fits(rows, columns, replicas):
    width = columns // replicas - LANES
    return (
        columns == replicas * LANES + LANES // 2
        and rows == (2 * replicas + 1) * SUBLANES
        and width * replicas == LANES // 2
        and width % 16 == 0
        and LANES // width == rows // SUBLANES - 1
    )


def pack_kernel(me_ref, grad_hbm, *refs):
    outs, last, sems = refs[:-2], refs[-2], refs[-1]
    replicas = len(outs)
    blocks, rows, columns = grad_hbm.shape
    half = LANES // 2
    copies = [pltpu.make_async_copy(grad_hbm.at[:, :, columns - half :], last, sems.at[replicas])]
    for step in range(replicas):
        share = lax.rem(me_ref[0] + step, replicas)
        col = pl.multiple_of(share * LANES, LANES)
        copies.append(
            pltpu.make_async_copy(
                grad_hbm.at[:, :, pl.ds(col, LANES)], outs[step].at[:, :rows, :], sems.at[step]
            )
        )
    for copy in copies:
        copy.start()
    copies[0].wait()
    for step in range(replicas):
        share = lax.rem(me_ref[0] + step, replicas)
        start = tail_start(share)
        row = pl.multiple_of(start * SUBLANES, SUBLANES)
        row_next = pl.multiple_of(row + SUBLANES, SUBLANES)
        row_third = pl.multiple_of(
            jnp.minimum(start + 2, rows // SUBLANES - 1) * SUBLANES, SUBLANES
        )
        out = outs[step]
        for b in range(blocks):
            out[b, rows : rows + SUBLANES, :half] = last[b, pl.ds(row, SUBLANES), :]
            out[b, rows + SUBLANES :, :half] = last[b, pl.ds(row_next, SUBLANES), :]
            out[b, rows : rows + SUBLANES, half:] = last[b, pl.ds(row_third, SUBLANES), :]
            out[b, rows + SUBLANES :, half:] = jnp.zeros((SUBLANES, half), out.dtype)
    for copy in copies[1:]:
        copy.wait()


SHARE, GROUP, FOUND, SLOTS = 0, 1, 2, 3


def table_kernel(share_ref, group_ref, owner_ref, offset_ref, table):
    blocks = owner_ref.shape[0]
    groups = table.shape[0] - SLOTS - blocks
    table[SHARE] = share_ref[0]
    table[GROUP] = group_ref[0]
    found = jnp.int32(0)
    for b in range(blocks):
        found = jnp.where(owner_ref[b] == group_ref[0], 1, found)
    table[FOUND] = found
    for group in range(groups):
        table[SLOTS + group] = jnp.int32(0)
    for b in range(blocks):
        table[SLOTS + owner_ref[b]] = offset_ref[b]
        table[SLOTS + groups + offset_ref[b]] = groups - 1 - owner_ref[b]


def route_kernel(table, *refs):
    parts, out, summed = refs[:-2], refs[-2], refs[-1]
    replicas = len(parts)
    groups = out.shape[0] // replicas
    blocks = summed.shape[0]
    for b in range(blocks):
        total = parts[0][b].astype(jnp.float32)
        for part in parts[1:]:
            total = total + part[b].astype(jnp.float32)
        summed[b] = total.astype(jnp.bfloat16)
    for group in range(groups):
        piece = summed[table[SLOTS + group]]
        for r in range(replicas):
            out[r * groups + group] = piece


def prepare_kernel(
    table, lbasis_hbm, rbasis_hbm, moment_hbm,
    lbasis_t, old_part, back_basis, lbasis, rbasis, moment, sems,
):
    found = table[FOUND]

    @pl.when(found == 1)
    def _():
        copies = [
            pltpu.make_async_copy(source, target, sems.at[n])
            for n, (source, target) in enumerate(
                ((lbasis_hbm, lbasis), (moment_hbm, moment), (rbasis_hbm, rbasis))
            )
        ]
        for copy in copies:
            copy.start()
        copies[0].wait()
        transposed = lbasis[...].T
        lbasis_t[...] = transposed
        copies[1].wait()
        turned = matmul(transposed, moment[...]).astype(jnp.bfloat16)
        copies[2].wait()
        old_part[...] = 0.9 * matmul(turned, rbasis[...])
        columns = rbasis.shape[0]
        col_share = columns // (columns // LANES)
        tail = col_share - LANES
        first = pl.multiple_of(table[SHARE] * col_share, tail)
        main = rbasis[pl.ds(first, LANES), :]
        last = rbasis[pl.ds(pl.multiple_of(first + LANES, tail), tail), :]
        back_basis[...] = jnp.concatenate([main] + [last] * (LANES // tail), axis=0).T


def assemble(arrived, gradient, groups, rows):
    half = LANES // 2
    tail = gradient.shape[1] - half
    for r in range(arrived.shape[0] // groups):
        start = tail_start(r)
        for m in range(groups):
            piece = r * groups + m
            base = m * rows
            gradient[base : base + rows, r * LANES : (r + 1) * LANES] = arrived[piece, :rows, :]
            for g in range(3 if r == 0 else 2):
                row = base + (start + g) * SUBLANES
                below = rows + (g % 2) * SUBLANES
                beside = (g // 2) * half
                gradient[row : row + SUBLANES, tail:] = arrived[
                    piece, below : below + SUBLANES, beside : beside + half
                ]


def owner_kernel(
    table, arrived, lbasis, rbasis, lbasis_t, old_part, back_basis, second,
    gradient, new_second, back_out, turned, scaled, back, sems,
):
    found = table[FOUND]
    groups = back.shape[0]
    copies = [
        pltpu.make_async_copy(back.at[n], back_out.at[n], sems.at[n]) for n in range(groups)
    ]
    columns = gradient.shape[1]
    rows = columns // groups

    @pl.when(found == 1)
    def _():
        assemble(arrived, gradient, groups, rows)
        turned[...] = matmul(lbasis_t[...], gradient[...]).astype(jnp.bfloat16)
        for low in range(0, columns, CUT):
            cols = slice(low, min(low + CUT, columns))
            rotated = matmul(turned[...], rbasis[:, cols])
            fresh = 0.95 * second[:, cols] + 0.05 * rotated * rotated
            new_second[:, cols] = fresh
            rotated_mom = old_part[:, cols] + 0.1 * rotated
            spread = fresh * lax.rsqrt(fresh) + 1e-08
            scaled[:, cols] = (rotated_mom * lax.rsqrt(spread * spread)).astype(jnp.bfloat16)
        total = matmul(scaled[...], back_basis[...])
        result = matmul(lbasis[...], total.astype(jnp.bfloat16))
        lane = lax.broadcasted_iota(jnp.int32, (SUBLANES, LANES), 1)
        tail_groups = rows // SUBLANES - 1
        width = LANES // tail_groups
        for m in range(groups):
            base = m * rows
            back[groups - 1 - m, :rows, :] = result[base : base + rows, :LANES].astype(jnp.bfloat16)
            mixed = result[base : base + SUBLANES, LANES:]
            for g in range(1, tail_groups):
                row = base + g * SUBLANES
                mixed = jnp.where(
                    lane < g * width, mixed, result[row : row + SUBLANES, LANES:]
                )
            back[groups - 1 - m, rows : rows + SUBLANES, :] = mixed.astype(jnp.bfloat16)
            back[groups - 1 - m, rows + SUBLANES :, :] = result[
                base + rows - SUBLANES : base + rows, LANES:
            ].astype(jnp.bfloat16)
        for copy in copies:
            copy.start()
        for copy in copies:
            copy.wait()

    @pl.when(found == 0)
    def _():
        new_second[...] = second[...]


def factor_kernel(
    table, gradient, second, moment_hbm, left_hbm, right_hbm,
    second_out, moment_out, left_out, right_out,
    moment, left_t, right_t, new_moment, new_left_t, new_right_t, sems,
):
    found = table[FOUND]
    col_share, columns = left_t.shape
    held = (moment, left_t, right_t)
    outs = (moment_out, left_out, right_out)

    def copies_of(first, sources, targets):
        return [
            pltpu.make_async_copy(a, b, sems.at[first + n])
            for n, (a, b) in enumerate(zip(sources, targets))
        ]

    loads = copies_of(0, (left_hbm, right_hbm, moment_hbm), (left_t, right_t, moment))
    fresh = copies_of(3, (new_left_t, new_right_t, new_moment), (left_out, right_out, moment_out))
    kept = copies_of(6, held, outs)
    second_copy = pltpu.make_async_copy(second, second_out, sems.at[9])
    for copy in loads + [second_copy]:
        copy.start()

    @pl.when(found == 1)
    def _():
        first = pl.multiple_of(table[SHARE] * col_share, 16)
        grad = gradient[...]
        left_term = 0.05 * contract_last(gradient[pl.ds(first, col_share), :], grad)
        picked = lax.broadcasted_iota(jnp.int32, (col_share, columns), 0) + first
        places = lax.broadcasted_iota(jnp.int32, (col_share, columns), 1)
        pick = jnp.where(picked == places, 1.0, 0.0).astype(jnp.bfloat16)
        grad_cols_t = contract_last(pick, grad).astype(jnp.bfloat16)
        right_term = 0.05 * matmul(grad_cols_t, grad)
        for copy in loads:
            copy.wait()
        new_left_t[...] = 0.95 * left_t[...] + left_term
        new_right_t[...] = 0.95 * right_t[...] + right_term
        for low in range(0, columns, STRIP):
            strip = slice(low, min(low + STRIP, columns))
            new_moment[strip, :] = (
                0.9 * moment[strip, :].astype(jnp.float32)
                + 0.1 * gradient[strip, :].astype(jnp.float32)
            ).astype(jnp.bfloat16)
        for copy in fresh:
            copy.start()
        for copy in fresh:
            copy.wait()

    @pl.when(found == 0)
    def _():
        for copy in loads:
            copy.wait()
        for copy in kept:
            copy.start()
        for copy in kept:
            copy.wait()

    second_copy.wait()


def place_kernel(table, returned, update, tails, sems):
    blocks, rows, col_share = update.shape
    groups = returned.shape[0]
    tail_groups = rows // SUBLANES - 1
    width = col_share - LANES
    copies = []
    for place in range(blocks):
        slot = table[SLOTS + groups + place]
        copies.append(
            pltpu.make_async_copy(
                returned.at[slot, :rows], update.at[place, :, :LANES], sems.at[place]
            )
        )
        copies[-1].start()
    for place in range(blocks):
        slot = table[SLOTS + groups + place]
        for g in range(tail_groups):
            tails[place, g * SUBLANES : (g + 1) * SUBLANES, :] = returned[
                slot, rows : rows + SUBLANES, g * width : (g + 1) * width
            ]
        tails[place, rows - SUBLANES :, :] = returned[slot, rows + SUBLANES :, :width]
        copies.append(
            pltpu.make_async_copy(
                tails.at[place], update.at[place, :, LANES:], sems.at[blocks + place]
            )
        )
        copies[-1].start()
    for copy in copies:
        copy.wait()


def run(name, kernel, scalars, arrays, outs, scratch=(), flops=0, sems=0, far=0, far_outs=0):
    moved = sum(a.size * a.dtype.itemsize for a in list(arrays) + list(outs))
    near = len(arrays) - far
    near_outs = len(outs) - far_outs
    return pl.pallas_call(
        kernel,
        out_shape=[pltpu.VMEM(o.shape, o.dtype) for o in outs[:near_outs]]
        + [pltpu.HBM(o.shape, o.dtype) for o in outs[near_outs:]],
        in_specs=[SMEM] * len(scalars) + [VMEM] * near + [FAR] * far,
        out_specs=[VMEM] * near_outs + [FAR] * far_outs,
        scratch_shapes=[pltpu.VMEM(o.shape, o.dtype) for o in scratch]
        + [pltpu.SemaphoreType.DMA((sems,))] * (sems > 0),
        compiler_params=pltpu.CompilerParams(vmem_limit_bytes=VMEM_GRANT),
        cost_estimate=pl.CostEstimate(flops=flops, bytes_accessed=moved, transcendentals=0),
        name=name,
    )(
        *scalars,
        *(pltpu.with_memory_space_constraint(a, pltpu.VMEM) for a in arrays[:near]),
        *(pltpu.with_memory_space_constraint(a, pltpu.HBM) for a in arrays[near:]),
    )


def per_device_packed(
    grad_partial,
    owner,
    offset,
    left_factor,
    right_factor,
    left_basis,
    right_basis,
    momentum,
    second_moment,
):
    pieces = grad_partial[0]
    blocks, rows, columns = pieces.shape
    groups = lax.axis_size("mp")
    replicas = lax.axis_size("dp")
    col_share = columns // replicas
    share = lax.axis_index("dp").astype(jnp.int32).reshape(1)
    group = lax.axis_index("mp").astype(jnp.int32).reshape(1)
    bf16, f32 = jnp.bfloat16, jnp.float32
    shape = jax.ShapeDtypeStruct
    packed = shape((blocks, rows + 2 * SUBLANES, LANES), bf16)
    square = (columns, columns)
    lbasis, rbasis, moment, second = left_basis[0], right_basis[0], momentum[0], second_moment[0]
    left_t, right_t = left_factor[0].T, right_factor[0].T
    product = 2 * columns**3

    parts = run(
        "pack",
        pack_kernel,
        [share],
        [pieces],
        [packed] * replicas,
        scratch=[shape((blocks, rows, LANES // 2), bf16)],
        sems=replicas + 1,
        far=1,
    )
    parts = [parts[0]] + [
        lax.ppermute(parts[s], "dp", [(i, (i + s) % replicas) for i in range(replicas)])
        for s in range(1, replicas)
    ]
    table = pl.pallas_call(
        table_kernel,
        out_shape=pltpu.SMEM((SLOTS + groups + blocks,), jnp.int32),
        in_specs=[SMEM] * 4,
        out_specs=SMEM,
        name="table",
    )(share, group, owner, offset)
    lbasis_t, old_part, back_basis = run(
        "prepare",
        prepare_kernel,
        [table],
        [lbasis, rbasis, moment],
        [shape(square, bf16), shape(square, f32), shape((columns, 2 * LANES), bf16)],
        scratch=[shape(square, bf16)] * 3,
        sems=3,
        far=3,
        flops=2 * product,
    )
    parts, lbasis_t, old_part, back_basis = lax.optimization_barrier(
        (parts, lbasis_t, old_part, back_basis)
    )
    (outgoing,) = run(
        "route",
        route_kernel,
        [table],
        parts,
        [shape((replicas * groups,) + packed.shape[1:], bf16)],
        scratch=[packed],
    )
    arrived = lax.all_to_all(outgoing, ("dp", "mp"), split_axis=0, concat_axis=0, tiled=True)
    chunks = shape((groups, rows + 2 * SUBLANES, LANES), bf16)
    factor_t = shape(left_t.shape, f32)
    gradient, new_second, back = run(
        "owner_step",
        owner_kernel,
        [table],
        [arrived, lbasis, rbasis, lbasis_t, old_part, back_basis, second],
        [shape(square, bf16), shape(square, f32), chunks],
        scratch=[shape(square, bf16)] * 2 + [chunks],
        sems=groups,
        far_outs=1,
        flops=3 * product,
    )
    returned = lax.all_to_all(
        back,
        "mp",
        split_axis=0,
        concat_axis=0,
        tiled=True,
        axis_index_groups=[list(range(groups))[::-1]],
    )
    new_second, new_moment, new_left_t, new_right_t = run(
        "factors",
        factor_kernel,
        [table],
        [gradient, new_second, moment, left_t, right_t],
        [shape(square, f32), shape(square, bf16), factor_t, factor_t],
        scratch=[shape(square, bf16), factor_t, factor_t] * 2,
        sems=10,
        far=3,
        far_outs=4,
        flops=product,
    )
    (update,) = run(
        "place",
        place_kernel,
        [table],
        [returned],
        [shape((blocks, rows, col_share), bf16)],
        scratch=[shape((blocks, rows, col_share - LANES), bf16)],
        sems=2 * blocks,
        far_outs=1,
    )
    return (
        update,
        new_left_t.T[None],
        new_right_t.T[None],
        new_moment[None],
        new_second[None],
    )


def per_device(grad_partial, *rest):
    _, _, rows, columns = grad_partial.shape
    fits = packed_fits(rows, columns, lax.axis_size("dp"))
    return (per_device_packed if fits else per_device_general)(grad_partial, *rest)


def per_device_general(
    grad_partial,
    owner,
    offset,
    left_factor,
    right_factor,
    left_basis,
    right_basis,
    momentum,
    second_moment,
):
    pieces = grad_partial[0]
    blocks, row_count, columns = pieces.shape
    groups = lax.axis_size("mp")
    replicas = lax.axis_size("dp")
    col_share = columns // replicas
    column = lax.axis_index("dp") * col_share
    my_group = lax.axis_index("mp")
    targets = lax.broadcasted_iota(jnp.int32, (groups, blocks), 0)
    positions = lax.broadcasted_iota(jnp.int32, (blocks, blocks), 0)
    routing = (owner[None, :] == targets).astype(jnp.float32)
    where_at = (offset[None, :] == positions).astype(jnp.float32)
    select = contract_last(routing, where_at).astype(jnp.bfloat16)
    occupied = jnp.any(owner == my_group)
    swapped = lax.all_to_all(grad_partial, "dp", split_axis=3, concat_axis=0, tiled=True)
    summed = jnp.sum(swapped.astype(jnp.float32), axis=0).astype(jnp.bfloat16)
    outgoing = jnp.dot(
        select, summed.reshape(blocks, row_count * col_share), preferred_element_type=jnp.float32
    )
    outgoing = outgoing.astype(jnp.bfloat16).reshape(groups, row_count, col_share)
    landed = lax.all_to_all(outgoing, "mp", split_axis=0, concat_axis=0, tiled=True)
    arrived = lax.all_gather(landed, "dp", axis=2, tiled=True)
    gradient = arrived.reshape(groups * row_count, columns)

    def refresh(operands):
        grad_in, left_fac, right_fac, lbasis, rbasis, moment, second = operands
        grad_rows = lax.dynamic_slice_in_dim(grad_in, column, col_share, 0)
        grad_cols = lax.dynamic_slice_in_dim(grad_in, column, col_share, 1)
        new_left = 0.95 * left_fac + 0.05 * contract_last(grad_in, grad_rows)
        new_right = 0.95 * right_fac + 0.05 * contract_first(grad_in, grad_cols)
        new_moment = (0.9 * moment.astype(jnp.float32) + 0.1 * grad_in.astype(jnp.float32)).astype(
            jnp.bfloat16
        )
        turned = contract_first(lbasis, grad_in).astype(jnp.bfloat16)
        rotated = jnp.dot(turned, rbasis, preferred_element_type=jnp.float32)
        turned_mom = contract_first(lbasis, new_moment).astype(jnp.bfloat16)
        rotated_mom = jnp.dot(turned_mom, rbasis, preferred_element_type=jnp.float32)
        new_second = 0.95 * second + 0.05 * rotated * rotated
        scaled = (rotated_mom / (jnp.sqrt(new_second) + 1e-08)).astype(jnp.bfloat16)
        unrotated = jnp.dot(lbasis, scaled, preferred_element_type=jnp.float32).astype(jnp.bfloat16)
        back_rows = lax.dynamic_slice_in_dim(rbasis, column, col_share, 0)
        return (new_left, new_right, new_moment, new_second, contract_last(unrotated, back_rows))

    def keep_old(operands):
        grad_in, left_fac, right_fac, lbasis, rbasis, moment, second = operands
        return (left_fac, right_fac, moment, second, jnp.zeros((columns, col_share), jnp.float32))

    operands = (
        gradient,
        left_factor[0],
        right_factor[0],
        left_basis[0],
        right_basis[0],
        momentum[0],
        second_moment[0],
    )
    new_left, new_right, new_moment, new_second, turned_cols = lax.cond(
        occupied, refresh, keep_old, operands
    )
    outgoing_back = turned_cols.astype(jnp.bfloat16).reshape(groups, row_count, col_share)
    returned = lax.all_to_all(outgoing_back, "mp", split_axis=0, concat_axis=0, tiled=True)
    update = contract_first(select, returned.reshape(groups, row_count * col_share)).astype(
        jnp.bfloat16
    )
    update = update.reshape(blocks, row_count, col_share)
    return (update, new_left[None], new_right[None], new_moment[None], new_second[None])


def solution(mesh):
    placed = (
        P("dp", None, "mp", None),
        P(),
        P(),
        P("mp", None, "dp"),
        P("mp", None, "dp"),
        P("mp", None, None),
        P("mp", None, None),
        P("mp", None, None),
        P("mp", None, None),
    )
    return jax.shard_map(
        per_device,
        mesh=mesh,
        in_specs=placed,
        out_specs=(
            P(None, "mp", "dp"),
            P("mp", None, "dp"),
            P("mp", None, "dp"),
            P("mp", None, None),
            P("mp", None, None),
        ),
        check_vma=False,
    )
```

```python
import jax
import jax.numpy as jnp
from jax import lax
from jax.experimental import pallas as pl
from jax.experimental.pallas import tpu as pltpu
from jax.sharding import PartitionSpec as P

LANES = 128
SUBLANES = 8
VMEM = pl.BlockSpec(memory_space=pltpu.VMEM)
SMEM = pl.BlockSpec(memory_space=pltpu.SMEM)
FAR = pl.BlockSpec(memory_space=pltpu.HBM)
VMEM_GRANT = 16 * 2**20
CUT = 2 * LANES
STRIP = 48

def contract_first(matrix_a, matrix_b):
    return lax.dot_general(
        matrix_a, matrix_b, (((0,), (0,)), ((), ())), preferred_element_type=jnp.float32
    )


def contract_last(matrix_a, matrix_b):
    return lax.dot_general(
        matrix_a, matrix_b, (((1,), (1,)), ((), ())), preferred_element_type=jnp.float32
    )


def matmul(matrix_a, matrix_b):
    return jnp.dot(matrix_a, matrix_b, preferred_element_type=jnp.float32)


def tail_start(share):
    return jnp.where(share == 0, 0, 2 * share + 1) if not isinstance(share, int) else (
        0 if share == 0 else 2 * share + 1
    )


def packed_fits(rows, columns, replicas):
    width = columns // replicas - LANES
    return (
        columns == replicas * LANES + LANES // 2
        and rows == (2 * replicas + 1) * SUBLANES
        and width * replicas == LANES // 2
        and width % 16 == 0
        and LANES // width == rows // SUBLANES - 1
    )


def tail_places(blocks, rows):
    for b in range(blocks):
        for g in range(3):
            place = 3 * b + g
            yield b, g, blocks * rows + place // 2 * SUBLANES, place % 2 * (LANES // 2)


def chunk_rows(blocks, rows):
    return blocks * rows + -(-3 * blocks // 2) * SUBLANES


def pack_kernel(me_ref, grad_hbm, *refs):
    outs, last, sems = refs[:-2], refs[-2], refs[-1]
    replicas = len(outs)
    blocks, rows, columns = grad_hbm.shape
    half = LANES // 2
    shares = [lax.rem(me_ref[0] + step, replicas) for step in range(replicas)]
    copies = [
        pltpu.make_async_copy(
            grad_hbm.at[:, :, columns - half :], last, sems.at[replicas * blocks]
        )
    ]
    for step in range(replicas):
        col = pl.multiple_of(shares[step] * LANES, LANES)
        for b in range(blocks):
            copies.append(
                pltpu.make_async_copy(
                    grad_hbm.at[b, :, pl.ds(col, LANES)],
                    outs[step].at[b * rows : (b + 1) * rows, :],
                    sems.at[step * blocks + b],
                )
            )
    for copy in copies:
        copy.start()
    copies[0].wait()
    for step in range(replicas):
        start = tail_start(shares[step])
        for b, g, row, lane in tail_places(blocks, rows):
            source = pl.multiple_of(
                jnp.minimum(start + g, rows // SUBLANES - 1) * SUBLANES, SUBLANES
            )
            outs[step][row : row + SUBLANES, lane : lane + half] = last[
                b, pl.ds(source, SUBLANES), :
            ]
    for copy in copies[1:]:
        copy.wait()


SHARE, GROUP, FOUND, SLOTS = 0, 1, 2, 3


def table_kernel(share_ref, group_ref, owner_ref, offset_ref, table):
    blocks = owner_ref.shape[0]
    groups = table.shape[0] - SLOTS - blocks
    table[SHARE] = share_ref[0]
    table[GROUP] = group_ref[0]
    found = jnp.int32(0)
    for b in range(blocks):
        found = jnp.where(owner_ref[b] == group_ref[0], 1, found)
    table[FOUND] = found
    for group in range(groups):
        table[SLOTS + group] = jnp.int32(0)
    for b in range(blocks):
        table[SLOTS + owner_ref[b]] = offset_ref[b]
        table[SLOTS + groups + offset_ref[b]] = groups - 1 - owner_ref[b]


def route_kernel(table, *refs):
    parts, out, summed = refs[:-2], refs[-2], refs[-1]
    replicas = len(parts)
    groups = out.shape[0] // replicas
    blocks = summed.shape[0]
    rows = summed.shape[1] - 2 * SUBLANES
    half = LANES // 2

    def add(*index):
        total = parts[0][index].astype(jnp.float32)
        for part in parts[1:]:
            total = total + part[index].astype(jnp.float32)
        return total.astype(jnp.bfloat16)

    for b in range(blocks):
        summed[b, :rows, :] = add(slice(b * rows, (b + 1) * rows), slice(None))
        summed[b, rows + SUBLANES :, half:] = jnp.zeros((SUBLANES, half), jnp.bfloat16)
    for b, g, row, lane in tail_places(blocks, rows):
        below = rows + (g % 2) * SUBLANES
        beside = (g // 2) * half
        summed[b, below : below + SUBLANES, beside : beside + half] = add(
            slice(row, row + SUBLANES), slice(lane, lane + half)
        )
    for group in range(groups):
        piece = summed[table[SLOTS + group]]
        for r in range(replicas):
            out[r * groups + group] = piece


def prepare_kernel(
    table, lbasis_hbm, rbasis_hbm, moment_hbm,
    lbasis_t, old_part, back_basis, lbasis, rbasis, moment, sems,
):
    found = table[FOUND]

    @pl.when(found == 1)
    def _():
        copies = [
            pltpu.make_async_copy(source, target, sems.at[n])
            for n, (source, target) in enumerate(
                ((lbasis_hbm, lbasis), (moment_hbm, moment), (rbasis_hbm, rbasis))
            )
        ]
        for copy in copies:
            copy.start()
        copies[0].wait()
        transposed = lbasis[...].T
        lbasis_t[...] = transposed
        copies[1].wait()
        turned = matmul(transposed, moment[...]).astype(jnp.bfloat16)
        copies[2].wait()
        old_part[...] = 0.9 * matmul(turned, rbasis[...])
        columns = rbasis.shape[0]
        col_share = columns // (columns // LANES)
        tail = col_share - LANES
        first = pl.multiple_of(table[SHARE] * col_share, tail)
        main = rbasis[pl.ds(first, LANES), :]
        last = rbasis[pl.ds(pl.multiple_of(first + LANES, tail), tail), :]
        back_basis[...] = jnp.concatenate([main] + [last] * (LANES // tail), axis=0).T


def assemble(arrived, gradient, groups, rows):
    half = LANES // 2
    tail = gradient.shape[1] - half
    for r in range(arrived.shape[0] // groups):
        start = tail_start(r)
        for m in range(groups):
            piece = r * groups + m
            base = m * rows
            gradient[base : base + rows, r * LANES : (r + 1) * LANES] = arrived[piece, :rows, :]
            for g in range(3 if r == 0 else 2):
                row = base + (start + g) * SUBLANES
                below = rows + (g % 2) * SUBLANES
                beside = (g // 2) * half
                gradient[row : row + SUBLANES, tail:] = arrived[
                    piece, below : below + SUBLANES, beside : beside + half
                ]


def owner_kernel(
    table, arrived, lbasis, rbasis, lbasis_t, old_part, back_basis, second,
    gradient, new_second, back_out, turned, scaled, back, sems,
):
    found = table[FOUND]
    groups = back.shape[0]
    copies = [
        pltpu.make_async_copy(back.at[n], back_out.at[n], sems.at[n]) for n in range(groups)
    ]
    columns = gradient.shape[1]
    rows = columns // groups

    @pl.when(found == 1)
    def _():
        assemble(arrived, gradient, groups, rows)
        turned[...] = matmul(lbasis_t[...], gradient[...]).astype(jnp.bfloat16)
        for low in range(0, columns, CUT):
            cols = slice(low, min(low + CUT, columns))
            rotated = matmul(turned[...], rbasis[:, cols])
            fresh = 0.95 * second[:, cols] + 0.05 * rotated * rotated
            new_second[:, cols] = fresh
            rotated_mom = old_part[:, cols] + 0.1 * rotated
            spread = fresh * lax.rsqrt(fresh) + 1e-08
            scaled[:, cols] = (rotated_mom * lax.rsqrt(spread * spread)).astype(jnp.bfloat16)
        total = matmul(scaled[...], back_basis[...])
        result = matmul(lbasis[...], total.astype(jnp.bfloat16))
        lane = lax.broadcasted_iota(jnp.int32, (SUBLANES, LANES), 1)
        tail_groups = rows // SUBLANES - 1
        width = LANES // tail_groups
        for m in range(groups):
            base = m * rows
            back[groups - 1 - m, :rows, :] = result[base : base + rows, :LANES].astype(jnp.bfloat16)
            mixed = result[base : base + SUBLANES, LANES:]
            for g in range(1, tail_groups):
                row = base + g * SUBLANES
                mixed = jnp.where(
                    lane < g * width, mixed, result[row : row + SUBLANES, LANES:]
                )
            back[groups - 1 - m, rows : rows + SUBLANES, :] = mixed.astype(jnp.bfloat16)
            back[groups - 1 - m, rows + SUBLANES :, :] = result[
                base + rows - SUBLANES : base + rows, LANES:
            ].astype(jnp.bfloat16)
        for copy in copies:
            copy.start()
        for copy in copies:
            copy.wait()

    @pl.when(found == 0)
    def _():
        new_second[...] = second[...]


def factor_kernel(
    table, gradient, second, moment_hbm, left_hbm, right_hbm,
    second_out, moment_out, left_out, right_out,
    moment, left_t, right_t, new_moment, new_left_t, new_right_t, sems,
):
    found = table[FOUND]
    col_share, columns = left_t.shape
    held = (moment, left_t, right_t)
    outs = (moment_out, left_out, right_out)

    def copies_of(first, sources, targets):
        return [
            pltpu.make_async_copy(a, b, sems.at[first + n])
            for n, (a, b) in enumerate(zip(sources, targets))
        ]

    loads = copies_of(0, (left_hbm, right_hbm, moment_hbm), (left_t, right_t, moment))
    fresh = copies_of(3, (new_left_t, new_right_t, new_moment), (left_out, right_out, moment_out))
    kept = copies_of(6, held, outs)
    second_copy = pltpu.make_async_copy(second, second_out, sems.at[9])
    for copy in loads + [second_copy]:
        copy.start()

    @pl.when(found == 1)
    def _():
        first = pl.multiple_of(table[SHARE] * col_share, 16)
        grad = gradient[...]
        left_term = 0.05 * contract_last(gradient[pl.ds(first, col_share), :], grad)
        picked = lax.broadcasted_iota(jnp.int32, (col_share, columns), 0) + first
        places = lax.broadcasted_iota(jnp.int32, (col_share, columns), 1)
        pick = jnp.where(picked == places, 1.0, 0.0).astype(jnp.bfloat16)
        grad_cols_t = contract_last(pick, grad).astype(jnp.bfloat16)
        right_term = 0.05 * matmul(grad_cols_t, grad)
        for copy in loads:
            copy.wait()
        new_left_t[...] = 0.95 * left_t[...] + left_term
        new_right_t[...] = 0.95 * right_t[...] + right_term
        for low in range(0, columns, STRIP):
            strip = slice(low, min(low + STRIP, columns))
            new_moment[strip, :] = (
                0.9 * moment[strip, :].astype(jnp.float32)
                + 0.1 * gradient[strip, :].astype(jnp.float32)
            ).astype(jnp.bfloat16)
        for copy in fresh:
            copy.start()
        for copy in fresh:
            copy.wait()

    @pl.when(found == 0)
    def _():
        for copy in loads:
            copy.wait()
        for copy in kept:
            copy.start()
        for copy in kept:
            copy.wait()

    second_copy.wait()


def place_kernel(table, returned, update, tails, sems):
    blocks, rows, col_share = update.shape
    groups = returned.shape[0]
    tail_groups = rows // SUBLANES - 1
    width = col_share - LANES
    copies = []
    for place in range(blocks):
        slot = table[SLOTS + groups + place]
        copies.append(
            pltpu.make_async_copy(
                returned.at[slot, :rows], update.at[place, :, :LANES], sems.at[place]
            )
        )
        copies[-1].start()
    for place in range(blocks):
        slot = table[SLOTS + groups + place]
        for g in range(tail_groups):
            tails[place, g * SUBLANES : (g + 1) * SUBLANES, :] = returned[
                slot, rows : rows + SUBLANES, g * width : (g + 1) * width
            ]
        tails[place, rows - SUBLANES :, :] = returned[slot, rows + SUBLANES :, :width]
        copies.append(
            pltpu.make_async_copy(
                tails.at[place], update.at[place, :, LANES:], sems.at[blocks + place]
            )
        )
        copies[-1].start()
    for copy in copies:
        copy.wait()


def run(name, kernel, scalars, arrays, outs, scratch=(), flops=0, sems=0, far=0, far_outs=0):
    moved = sum(a.size * a.dtype.itemsize for a in list(arrays) + list(outs))
    near = len(arrays) - far
    near_outs = len(outs) - far_outs
    return pl.pallas_call(
        kernel,
        out_shape=[pltpu.VMEM(o.shape, o.dtype) for o in outs[:near_outs]]
        + [pltpu.HBM(o.shape, o.dtype) for o in outs[near_outs:]],
        in_specs=[SMEM] * len(scalars) + [VMEM] * near + [FAR] * far,
        out_specs=[VMEM] * near_outs + [FAR] * far_outs,
        scratch_shapes=[pltpu.VMEM(o.shape, o.dtype) for o in scratch]
        + [pltpu.SemaphoreType.DMA((sems,))] * (sems > 0),
        compiler_params=pltpu.CompilerParams(vmem_limit_bytes=VMEM_GRANT),
        cost_estimate=pl.CostEstimate(flops=flops, bytes_accessed=moved, transcendentals=0),
        name=name,
    )(
        *scalars,
        *(pltpu.with_memory_space_constraint(a, pltpu.VMEM) for a in arrays[:near]),
        *(pltpu.with_memory_space_constraint(a, pltpu.HBM) for a in arrays[near:]),
    )


def per_device_packed(
    grad_partial,
    owner,
    offset,
    left_factor,
    right_factor,
    left_basis,
    right_basis,
    momentum,
    second_moment,
):
    pieces = grad_partial[0]
    blocks, rows, columns = pieces.shape
    groups = lax.axis_size("mp")
    replicas = lax.axis_size("dp")
    col_share = columns // replicas
    share = lax.axis_index("dp").astype(jnp.int32).reshape(1)
    group = lax.axis_index("mp").astype(jnp.int32).reshape(1)
    bf16, f32 = jnp.bfloat16, jnp.float32
    shape = jax.ShapeDtypeStruct
    packed = shape((blocks, rows + 2 * SUBLANES, LANES), bf16)
    sent = shape((chunk_rows(blocks, rows), LANES), bf16)
    square = (columns, columns)
    lbasis, rbasis, moment, second = left_basis[0], right_basis[0], momentum[0], second_moment[0]
    left_t, right_t = left_factor[0].T, right_factor[0].T
    product = 2 * columns**3

    parts = run(
        "pack",
        pack_kernel,
        [share],
        [pieces],
        [sent] * replicas,
        scratch=[shape((blocks, rows, LANES // 2), bf16)],
        sems=replicas * blocks + 1,
        far=1,
    )
    parts = [parts[0]] + [
        lax.ppermute(parts[s], "dp", [(i, (i + s) % replicas) for i in range(replicas)])
        for s in range(1, replicas)
    ]
    table = pl.pallas_call(
        table_kernel,
        out_shape=pltpu.SMEM((SLOTS + groups + blocks,), jnp.int32),
        in_specs=[SMEM] * 4,
        out_specs=SMEM,
        name="table",
    )(share, group, owner, offset)
    lbasis_t, old_part, back_basis = run(
        "prepare",
        prepare_kernel,
        [table],
        [lbasis, rbasis, moment],
        [shape(square, bf16), shape(square, f32), shape((columns, 2 * LANES), bf16)],
        scratch=[shape(square, bf16)] * 3,
        sems=3,
        far=3,
        flops=2 * product,
    )
    parts, lbasis_t, old_part, back_basis = lax.optimization_barrier(
        (parts, lbasis_t, old_part, back_basis)
    )
    (outgoing,) = run(
        "route",
        route_kernel,
        [table],
        parts,
        [shape((replicas * groups,) + packed.shape[1:], bf16)],
        scratch=[packed],
    )
    arrived = lax.all_to_all(outgoing, ("dp", "mp"), split_axis=0, concat_axis=0, tiled=True)
    chunks = shape((groups, rows + 2 * SUBLANES, LANES), bf16)
    factor_t = shape(left_t.shape, f32)
    gradient, new_second, back = run(
        "owner_step",
        owner_kernel,
        [table],
        [arrived, lbasis, rbasis, lbasis_t, old_part, back_basis, second],
        [shape(square, bf16), shape(square, f32), chunks],
        scratch=[shape(square, bf16)] * 2 + [chunks],
        sems=groups,
        far_outs=1,
        flops=3 * product,
    )
    returned = lax.all_to_all(
        back,
        "mp",
        split_axis=0,
        concat_axis=0,
        tiled=True,
        axis_index_groups=[list(range(groups))[::-1]],
    )
    new_second, new_moment, new_left_t, new_right_t = run(
        "factors",
        factor_kernel,
        [table],
        [gradient, new_second, moment, left_t, right_t],
        [shape(square, f32), shape(square, bf16), factor_t, factor_t],
        scratch=[shape(square, bf16), factor_t, factor_t] * 2,
        sems=10,
        far=3,
        far_outs=4,
        flops=product,
    )
    (update,) = run(
        "place",
        place_kernel,
        [table],
        [returned],
        [shape((blocks, rows, col_share), bf16)],
        scratch=[shape((blocks, rows, col_share - LANES), bf16)],
        sems=2 * blocks,
        far_outs=1,
    )
    return (
        update,
        new_left_t.T[None],
        new_right_t.T[None],
        new_moment[None],
        new_second[None],
    )


def per_device(grad_partial, *rest):
    _, _, rows, columns = grad_partial.shape
    fits = packed_fits(rows, columns, lax.axis_size("dp"))
    return (per_device_packed if fits else per_device_general)(grad_partial, *rest)


def per_device_general(
    grad_partial,
    owner,
    offset,
    left_factor,
    right_factor,
    left_basis,
    right_basis,
    momentum,
    second_moment,
):
    pieces = grad_partial[0]
    blocks, row_count, columns = pieces.shape
    groups = lax.axis_size("mp")
    replicas = lax.axis_size("dp")
    col_share = columns // replicas
    column = lax.axis_index("dp") * col_share
    my_group = lax.axis_index("mp")
    targets = lax.broadcasted_iota(jnp.int32, (groups, blocks), 0)
    positions = lax.broadcasted_iota(jnp.int32, (blocks, blocks), 0)
    routing = (owner[None, :] == targets).astype(jnp.float32)
    where_at = (offset[None, :] == positions).astype(jnp.float32)
    select = contract_last(routing, where_at).astype(jnp.bfloat16)
    occupied = jnp.any(owner == my_group)
    swapped = lax.all_to_all(grad_partial, "dp", split_axis=3, concat_axis=0, tiled=True)
    summed = jnp.sum(swapped.astype(jnp.float32), axis=0).astype(jnp.bfloat16)
    outgoing = jnp.dot(
        select, summed.reshape(blocks, row_count * col_share), preferred_element_type=jnp.float32
    )
    outgoing = outgoing.astype(jnp.bfloat16).reshape(groups, row_count, col_share)
    landed = lax.all_to_all(outgoing, "mp", split_axis=0, concat_axis=0, tiled=True)
    arrived = lax.all_gather(landed, "dp", axis=2, tiled=True)
    gradient = arrived.reshape(groups * row_count, columns)

    def refresh(operands):
        grad_in, left_fac, right_fac, lbasis, rbasis, moment, second = operands
        grad_rows = lax.dynamic_slice_in_dim(grad_in, column, col_share, 0)
        grad_cols = lax.dynamic_slice_in_dim(grad_in, column, col_share, 1)
        new_left = 0.95 * left_fac + 0.05 * contract_last(grad_in, grad_rows)
        new_right = 0.95 * right_fac + 0.05 * contract_first(grad_in, grad_cols)
        new_moment = (0.9 * moment.astype(jnp.float32) + 0.1 * grad_in.astype(jnp.float32)).astype(
            jnp.bfloat16
        )
        turned = contract_first(lbasis, grad_in).astype(jnp.bfloat16)
        rotated = jnp.dot(turned, rbasis, preferred_element_type=jnp.float32)
        turned_mom = contract_first(lbasis, new_moment).astype(jnp.bfloat16)
        rotated_mom = jnp.dot(turned_mom, rbasis, preferred_element_type=jnp.float32)
        new_second = 0.95 * second + 0.05 * rotated * rotated
        scaled = (rotated_mom / (jnp.sqrt(new_second) + 1e-08)).astype(jnp.bfloat16)
        unrotated = jnp.dot(lbasis, scaled, preferred_element_type=jnp.float32).astype(jnp.bfloat16)
        back_rows = lax.dynamic_slice_in_dim(rbasis, column, col_share, 0)
        return (new_left, new_right, new_moment, new_second, contract_last(unrotated, back_rows))

    def keep_old(operands):
        grad_in, left_fac, right_fac, lbasis, rbasis, moment, second = operands
        return (left_fac, right_fac, moment, second, jnp.zeros((columns, col_share), jnp.float32))

    operands = (
        gradient,
        left_factor[0],
        right_factor[0],
        left_basis[0],
        right_basis[0],
        momentum[0],
        second_moment[0],
    )
    new_left, new_right, new_moment, new_second, turned_cols = lax.cond(
        occupied, refresh, keep_old, operands
    )
    outgoing_back = turned_cols.astype(jnp.bfloat16).reshape(groups, row_count, col_share)
    returned = lax.all_to_all(outgoing_back, "mp", split_axis=0, concat_axis=0, tiled=True)
    update = contract_first(select, returned.reshape(groups, row_count * col_share)).astype(
        jnp.bfloat16
    )
    update = update.reshape(blocks, row_count, col_share)
    return (update, new_left[None], new_right[None], new_moment[None], new_second[None])


def solution(mesh):
    placed = (
        P("dp", None, "mp", None),
        P(),
        P(),
        P("mp", None, "dp"),
        P("mp", None, "dp"),
        P("mp", None, None),
        P("mp", None, None),
        P("mp", None, None),
        P("mp", None, None),
    )
    return jax.shard_map(
        per_device,
        mesh=mesh,
        in_specs=placed,
        out_specs=(
            P(None, "mp", "dp"),
            P("mp", None, "dp"),
            P("mp", None, "dp"),
            P("mp", None, None),
            P("mp", None, None),
        ),
        check_vma=False,
    )
```

```python
import jax
import jax.numpy as jnp
from jax import lax
from jax.experimental import pallas as pl
from jax.experimental.pallas import tpu as pltpu
from jax.sharding import PartitionSpec as P

LANES = 128
SUBLANES = 8
VMEM = pl.BlockSpec(memory_space=pltpu.VMEM)
SMEM = pl.BlockSpec(memory_space=pltpu.SMEM)
FAR = pl.BlockSpec(memory_space=pltpu.HBM)
VMEM_GRANT = 16 * 2**20
CUT = 2 * LANES
STRIP = 48

def contract_first(matrix_a, matrix_b):
    return lax.dot_general(
        matrix_a, matrix_b, (((0,), (0,)), ((), ())), preferred_element_type=jnp.float32
    )


def contract_last(matrix_a, matrix_b):
    return lax.dot_general(
        matrix_a, matrix_b, (((1,), (1,)), ((), ())), preferred_element_type=jnp.float32
    )


def matmul(matrix_a, matrix_b):
    return jnp.dot(matrix_a, matrix_b, preferred_element_type=jnp.float32)


def tail_start(share):
    return jnp.where(share == 0, 0, 2 * share + 1) if not isinstance(share, int) else (
        0 if share == 0 else 2 * share + 1
    )


def packed_fits(rows, columns, replicas):
    width = columns // replicas - LANES
    return (
        columns == replicas * LANES + LANES // 2
        and rows == (2 * replicas + 1) * SUBLANES
        and width * replicas == LANES // 2
        and width % 16 == 0
        and LANES // width == rows // SUBLANES - 1
    )


def tail_places(blocks, rows):
    for b in range(blocks):
        for g in range(3):
            place = 3 * b + g
            yield b, g, blocks * rows + place // 2 * SUBLANES, place % 2 * (LANES // 2)


def chunk_rows(blocks, rows):
    return blocks * rows + -(-3 * blocks // 2) * SUBLANES


def pack_kernel(me_ref, grad_hbm, *refs):
    outs, last, sems = refs[:-2], refs[-2], refs[-1]
    replicas = len(outs)
    blocks, rows, columns = grad_hbm.shape
    half = LANES // 2
    shares = [lax.rem(me_ref[0] + step, replicas) for step in range(replicas)]
    copies = [
        pltpu.make_async_copy(
            grad_hbm.at[:, :, columns - half :], last, sems.at[replicas * blocks]
        )
    ]
    for step in range(replicas):
        col = pl.multiple_of(shares[step] * LANES, LANES)
        for b in range(blocks):
            copies.append(
                pltpu.make_async_copy(
                    grad_hbm.at[b, :, pl.ds(col, LANES)],
                    outs[step].at[b * rows : (b + 1) * rows, :],
                    sems.at[step * blocks + b],
                )
            )
    for copy in copies:
        copy.start()
    copies[0].wait()
    for step in range(replicas):
        start = tail_start(shares[step])
        for b, g, row, lane in tail_places(blocks, rows):
            source = pl.multiple_of(
                jnp.minimum(start + g, rows // SUBLANES - 1) * SUBLANES, SUBLANES
            )
            outs[step][row : row + SUBLANES, lane : lane + half] = last[
                b, pl.ds(source, SUBLANES), :
            ]
    for copy in copies[1:]:
        copy.wait()


SHARE, GROUP, FOUND, SLOTS = 0, 1, 2, 3


def table_kernel(share_ref, group_ref, owner_ref, offset_ref, table):
    blocks = owner_ref.shape[0]
    groups = table.shape[0] - SLOTS - blocks
    table[SHARE] = share_ref[0]
    table[GROUP] = group_ref[0]
    found = jnp.int32(0)
    for b in range(blocks):
        found = jnp.where(owner_ref[b] == group_ref[0], 1, found)
    table[FOUND] = found
    for group in range(groups):
        table[SLOTS + group] = jnp.int32(0)
    for b in range(blocks):
        table[SLOTS + owner_ref[b]] = offset_ref[b]
        table[SLOTS + groups + offset_ref[b]] = groups - 1 - owner_ref[b]


def route_kernel(table, *refs):
    parts, out, summed = refs[:-2], refs[-2], refs[-1]
    replicas = len(parts)
    groups = out.shape[0] // replicas
    blocks = summed.shape[0]
    rows = summed.shape[1] - 2 * SUBLANES
    half = LANES // 2

    def add(*index):
        total = parts[0][index].astype(jnp.float32)
        for part in parts[1:]:
            total = total + part[index].astype(jnp.float32)
        return total.astype(jnp.bfloat16)

    for b in range(blocks):
        summed[b, :rows, :] = add(slice(b * rows, (b + 1) * rows), slice(None))
        summed[b, rows + SUBLANES :, half:] = jnp.zeros((SUBLANES, half), jnp.bfloat16)
    for b, g, row, lane in tail_places(blocks, rows):
        below = rows + (g % 2) * SUBLANES
        beside = (g // 2) * half
        summed[b, below : below + SUBLANES, beside : beside + half] = add(
            slice(row, row + SUBLANES), slice(lane, lane + half)
        )
    for group in range(groups):
        piece = summed[table[SLOTS + group]]
        for r in range(replicas):
            out[(replicas - r) * groups - 1 - group] = piece


def prepare_kernel(
    table, lbasis_hbm, rbasis_hbm, moment_hbm,
    lbasis_t, old_part, back_basis, lbasis, rbasis, moment, sems,
):
    found = table[FOUND]

    @pl.when(found == 1)
    def _():
        copies = [
            pltpu.make_async_copy(source, target, sems.at[n])
            for n, (source, target) in enumerate(
                ((lbasis_hbm, lbasis), (moment_hbm, moment), (rbasis_hbm, rbasis))
            )
        ]
        for copy in copies:
            copy.start()
        copies[0].wait()
        transposed = lbasis[...].T
        lbasis_t[...] = transposed
        copies[1].wait()
        turned = matmul(transposed, moment[...]).astype(jnp.bfloat16)
        copies[2].wait()
        old_part[...] = 0.9 * matmul(turned, rbasis[...])
        columns = rbasis.shape[0]
        col_share = columns // (columns // LANES)
        tail = col_share - LANES
        first = pl.multiple_of(table[SHARE] * col_share, tail)
        main = rbasis[pl.ds(first, LANES), :]
        last = rbasis[pl.ds(pl.multiple_of(first + LANES, tail), tail), :]
        back_basis[...] = jnp.concatenate([main] + [last] * (LANES // tail), axis=0).T


def assemble(arrived, gradient, groups, rows):
    half = LANES // 2
    tail = gradient.shape[1] - half
    for r in range(arrived.shape[0] // groups):
        start = tail_start(r)
        for m in range(groups):
            piece = arrived.shape[0] - 1 - (r * groups + m)
            base = m * rows
            gradient[base : base + rows, r * LANES : (r + 1) * LANES] = arrived[piece, :rows, :]
            for g in range(3 if r == 0 else 2):
                row = base + (start + g) * SUBLANES
                below = rows + (g % 2) * SUBLANES
                beside = (g // 2) * half
                gradient[row : row + SUBLANES, tail:] = arrived[
                    piece, below : below + SUBLANES, beside : beside + half
                ]


def owner_kernel(
    table, arrived, lbasis, rbasis, lbasis_t, old_part, back_basis, second,
    gradient, new_second, back_out, turned, scaled, back, sems,
):
    found = table[FOUND]
    groups = back.shape[0]
    copies = [
        pltpu.make_async_copy(back.at[n], back_out.at[n], sems.at[n]) for n in range(groups)
    ]
    columns = gradient.shape[1]
    rows = columns // groups

    @pl.when(found == 1)
    def _():
        assemble(arrived, gradient, groups, rows)
        turned[...] = matmul(lbasis_t[...], gradient[...]).astype(jnp.bfloat16)
        for low in range(0, columns, CUT):
            cols = slice(low, min(low + CUT, columns))
            rotated = matmul(turned[...], rbasis[:, cols])
            fresh = 0.95 * second[:, cols] + 0.05 * rotated * rotated
            new_second[:, cols] = fresh
            rotated_mom = old_part[:, cols] + 0.1 * rotated
            spread = fresh * lax.rsqrt(fresh) + 1e-08
            scaled[:, cols] = (rotated_mom * lax.rsqrt(spread * spread)).astype(jnp.bfloat16)
        total = matmul(scaled[...], back_basis[...])
        result = matmul(lbasis[...], total.astype(jnp.bfloat16))
        lane = lax.broadcasted_iota(jnp.int32, (SUBLANES, LANES), 1)
        tail_groups = rows // SUBLANES - 1
        width = LANES // tail_groups
        for m in range(groups):
            base = m * rows
            back[groups - 1 - m, :rows, :] = result[base : base + rows, :LANES].astype(jnp.bfloat16)
            mixed = result[base : base + SUBLANES, LANES:]
            for g in range(1, tail_groups):
                row = base + g * SUBLANES
                mixed = jnp.where(
                    lane < g * width, mixed, result[row : row + SUBLANES, LANES:]
                )
            back[groups - 1 - m, rows : rows + SUBLANES, :] = mixed.astype(jnp.bfloat16)
            back[groups - 1 - m, rows + SUBLANES :, :] = result[
                base + rows - SUBLANES : base + rows, LANES:
            ].astype(jnp.bfloat16)
        for copy in copies:
            copy.start()
        for copy in copies:
            copy.wait()

    @pl.when(found == 0)
    def _():
        new_second[...] = second[...]


def factor_kernel(
    table, gradient, second, moment_hbm, left_hbm, right_hbm,
    second_out, moment_out, left_out, right_out,
    moment, left_t, right_t, new_moment, new_left_t, new_right_t, sems,
):
    found = table[FOUND]
    col_share, columns = left_t.shape
    held = (moment, left_t, right_t)
    outs = (moment_out, left_out, right_out)

    def copies_of(first, sources, targets):
        return [
            pltpu.make_async_copy(a, b, sems.at[first + n])
            for n, (a, b) in enumerate(zip(sources, targets))
        ]

    loads = copies_of(0, (left_hbm, right_hbm, moment_hbm), (left_t, right_t, moment))
    fresh = copies_of(3, (new_left_t, new_right_t, new_moment), (left_out, right_out, moment_out))
    kept = copies_of(6, held, outs)
    second_copy = pltpu.make_async_copy(second, second_out, sems.at[9])
    for copy in loads + [second_copy]:
        copy.start()

    @pl.when(found == 1)
    def _():
        first = pl.multiple_of(table[SHARE] * col_share, 16)
        grad = gradient[...]
        left_term = 0.05 * contract_last(gradient[pl.ds(first, col_share), :], grad)
        picked = lax.broadcasted_iota(jnp.int32, (col_share, columns), 0) + first
        places = lax.broadcasted_iota(jnp.int32, (col_share, columns), 1)
        pick = jnp.where(picked == places, 1.0, 0.0).astype(jnp.bfloat16)
        grad_cols_t = contract_last(pick, grad).astype(jnp.bfloat16)
        right_term = 0.05 * matmul(grad_cols_t, grad)
        for copy in loads:
            copy.wait()
        new_left_t[...] = 0.95 * left_t[...] + left_term
        new_right_t[...] = 0.95 * right_t[...] + right_term
        for low in range(0, columns, STRIP):
            strip = slice(low, min(low + STRIP, columns))
            new_moment[strip, :] = (
                0.9 * moment[strip, :].astype(jnp.float32)
                + 0.1 * gradient[strip, :].astype(jnp.float32)
            ).astype(jnp.bfloat16)
        for copy in fresh:
            copy.start()
        for copy in fresh:
            copy.wait()

    @pl.when(found == 0)
    def _():
        for copy in loads:
            copy.wait()
        for copy in kept:
            copy.start()
        for copy in kept:
            copy.wait()

    second_copy.wait()


def place_kernel(table, returned, update, tails, sems):
    blocks, rows, col_share = update.shape
    groups = returned.shape[0]
    tail_groups = rows // SUBLANES - 1
    width = col_share - LANES
    copies = []
    for place in range(blocks):
        slot = table[SLOTS + groups + place]
        copies.append(
            pltpu.make_async_copy(
                returned.at[slot, :rows], update.at[place, :, :LANES], sems.at[place]
            )
        )
        copies[-1].start()
    for place in range(blocks):
        slot = table[SLOTS + groups + place]
        for g in range(tail_groups):
            tails[place, g * SUBLANES : (g + 1) * SUBLANES, :] = returned[
                slot, rows : rows + SUBLANES, g * width : (g + 1) * width
            ]
        tails[place, rows - SUBLANES :, :] = returned[slot, rows + SUBLANES :, :width]
        copies.append(
            pltpu.make_async_copy(
                tails.at[place], update.at[place, :, LANES:], sems.at[blocks + place]
            )
        )
        copies[-1].start()
    for copy in copies:
        copy.wait()


def run(name, kernel, scalars, arrays, outs, scratch=(), flops=0, sems=0, far=0, far_outs=0):
    moved = sum(a.size * a.dtype.itemsize for a in list(arrays) + list(outs))
    near = len(arrays) - far
    near_outs = len(outs) - far_outs
    return pl.pallas_call(
        kernel,
        out_shape=[pltpu.VMEM(o.shape, o.dtype) for o in outs[:near_outs]]
        + [pltpu.HBM(o.shape, o.dtype) for o in outs[near_outs:]],
        in_specs=[SMEM] * len(scalars) + [VMEM] * near + [FAR] * far,
        out_specs=[VMEM] * near_outs + [FAR] * far_outs,
        scratch_shapes=[pltpu.VMEM(o.shape, o.dtype) for o in scratch]
        + [pltpu.SemaphoreType.DMA((sems,))] * (sems > 0),
        compiler_params=pltpu.CompilerParams(vmem_limit_bytes=VMEM_GRANT),
        cost_estimate=pl.CostEstimate(flops=flops, bytes_accessed=moved, transcendentals=0),
        name=name,
    )(
        *scalars,
        *(pltpu.with_memory_space_constraint(a, pltpu.VMEM) for a in arrays[:near]),
        *(pltpu.with_memory_space_constraint(a, pltpu.HBM) for a in arrays[near:]),
    )


def per_device_packed(
    grad_partial,
    owner,
    offset,
    left_factor,
    right_factor,
    left_basis,
    right_basis,
    momentum,
    second_moment,
):
    pieces = grad_partial[0]
    blocks, rows, columns = pieces.shape
    groups = lax.axis_size("mp")
    replicas = lax.axis_size("dp")
    col_share = columns // replicas
    share = lax.axis_index("dp").astype(jnp.int32).reshape(1)
    group = lax.axis_index("mp").astype(jnp.int32).reshape(1)
    bf16, f32 = jnp.bfloat16, jnp.float32
    shape = jax.ShapeDtypeStruct
    packed = shape((blocks, rows + 2 * SUBLANES, LANES), bf16)
    sent = shape((chunk_rows(blocks, rows), LANES), bf16)
    square = (columns, columns)
    lbasis, rbasis, moment, second = left_basis[0], right_basis[0], momentum[0], second_moment[0]
    left_t, right_t = left_factor[0].T, right_factor[0].T
    product = 2 * columns**3

    parts = run(
        "pack",
        pack_kernel,
        [share],
        [pieces],
        [sent] * replicas,
        scratch=[shape((blocks, rows, LANES // 2), bf16)],
        sems=replicas * blocks + 1,
        far=1,
    )
    parts = [parts[0]] + [
        lax.ppermute(parts[s], "dp", [(i, (i + s) % replicas) for i in range(replicas)])
        for s in range(1, replicas)
    ]
    table = pl.pallas_call(
        table_kernel,
        out_shape=pltpu.SMEM((SLOTS + groups + blocks,), jnp.int32),
        in_specs=[SMEM] * 4,
        out_specs=SMEM,
        name="table",
    )(share, group, owner, offset)
    lbasis_t, old_part, back_basis = run(
        "prepare",
        prepare_kernel,
        [table],
        [lbasis, rbasis, moment],
        [shape(square, bf16), shape(square, f32), shape((columns, 2 * LANES), bf16)],
        scratch=[shape(square, bf16)] * 3,
        sems=3,
        far=3,
        flops=2 * product,
    )
    parts, lbasis_t, old_part, back_basis = lax.optimization_barrier(
        (parts, lbasis_t, old_part, back_basis)
    )
    (outgoing,) = run(
        "route",
        route_kernel,
        [table],
        parts,
        [shape((replicas * groups,) + packed.shape[1:], bf16)],
        scratch=[packed],
    )
    arrived = lax.all_to_all(
        outgoing,
        ("dp", "mp"),
        split_axis=0,
        concat_axis=0,
        tiled=True,
        axis_index_groups=[list(range(replicas * groups))[::-1]],
    )
    chunks = shape((groups, rows + 2 * SUBLANES, LANES), bf16)
    factor_t = shape(left_t.shape, f32)
    gradient, new_second, back = run(
        "owner_step",
        owner_kernel,
        [table],
        [arrived, lbasis, rbasis, lbasis_t, old_part, back_basis, second],
        [shape(square, bf16), shape(square, f32), chunks],
        scratch=[shape(square, bf16)] * 2 + [chunks],
        sems=groups,
        far_outs=1,
        flops=3 * product,
    )
    returned = lax.all_to_all(
        back,
        "mp",
        split_axis=0,
        concat_axis=0,
        tiled=True,
        axis_index_groups=[list(range(groups))[::-1]],
    )
    new_second, new_moment, new_left_t, new_right_t = run(
        "factors",
        factor_kernel,
        [table],
        [gradient, new_second, moment, left_t, right_t],
        [shape(square, f32), shape(square, bf16), factor_t, factor_t],
        scratch=[shape(square, bf16), factor_t, factor_t] * 2,
        sems=10,
        far=3,
        far_outs=4,
        flops=product,
    )
    (update,) = run(
        "place",
        place_kernel,
        [table],
        [returned],
        [shape((blocks, rows, col_share), bf16)],
        scratch=[shape((blocks, rows, col_share - LANES), bf16)],
        sems=2 * blocks,
        far_outs=1,
    )
    return (
        update,
        new_left_t.T[None],
        new_right_t.T[None],
        new_moment[None],
        new_second[None],
    )


def per_device(grad_partial, *rest):
    _, _, rows, columns = grad_partial.shape
    fits = packed_fits(rows, columns, lax.axis_size("dp"))
    return (per_device_packed if fits else per_device_general)(grad_partial, *rest)


def per_device_general(
    grad_partial,
    owner,
    offset,
    left_factor,
    right_factor,
    left_basis,
    right_basis,
    momentum,
    second_moment,
):
    pieces = grad_partial[0]
    blocks, row_count, columns = pieces.shape
    groups = lax.axis_size("mp")
    replicas = lax.axis_size("dp")
    col_share = columns // replicas
    column = lax.axis_index("dp") * col_share
    my_group = lax.axis_index("mp")
    targets = lax.broadcasted_iota(jnp.int32, (groups, blocks), 0)
    positions = lax.broadcasted_iota(jnp.int32, (blocks, blocks), 0)
    routing = (owner[None, :] == targets).astype(jnp.float32)
    where_at = (offset[None, :] == positions).astype(jnp.float32)
    select = contract_last(routing, where_at).astype(jnp.bfloat16)
    occupied = jnp.any(owner == my_group)
    swapped = lax.all_to_all(grad_partial, "dp", split_axis=3, concat_axis=0, tiled=True)
    summed = jnp.sum(swapped.astype(jnp.float32), axis=0).astype(jnp.bfloat16)
    outgoing = jnp.dot(
        select, summed.reshape(blocks, row_count * col_share), preferred_element_type=jnp.float32
    )
    outgoing = outgoing.astype(jnp.bfloat16).reshape(groups, row_count, col_share)
    landed = lax.all_to_all(outgoing, "mp", split_axis=0, concat_axis=0, tiled=True)
    arrived = lax.all_gather(landed, "dp", axis=2, tiled=True)
    gradient = arrived.reshape(groups * row_count, columns)

    def refresh(operands):
        grad_in, left_fac, right_fac, lbasis, rbasis, moment, second = operands
        grad_rows = lax.dynamic_slice_in_dim(grad_in, column, col_share, 0)
        grad_cols = lax.dynamic_slice_in_dim(grad_in, column, col_share, 1)
        new_left = 0.95 * left_fac + 0.05 * contract_last(grad_in, grad_rows)
        new_right = 0.95 * right_fac + 0.05 * contract_first(grad_in, grad_cols)
        new_moment = (0.9 * moment.astype(jnp.float32) + 0.1 * grad_in.astype(jnp.float32)).astype(
            jnp.bfloat16
        )
        turned = contract_first(lbasis, grad_in).astype(jnp.bfloat16)
        rotated = jnp.dot(turned, rbasis, preferred_element_type=jnp.float32)
        turned_mom = contract_first(lbasis, new_moment).astype(jnp.bfloat16)
        rotated_mom = jnp.dot(turned_mom, rbasis, preferred_element_type=jnp.float32)
        new_second = 0.95 * second + 0.05 * rotated * rotated
        scaled = (rotated_mom / (jnp.sqrt(new_second) + 1e-08)).astype(jnp.bfloat16)
        unrotated = jnp.dot(lbasis, scaled, preferred_element_type=jnp.float32).astype(jnp.bfloat16)
        back_rows = lax.dynamic_slice_in_dim(rbasis, column, col_share, 0)
        return (new_left, new_right, new_moment, new_second, contract_last(unrotated, back_rows))

    def keep_old(operands):
        grad_in, left_fac, right_fac, lbasis, rbasis, moment, second = operands
        return (left_fac, right_fac, moment, second, jnp.zeros((columns, col_share), jnp.float32))

    operands = (
        gradient,
        left_factor[0],
        right_factor[0],
        left_basis[0],
        right_basis[0],
        momentum[0],
        second_moment[0],
    )
    new_left, new_right, new_moment, new_second, turned_cols = lax.cond(
        occupied, refresh, keep_old, operands
    )
    outgoing_back = turned_cols.astype(jnp.bfloat16).reshape(groups, row_count, col_share)
    returned = lax.all_to_all(outgoing_back, "mp", split_axis=0, concat_axis=0, tiled=True)
    update = contract_first(select, returned.reshape(groups, row_count * col_share)).astype(
        jnp.bfloat16
    )
    update = update.reshape(blocks, row_count, col_share)
    return (update, new_left[None], new_right[None], new_moment[None], new_second[None])


def solution(mesh):
    placed = (
        P("dp", None, "mp", None),
        P(),
        P(),
        P("mp", None, "dp"),
        P("mp", None, "dp"),
        P("mp", None, None),
        P("mp", None, None),
        P("mp", None, None),
        P("mp", None, None),
    )
    return jax.shard_map(
        per_device,
        mesh=mesh,
        in_specs=placed,
        out_specs=(
            P(None, "mp", "dp"),
            P("mp", None, "dp"),
            P("mp", None, "dp"),
            P("mp", None, None),
            P("mp", None, None),
        ),
        check_vma=False,
    )
```

```python
from functools import partial

import jax
import jax.numpy as jnp
from jax import lax
from jax.experimental import pallas as pl
from jax.experimental.pallas import tpu as pltpu
from jax.sharding import PartitionSpec as P

LANES = 128
SUBLANES = 8
VMEM = pl.BlockSpec(memory_space=pltpu.VMEM)
SMEM = pl.BlockSpec(memory_space=pltpu.SMEM)
FAR = pl.BlockSpec(memory_space=pltpu.HBM)
VMEM_GRANT = 16 * 2**20
CUT = 2 * LANES
STRIP = 48

def contract_first(matrix_a, matrix_b):
    return lax.dot_general(
        matrix_a, matrix_b, (((0,), (0,)), ((), ())), preferred_element_type=jnp.float32
    )


def contract_last(matrix_a, matrix_b):
    return lax.dot_general(
        matrix_a, matrix_b, (((1,), (1,)), ((), ())), preferred_element_type=jnp.float32
    )


def matmul(matrix_a, matrix_b):
    return jnp.dot(matrix_a, matrix_b, preferred_element_type=jnp.float32)


def tail_start(share):
    return jnp.where(share == 0, 0, 2 * share + 1) if not isinstance(share, int) else (
        0 if share == 0 else 2 * share + 1
    )


def packed_fits(rows, columns, replicas):
    width = columns // replicas - LANES
    return (
        columns == replicas * LANES + LANES // 2
        and rows == (2 * replicas + 1) * SUBLANES
        and width * replicas == LANES // 2
        and width % 16 == 0
        and LANES // width == rows // SUBLANES - 1
    )


def tail_places(blocks, rows):
    for b in range(blocks):
        for g in range(3):
            place = 3 * b + g
            yield b, g, blocks * rows + place // 2 * SUBLANES, place % 2 * (LANES // 2)


def chunk_rows(blocks, rows):
    return blocks * rows + -(-3 * blocks // 2) * SUBLANES


def pack_kernel(me_ref, grad_hbm, *refs, steps):
    outs, last, sems = refs[:-2], refs[-2], refs[-1]
    blocks, rows, columns = grad_hbm.shape
    half = LANES // 2
    replicas = columns // LANES
    shares = [lax.rem(me_ref[0] + step, replicas) for step in steps]
    copies = [
        pltpu.make_async_copy(
            grad_hbm.at[:, :, columns - half :], last, sems.at[len(outs) * blocks]
        )
    ]
    for n, out in enumerate(outs):
        col = pl.multiple_of(shares[n] * LANES, LANES)
        for b in range(blocks):
            copies.append(
                pltpu.make_async_copy(
                    grad_hbm.at[b, :, pl.ds(col, LANES)],
                    out.at[b * rows : (b + 1) * rows, :],
                    sems.at[n * blocks + b],
                )
            )
    for copy in copies:
        copy.start()
    copies[0].wait()
    for n, out in enumerate(outs):
        start = tail_start(shares[n])
        for b, g, row, lane in tail_places(blocks, rows):
            source = pl.multiple_of(
                jnp.minimum(start + g, rows // SUBLANES - 1) * SUBLANES, SUBLANES
            )
            out[row : row + SUBLANES, lane : lane + half] = last[b, pl.ds(source, SUBLANES), :]
    for copy in copies[1:]:
        copy.wait()


SHARE, GROUP, FOUND, SLOTS = 0, 1, 2, 3


def table_kernel(share_ref, group_ref, owner_ref, offset_ref, table):
    blocks = owner_ref.shape[0]
    groups = table.shape[0] - SLOTS - blocks
    table[SHARE] = share_ref[0]
    table[GROUP] = group_ref[0]
    found = jnp.int32(0)
    for b in range(blocks):
        found = jnp.where(owner_ref[b] == group_ref[0], 1, found)
    table[FOUND] = found
    for group in range(groups):
        table[SLOTS + group] = jnp.int32(0)
    for b in range(blocks):
        table[SLOTS + owner_ref[b]] = offset_ref[b]
        table[SLOTS + groups + offset_ref[b]] = groups - 1 - owner_ref[b]


def route_kernel(table, *refs):
    parts, out, summed = refs[:-2], refs[-2], refs[-1]
    replicas = len(parts)
    groups = out.shape[0] // replicas
    blocks = summed.shape[0]
    rows = summed.shape[1] - 2 * SUBLANES
    half = LANES // 2

    def add(*index):
        total = parts[0][index].astype(jnp.float32)
        for part in parts[1:]:
            total = total + part[index].astype(jnp.float32)
        return total.astype(jnp.bfloat16)

    for b in range(blocks):
        summed[b, :rows, :] = add(slice(b * rows, (b + 1) * rows), slice(None))
        summed[b, rows + SUBLANES :, half:] = jnp.zeros((SUBLANES, half), jnp.bfloat16)
    for b, g, row, lane in tail_places(blocks, rows):
        below = rows + (g % 2) * SUBLANES
        beside = (g // 2) * half
        summed[b, below : below + SUBLANES, beside : beside + half] = add(
            slice(row, row + SUBLANES), slice(lane, lane + half)
        )
    for group in range(groups):
        piece = summed[table[SLOTS + group]]
        for r in range(replicas):
            out[r * groups + group] = piece


def prepare_kernel(
    table, lbasis_hbm, rbasis_hbm, moment_hbm,
    lbasis_t, old_part, back_basis, lbasis, rbasis, moment, sems,
):
    found = table[FOUND]

    @pl.when(found == 1)
    def _():
        copies = [
            pltpu.make_async_copy(source, target, sems.at[n])
            for n, (source, target) in enumerate(
                ((lbasis_hbm, lbasis), (moment_hbm, moment), (rbasis_hbm, rbasis))
            )
        ]
        for copy in copies:
            copy.start()
        copies[0].wait()
        transposed = lbasis[...].T
        lbasis_t[...] = transposed
        copies[1].wait()
        turned = matmul(transposed, moment[...]).astype(jnp.bfloat16)
        copies[2].wait()
        old_part[...] = 0.9 * matmul(turned, rbasis[...])
        columns = rbasis.shape[0]
        col_share = columns // (columns // LANES)
        tail = col_share - LANES
        first = pl.multiple_of(table[SHARE] * col_share, tail)
        main = rbasis[pl.ds(first, LANES), :]
        last = rbasis[pl.ds(pl.multiple_of(first + LANES, tail), tail), :]
        back_basis[...] = jnp.concatenate([main] + [last] * (LANES // tail), axis=0).T


def assemble(arrived, gradient, groups, rows):
    half = LANES // 2
    tail = gradient.shape[1] - half
    for r in range(arrived.shape[0] // groups):
        start = tail_start(r)
        for m in range(groups):
            piece = r * groups + m
            base = m * rows
            gradient[base : base + rows, r * LANES : (r + 1) * LANES] = arrived[piece, :rows, :]
            for g in range(3 if r == 0 else 2):
                row = base + (start + g) * SUBLANES
                below = rows + (g % 2) * SUBLANES
                beside = (g // 2) * half
                gradient[row : row + SUBLANES, tail:] = arrived[
                    piece, below : below + SUBLANES, beside : beside + half
                ]


def owner_kernel(
    table, arrived, lbasis, rbasis, lbasis_t, old_part, back_basis, second,
    gradient, new_second, back_out, turned, scaled, back, sems,
):
    found = table[FOUND]
    groups = back.shape[0]
    copies = [
        pltpu.make_async_copy(back.at[n], back_out.at[n], sems.at[n]) for n in range(groups)
    ]
    columns = gradient.shape[1]
    rows = columns // groups

    @pl.when(found == 1)
    def _():
        assemble(arrived, gradient, groups, rows)
        turned[...] = matmul(lbasis_t[...], gradient[...]).astype(jnp.bfloat16)
        for low in range(0, columns, CUT):
            cols = slice(low, min(low + CUT, columns))
            rotated = matmul(turned[...], rbasis[:, cols])
            fresh = 0.95 * second[:, cols] + 0.05 * rotated * rotated
            new_second[:, cols] = fresh
            rotated_mom = old_part[:, cols] + 0.1 * rotated
            spread = fresh * lax.rsqrt(fresh) + 1e-08
            scaled[:, cols] = (rotated_mom * lax.rsqrt(spread * spread)).astype(jnp.bfloat16)
        total = matmul(scaled[...], back_basis[...])
        result = matmul(lbasis[...], total.astype(jnp.bfloat16))
        lane = lax.broadcasted_iota(jnp.int32, (SUBLANES, LANES), 1)
        tail_groups = rows // SUBLANES - 1
        width = LANES // tail_groups
        for m in range(groups):
            base = m * rows
            back[groups - 1 - m, :rows, :] = result[base : base + rows, :LANES].astype(jnp.bfloat16)
            mixed = result[base : base + SUBLANES, LANES:]
            for g in range(1, tail_groups):
                row = base + g * SUBLANES
                mixed = jnp.where(
                    lane < g * width, mixed, result[row : row + SUBLANES, LANES:]
                )
            back[groups - 1 - m, rows : rows + SUBLANES, :] = mixed.astype(jnp.bfloat16)
            back[groups - 1 - m, rows + SUBLANES :, :] = result[
                base + rows - SUBLANES : base + rows, LANES:
            ].astype(jnp.bfloat16)
        for copy in copies:
            copy.start()
        for copy in copies:
            copy.wait()

    @pl.when(found == 0)
    def _():
        new_second[...] = second[...]


def factor_kernel(
    table, gradient, second, moment_hbm, left_hbm, right_hbm,
    second_out, moment_out, left_out, right_out,
    moment, left_t, right_t, new_moment, new_left_t, new_right_t, sems,
):
    found = table[FOUND]
    col_share, columns = left_t.shape
    held = (moment, left_t, right_t)
    outs = (moment_out, left_out, right_out)

    def copies_of(first, sources, targets):
        return [
            pltpu.make_async_copy(a, b, sems.at[first + n])
            for n, (a, b) in enumerate(zip(sources, targets))
        ]

    loads = copies_of(0, (left_hbm, right_hbm, moment_hbm), (left_t, right_t, moment))
    fresh = copies_of(3, (new_left_t, new_right_t, new_moment), (left_out, right_out, moment_out))
    kept = copies_of(6, held, outs)
    second_copy = pltpu.make_async_copy(second, second_out, sems.at[9])
    for copy in loads + [second_copy]:
        copy.start()

    @pl.when(found == 1)
    def _():
        first = pl.multiple_of(table[SHARE] * col_share, 16)
        grad = gradient[...]
        left_term = 0.05 * contract_last(gradient[pl.ds(first, col_share), :], grad)
        picked = lax.broadcasted_iota(jnp.int32, (col_share, columns), 0) + first
        places = lax.broadcasted_iota(jnp.int32, (col_share, columns), 1)
        pick = jnp.where(picked == places, 1.0, 0.0).astype(jnp.bfloat16)
        grad_cols_t = contract_last(pick, grad).astype(jnp.bfloat16)
        right_term = 0.05 * matmul(grad_cols_t, grad)
        for copy in loads:
            copy.wait()
        new_left_t[...] = 0.95 * left_t[...] + left_term
        new_right_t[...] = 0.95 * right_t[...] + right_term
        for low in range(0, columns, STRIP):
            strip = slice(low, min(low + STRIP, columns))
            new_moment[strip, :] = (
                0.9 * moment[strip, :].astype(jnp.float32)
                + 0.1 * gradient[strip, :].astype(jnp.float32)
            ).astype(jnp.bfloat16)
        for copy in fresh:
            copy.start()
        for copy in fresh:
            copy.wait()

    @pl.when(found == 0)
    def _():
        for copy in loads:
            copy.wait()
        for copy in kept:
            copy.start()
        for copy in kept:
            copy.wait()

    second_copy.wait()


def place_kernel(table, returned, update, tails, sems):
    blocks, rows, col_share = update.shape
    groups = returned.shape[0]
    tail_groups = rows // SUBLANES - 1
    width = col_share - LANES
    copies = []
    for place in range(blocks):
        slot = table[SLOTS + groups + place]
        copies.append(
            pltpu.make_async_copy(
                returned.at[slot, :rows], update.at[place, :, :LANES], sems.at[place]
            )
        )
        copies[-1].start()
    for place in range(blocks):
        slot = table[SLOTS + groups + place]
        for g in range(tail_groups):
            tails[place, g * SUBLANES : (g + 1) * SUBLANES, :] = returned[
                slot, rows : rows + SUBLANES, g * width : (g + 1) * width
            ]
        tails[place, rows - SUBLANES :, :] = returned[slot, rows + SUBLANES :, :width]
        copies.append(
            pltpu.make_async_copy(
                tails.at[place], update.at[place, :, LANES:], sems.at[blocks + place]
            )
        )
        copies[-1].start()
    for copy in copies:
        copy.wait()


def run(name, kernel, scalars, arrays, outs, scratch=(), flops=0, sems=0, far=0, far_outs=0):
    moved = sum(a.size * a.dtype.itemsize for a in list(arrays) + list(outs))
    near = len(arrays) - far
    near_outs = len(outs) - far_outs
    return pl.pallas_call(
        kernel,
        out_shape=[pltpu.VMEM(o.shape, o.dtype) for o in outs[:near_outs]]
        + [pltpu.HBM(o.shape, o.dtype) for o in outs[near_outs:]],
        in_specs=[SMEM] * len(scalars) + [VMEM] * near + [FAR] * far,
        out_specs=[VMEM] * near_outs + [FAR] * far_outs,
        scratch_shapes=[pltpu.VMEM(o.shape, o.dtype) for o in scratch]
        + [pltpu.SemaphoreType.DMA((sems,))] * (sems > 0),
        compiler_params=pltpu.CompilerParams(vmem_limit_bytes=VMEM_GRANT),
        cost_estimate=pl.CostEstimate(flops=flops, bytes_accessed=moved, transcendentals=0),
        name=name,
    )(
        *scalars,
        *(pltpu.with_memory_space_constraint(a, pltpu.VMEM) for a in arrays[:near]),
        *(pltpu.with_memory_space_constraint(a, pltpu.HBM) for a in arrays[near:]),
    )


def per_device_packed(
    grad_partial,
    owner,
    offset,
    left_factor,
    right_factor,
    left_basis,
    right_basis,
    momentum,
    second_moment,
):
    pieces = grad_partial[0]
    blocks, rows, columns = pieces.shape
    groups = lax.axis_size("mp")
    replicas = lax.axis_size("dp")
    col_share = columns // replicas
    share = lax.axis_index("dp").astype(jnp.int32).reshape(1)
    group = lax.axis_index("mp").astype(jnp.int32).reshape(1)
    bf16, f32 = jnp.bfloat16, jnp.float32
    shape = jax.ShapeDtypeStruct
    packed = shape((blocks, rows + 2 * SUBLANES, LANES), bf16)
    sent = shape((chunk_rows(blocks, rows), LANES), bf16)
    square = (columns, columns)
    lbasis, rbasis, moment, second = left_basis[0], right_basis[0], momentum[0], second_moment[0]
    left_t, right_t = left_factor[0].T, right_factor[0].T
    product = 2 * columns**3

    middle = replicas // 2
    others = [step for step in range(1, replicas) if step != middle]

    def pack(name, steps):
        return run(
            name,
            partial(pack_kernel, steps=steps),
            [share],
            [pieces],
            [sent] * len(steps),
            scratch=[shape((blocks, rows, LANES // 2), bf16)],
            sems=len(steps) * blocks + 1,
            far=1,
        )

    def send(chunk, step):
        return lax.ppermute(chunk, "dp", [(i, (i + step) % replicas) for i in range(replicas)])

    first_sent = pack("pack_first", [middle])
    own, *rest = pack("pack_rest", [0] + others)
    parts = [own, send(first_sent[0], middle)]
    parts += [send(chunk, step) for chunk, step in zip(rest, others)]
    table = pl.pallas_call(
        table_kernel,
        out_shape=pltpu.SMEM((SLOTS + groups + blocks,), jnp.int32),
        in_specs=[SMEM] * 4,
        out_specs=SMEM,
        name="table",
    )(share, group, owner, offset)
    lbasis_t, old_part, back_basis = run(
        "prepare",
        prepare_kernel,
        [table],
        [lbasis, rbasis, moment],
        [shape(square, bf16), shape(square, f32), shape((columns, 2 * LANES), bf16)],
        scratch=[shape(square, bf16)] * 3,
        sems=3,
        far=3,
        flops=2 * product,
    )
    parts, lbasis_t, old_part, back_basis = lax.optimization_barrier(
        (parts, lbasis_t, old_part, back_basis)
    )
    (outgoing,) = run(
        "route",
        route_kernel,
        [table],
        parts,
        [shape((replicas * groups,) + packed.shape[1:], bf16)],
        scratch=[packed],
    )
    arrived = lax.all_to_all(outgoing, ("dp", "mp"), split_axis=0, concat_axis=0, tiled=True)
    chunks = shape((groups, rows + 2 * SUBLANES, LANES), bf16)
    factor_t = shape(left_t.shape, f32)
    gradient, new_second, back = run(
        "owner_step",
        owner_kernel,
        [table],
        [arrived, lbasis, rbasis, lbasis_t, old_part, back_basis, second],
        [shape(square, bf16), shape(square, f32), chunks],
        scratch=[shape(square, bf16)] * 2 + [chunks],
        sems=groups,
        far_outs=1,
        flops=3 * product,
    )
    returned = lax.all_to_all(
        back,
        "mp",
        split_axis=0,
        concat_axis=0,
        tiled=True,
        axis_index_groups=[list(range(groups))[::-1]],
    )
    new_second, new_moment, new_left_t, new_right_t = run(
        "factors",
        factor_kernel,
        [table],
        [gradient, new_second, moment, left_t, right_t],
        [shape(square, f32), shape(square, bf16), factor_t, factor_t],
        scratch=[shape(square, bf16), factor_t, factor_t] * 2,
        sems=10,
        far=3,
        far_outs=4,
        flops=product,
    )
    (update,) = run(
        "place",
        place_kernel,
        [table],
        [returned],
        [shape((blocks, rows, col_share), bf16)],
        scratch=[shape((blocks, rows, col_share - LANES), bf16)],
        sems=2 * blocks,
        far_outs=1,
    )
    return (
        update,
        new_left_t.T[None],
        new_right_t.T[None],
        new_moment[None],
        new_second[None],
    )


def per_device(grad_partial, *rest):
    _, _, rows, columns = grad_partial.shape
    fits = packed_fits(rows, columns, lax.axis_size("dp"))
    return (per_device_packed if fits else per_device_general)(grad_partial, *rest)


def per_device_general(
    grad_partial,
    owner,
    offset,
    left_factor,
    right_factor,
    left_basis,
    right_basis,
    momentum,
    second_moment,
):
    pieces = grad_partial[0]
    blocks, row_count, columns = pieces.shape
    groups = lax.axis_size("mp")
    replicas = lax.axis_size("dp")
    col_share = columns // replicas
    column = lax.axis_index("dp") * col_share
    my_group = lax.axis_index("mp")
    targets = lax.broadcasted_iota(jnp.int32, (groups, blocks), 0)
    positions = lax.broadcasted_iota(jnp.int32, (blocks, blocks), 0)
    routing = (owner[None, :] == targets).astype(jnp.float32)
    where_at = (offset[None, :] == positions).astype(jnp.float32)
    select = contract_last(routing, where_at).astype(jnp.bfloat16)
    occupied = jnp.any(owner == my_group)
    swapped = lax.all_to_all(grad_partial, "dp", split_axis=3, concat_axis=0, tiled=True)
    summed = jnp.sum(swapped.astype(jnp.float32), axis=0).astype(jnp.bfloat16)
    outgoing = jnp.dot(
        select, summed.reshape(blocks, row_count * col_share), preferred_element_type=jnp.float32
    )
    outgoing = outgoing.astype(jnp.bfloat16).reshape(groups, row_count, col_share)
    landed = lax.all_to_all(outgoing, "mp", split_axis=0, concat_axis=0, tiled=True)
    arrived = lax.all_gather(landed, "dp", axis=2, tiled=True)
    gradient = arrived.reshape(groups * row_count, columns)

    def refresh(operands):
        grad_in, left_fac, right_fac, lbasis, rbasis, moment, second = operands
        grad_rows = lax.dynamic_slice_in_dim(grad_in, column, col_share, 0)
        grad_cols = lax.dynamic_slice_in_dim(grad_in, column, col_share, 1)
        new_left = 0.95 * left_fac + 0.05 * contract_last(grad_in, grad_rows)
        new_right = 0.95 * right_fac + 0.05 * contract_first(grad_in, grad_cols)
        new_moment = (0.9 * moment.astype(jnp.float32) + 0.1 * grad_in.astype(jnp.float32)).astype(
            jnp.bfloat16
        )
        turned = contract_first(lbasis, grad_in).astype(jnp.bfloat16)
        rotated = jnp.dot(turned, rbasis, preferred_element_type=jnp.float32)
        turned_mom = contract_first(lbasis, new_moment).astype(jnp.bfloat16)
        rotated_mom = jnp.dot(turned_mom, rbasis, preferred_element_type=jnp.float32)
        new_second = 0.95 * second + 0.05 * rotated * rotated
        scaled = (rotated_mom / (jnp.sqrt(new_second) + 1e-08)).astype(jnp.bfloat16)
        unrotated = jnp.dot(lbasis, scaled, preferred_element_type=jnp.float32).astype(jnp.bfloat16)
        back_rows = lax.dynamic_slice_in_dim(rbasis, column, col_share, 0)
        return (new_left, new_right, new_moment, new_second, contract_last(unrotated, back_rows))

    def keep_old(operands):
        grad_in, left_fac, right_fac, lbasis, rbasis, moment, second = operands
        return (left_fac, right_fac, moment, second, jnp.zeros((columns, col_share), jnp.float32))

    operands = (
        gradient,
        left_factor[0],
        right_factor[0],
        left_basis[0],
        right_basis[0],
        momentum[0],
        second_moment[0],
    )
    new_left, new_right, new_moment, new_second, turned_cols = lax.cond(
        occupied, refresh, keep_old, operands
    )
    outgoing_back = turned_cols.astype(jnp.bfloat16).reshape(groups, row_count, col_share)
    returned = lax.all_to_all(outgoing_back, "mp", split_axis=0, concat_axis=0, tiled=True)
    update = contract_first(select, returned.reshape(groups, row_count * col_share)).astype(
        jnp.bfloat16
    )
    update = update.reshape(blocks, row_count, col_share)
    return (update, new_left[None], new_right[None], new_moment[None], new_second[None])


def solution(mesh):
    placed = (
        P("dp", None, "mp", None),
        P(),
        P(),
        P("mp", None, "dp"),
        P("mp", None, "dp"),
        P("mp", None, None),
        P("mp", None, None),
        P("mp", None, None),
        P("mp", None, None),
    )
    return jax.shard_map(
        per_device,
        mesh=mesh,
        in_specs=placed,
        out_specs=(
            P(None, "mp", "dp"),
            P("mp", None, "dp"),
            P("mp", None, "dp"),
            P("mp", None, None),
            P("mp", None, None),
        ),
        check_vma=False,
    )
```

```python
import jax
import jax.numpy as jnp
from jax import lax
from jax.experimental import pallas as pl
from jax.experimental.pallas import tpu as pltpu
from jax.sharding import PartitionSpec as P

LANES = 128
SUBLANES = 8
VMEM = pl.BlockSpec(memory_space=pltpu.VMEM)
SMEM = pl.BlockSpec(memory_space=pltpu.SMEM)
FAR = pl.BlockSpec(memory_space=pltpu.HBM)
VMEM_GRANT = 16 * 2**20
CUT = 2 * LANES
STRIP = 48

def contract_first(matrix_a, matrix_b):
    return lax.dot_general(
        matrix_a, matrix_b, (((0,), (0,)), ((), ())), preferred_element_type=jnp.float32
    )


def contract_last(matrix_a, matrix_b):
    return lax.dot_general(
        matrix_a, matrix_b, (((1,), (1,)), ((), ())), preferred_element_type=jnp.float32
    )


def matmul(matrix_a, matrix_b):
    return jnp.dot(matrix_a, matrix_b, preferred_element_type=jnp.float32)


def tail_start(share):
    return jnp.where(share == 0, 0, 2 * share + 1) if not isinstance(share, int) else (
        0 if share == 0 else 2 * share + 1
    )


def packed_fits(rows, columns, replicas):
    width = columns // replicas - LANES
    return (
        columns == replicas * LANES + LANES // 2
        and rows == (2 * replicas + 1) * SUBLANES
        and width * replicas == LANES // 2
        and width % 16 == 0
        and LANES // width == rows // SUBLANES - 1
    )


def tail_places(blocks, rows):
    for b in range(blocks):
        for g in range(3):
            place = 3 * b + g
            yield b, g, blocks * rows + place // 2 * SUBLANES, place % 2 * (LANES // 2)


def chunk_rows(blocks, rows):
    return blocks * rows + -(-3 * blocks // 2) * SUBLANES


def pack_kernel(me_ref, grad_hbm, *refs):
    outs, last, sems = refs[:-2], refs[-2], refs[-1]
    replicas = len(outs)
    blocks, rows, columns = grad_hbm.shape
    half = LANES // 2
    shares = [lax.rem(me_ref[0] + step, replicas) for step in range(replicas)]
    copies = [
        pltpu.make_async_copy(
            grad_hbm.at[:, :, columns - half :], last, sems.at[replicas * blocks]
        )
    ]
    for step in range(replicas):
        col = pl.multiple_of(shares[step] * LANES, LANES)
        for b in range(blocks):
            copies.append(
                pltpu.make_async_copy(
                    grad_hbm.at[b, :, pl.ds(col, LANES)],
                    outs[step].at[b * rows : (b + 1) * rows, :],
                    sems.at[step * blocks + b],
                )
            )
    for copy in copies:
        copy.start()
    copies[0].wait()
    for step in range(replicas):
        start = tail_start(shares[step])
        for b, g, row, lane in tail_places(blocks, rows):
            source = pl.multiple_of(
                jnp.minimum(start + g, rows // SUBLANES - 1) * SUBLANES, SUBLANES
            )
            outs[step][row : row + SUBLANES, lane : lane + half] = last[
                b, pl.ds(source, SUBLANES), :
            ]
    for copy in copies[1:]:
        copy.wait()


SHARE, GROUP, FOUND, SLOTS = 0, 1, 2, 3


def table_kernel(share_ref, group_ref, owner_ref, offset_ref, table):
    blocks = owner_ref.shape[0]
    groups = table.shape[0] - SLOTS - blocks
    table[SHARE] = share_ref[0]
    table[GROUP] = group_ref[0]
    found = jnp.int32(0)
    for b in range(blocks):
        found = jnp.where(owner_ref[b] == group_ref[0], 1, found)
    table[FOUND] = found
    for group in range(groups):
        table[SLOTS + group] = jnp.int32(0)
    for b in range(blocks):
        table[SLOTS + owner_ref[b]] = offset_ref[b]
        table[SLOTS + groups + offset_ref[b]] = groups - 1 - owner_ref[b]


def route_kernel(table, *refs):
    parts, out, summed = refs[:-2], refs[-2], refs[-1]
    replicas = len(parts)
    groups = out.shape[0] // replicas
    blocks = summed.shape[0]
    rows = summed.shape[1] - 2 * SUBLANES
    half = LANES // 2

    def add(*index):
        total = parts[0][index].astype(jnp.float32)
        for part in parts[1:]:
            total = total + part[index].astype(jnp.float32)
        return total.astype(jnp.bfloat16)

    for b in range(blocks):
        summed[b, :rows, :] = add(slice(b * rows, (b + 1) * rows), slice(None))
        summed[b, rows + SUBLANES :, half:] = jnp.zeros((SUBLANES, half), jnp.bfloat16)
    for b, g, row, lane in tail_places(blocks, rows):
        below = rows + (g % 2) * SUBLANES
        beside = (g // 2) * half
        summed[b, below : below + SUBLANES, beside : beside + half] = add(
            slice(row, row + SUBLANES), slice(lane, lane + half)
        )
    for group in range(groups):
        piece = summed[table[SLOTS + group]]
        for r in range(replicas):
            out[r * groups + group] = piece


def prepare_kernel(
    table, lbasis_hbm, rbasis_hbm, moment_hbm,
    lbasis_t, old_part, back_basis, lbasis, rbasis, moment, sems,
):
    found = table[FOUND]

    @pl.when(found == 1)
    def _():
        copies = [
            pltpu.make_async_copy(source, target, sems.at[n])
            for n, (source, target) in enumerate(
                ((lbasis_hbm, lbasis), (moment_hbm, moment), (rbasis_hbm, rbasis))
            )
        ]
        for copy in copies:
            copy.start()
        copies[0].wait()
        transposed = lbasis[...].T
        lbasis_t[...] = transposed
        copies[1].wait()
        turned = matmul(transposed, moment[...]).astype(jnp.bfloat16)
        copies[2].wait()
        old_part[...] = 0.9 * matmul(turned, rbasis[...])
        columns = rbasis.shape[0]
        col_share = columns // (columns // LANES)
        tail = col_share - LANES
        first = pl.multiple_of(table[SHARE] * col_share, tail)
        main = rbasis[pl.ds(first, LANES), :]
        last = rbasis[pl.ds(pl.multiple_of(first + LANES, tail), tail), :]
        back_basis[...] = jnp.concatenate([main] + [last] * (LANES // tail), axis=0).T


def assemble(arrived, gradient, groups, rows):
    half = LANES // 2
    tail = gradient.shape[1] - half
    for r in range(arrived.shape[0] // groups):
        start = tail_start(r)
        for m in range(groups):
            piece = r * groups + m
            base = m * rows
            gradient[base : base + rows, r * LANES : (r + 1) * LANES] = arrived[piece, :rows, :]
            for g in range(3 if r == 0 else 2):
                row = base + (start + g) * SUBLANES
                below = rows + (g % 2) * SUBLANES
                beside = (g // 2) * half
                gradient[row : row + SUBLANES, tail:] = arrived[
                    piece, below : below + SUBLANES, beside : beside + half
                ]


def owner_kernel(
    table, arrived, lbasis, rbasis, lbasis_t, old_part, back_basis, second,
    gradient, new_second, back_out, turned, scaled, back, sems,
):
    found = table[FOUND]
    groups = back.shape[0]
    copies = [
        pltpu.make_async_copy(back.at[n], back_out.at[n], sems.at[n]) for n in range(groups)
    ]
    columns = gradient.shape[1]
    rows = columns // groups

    @pl.when(found == 1)
    def _():
        assemble(arrived, gradient, groups, rows)
        turned[...] = matmul(lbasis_t[...], gradient[...]).astype(jnp.bfloat16)
        for low in range(0, columns, CUT):
            cols = slice(low, min(low + CUT, columns))
            rotated = matmul(turned[...], rbasis[:, cols])
            fresh = 0.95 * second[:, cols] + 0.05 * rotated * rotated
            new_second[:, cols] = fresh
            rotated_mom = old_part[:, cols] + 0.1 * rotated
            spread = fresh * lax.rsqrt(fresh) + 1e-08
            scaled[:, cols] = (rotated_mom * lax.rsqrt(spread * spread)).astype(jnp.bfloat16)
        total = matmul(scaled[...], back_basis[...])
        sums = total.astype(jnp.bfloat16)
        lane = lax.broadcasted_iota(jnp.int32, (SUBLANES, LANES), 1)
        tail_groups = rows // SUBLANES - 1
        width = LANES // tail_groups
        half_groups = groups // 2
        for side in range(2):
            first = side * half_groups
            result = matmul(lbasis[first * rows : (first + half_groups) * rows, :], sums)
            for m in range(first, first + half_groups):
                off = (m - first) * rows
                back[groups - 1 - m, :rows, :] = result[off : off + rows, :LANES].astype(jnp.bfloat16)
                mixed = result[off : off + SUBLANES, LANES:]
                for g in range(1, tail_groups):
                    row = off + g * SUBLANES
                    mixed = jnp.where(
                        lane < g * width, mixed, result[row : row + SUBLANES, LANES:]
                    )
                back[groups - 1 - m, rows : rows + SUBLANES, :] = mixed.astype(jnp.bfloat16)
                back[groups - 1 - m, rows + SUBLANES :, :] = result[
                    off + rows - SUBLANES : off + rows, LANES:
                ].astype(jnp.bfloat16)
            for m in range(first, first + half_groups):
                copies[groups - 1 - m].start()
        for copy in copies:
            copy.wait()

    @pl.when(found == 0)
    def _():
        new_second[...] = second[...]


def factor_kernel(
    table, gradient, second, moment_hbm, left_hbm, right_hbm,
    second_out, moment_out, left_out, right_out,
    moment, left_t, right_t, new_moment, new_left_t, new_right_t, sems,
):
    found = table[FOUND]
    col_share, columns = left_t.shape
    held = (moment, left_t, right_t)
    outs = (moment_out, left_out, right_out)

    def copies_of(first, sources, targets):
        return [
            pltpu.make_async_copy(a, b, sems.at[first + n])
            for n, (a, b) in enumerate(zip(sources, targets))
        ]

    loads = copies_of(0, (left_hbm, right_hbm, moment_hbm), (left_t, right_t, moment))
    fresh = copies_of(3, (new_left_t, new_right_t, new_moment), (left_out, right_out, moment_out))
    kept = copies_of(6, held, outs)
    second_copy = pltpu.make_async_copy(second, second_out, sems.at[9])
    for copy in loads + [second_copy]:
        copy.start()

    @pl.when(found == 1)
    def _():
        first = pl.multiple_of(table[SHARE] * col_share, 16)
        grad = gradient[...]
        left_term = 0.05 * contract_last(gradient[pl.ds(first, col_share), :], grad)
        picked = lax.broadcasted_iota(jnp.int32, (col_share, columns), 0) + first
        places = lax.broadcasted_iota(jnp.int32, (col_share, columns), 1)
        pick = jnp.where(picked == places, 1.0, 0.0).astype(jnp.bfloat16)
        grad_cols_t = contract_last(pick, grad).astype(jnp.bfloat16)
        right_term = 0.05 * matmul(grad_cols_t, grad)
        for copy in loads:
            copy.wait()
        new_left_t[...] = 0.95 * left_t[...] + left_term
        new_right_t[...] = 0.95 * right_t[...] + right_term
        for low in range(0, columns, STRIP):
            strip = slice(low, min(low + STRIP, columns))
            new_moment[strip, :] = (
                0.9 * moment[strip, :].astype(jnp.float32)
                + 0.1 * gradient[strip, :].astype(jnp.float32)
            ).astype(jnp.bfloat16)
        for copy in fresh:
            copy.start()
        for copy in fresh:
            copy.wait()

    @pl.when(found == 0)
    def _():
        for copy in loads:
            copy.wait()
        for copy in kept:
            copy.start()
        for copy in kept:
            copy.wait()

    second_copy.wait()


def place_kernel(table, returned, update, tails, sems):
    blocks, rows, col_share = update.shape
    groups = returned.shape[0]
    tail_groups = rows // SUBLANES - 1
    width = col_share - LANES
    copies = []
    for place in range(blocks):
        slot = table[SLOTS + groups + place]
        copies.append(
            pltpu.make_async_copy(
                returned.at[slot, :rows], update.at[place, :, :LANES], sems.at[place]
            )
        )
        copies[-1].start()
    for place in range(blocks):
        slot = table[SLOTS + groups + place]
        for g in range(tail_groups):
            tails[place, g * SUBLANES : (g + 1) * SUBLANES, :] = returned[
                slot, rows : rows + SUBLANES, g * width : (g + 1) * width
            ]
        tails[place, rows - SUBLANES :, :] = returned[slot, rows + SUBLANES :, :width]
        copies.append(
            pltpu.make_async_copy(
                tails.at[place], update.at[place, :, LANES:], sems.at[blocks + place]
            )
        )
        copies[-1].start()
    for copy in copies:
        copy.wait()


def run(name, kernel, scalars, arrays, outs, scratch=(), flops=0, sems=0, far=0, far_outs=0):
    moved = sum(a.size * a.dtype.itemsize for a in list(arrays) + list(outs))
    near = len(arrays) - far
    near_outs = len(outs) - far_outs
    return pl.pallas_call(
        kernel,
        out_shape=[pltpu.VMEM(o.shape, o.dtype) for o in outs[:near_outs]]
        + [pltpu.HBM(o.shape, o.dtype) for o in outs[near_outs:]],
        in_specs=[SMEM] * len(scalars) + [VMEM] * near + [FAR] * far,
        out_specs=[VMEM] * near_outs + [FAR] * far_outs,
        scratch_shapes=[pltpu.VMEM(o.shape, o.dtype) for o in scratch]
        + [pltpu.SemaphoreType.DMA((sems,))] * (sems > 0),
        compiler_params=pltpu.CompilerParams(vmem_limit_bytes=VMEM_GRANT),
        cost_estimate=pl.CostEstimate(flops=flops, bytes_accessed=moved, transcendentals=0),
        name=name,
    )(
        *scalars,
        *(pltpu.with_memory_space_constraint(a, pltpu.VMEM) for a in arrays[:near]),
        *(pltpu.with_memory_space_constraint(a, pltpu.HBM) for a in arrays[near:]),
    )


def per_device_packed(
    grad_partial,
    owner,
    offset,
    left_factor,
    right_factor,
    left_basis,
    right_basis,
    momentum,
    second_moment,
):
    pieces = grad_partial[0]
    blocks, rows, columns = pieces.shape
    groups = lax.axis_size("mp")
    replicas = lax.axis_size("dp")
    col_share = columns // replicas
    share = lax.axis_index("dp").astype(jnp.int32).reshape(1)
    group = lax.axis_index("mp").astype(jnp.int32).reshape(1)
    bf16, f32 = jnp.bfloat16, jnp.float32
    shape = jax.ShapeDtypeStruct
    packed = shape((blocks, rows + 2 * SUBLANES, LANES), bf16)
    sent = shape((chunk_rows(blocks, rows), LANES), bf16)
    square = (columns, columns)
    lbasis, rbasis, moment, second = left_basis[0], right_basis[0], momentum[0], second_moment[0]
    left_t, right_t = left_factor[0].T, right_factor[0].T
    product = 2 * columns**3

    parts = run(
        "pack",
        pack_kernel,
        [share],
        [pieces],
        [sent] * replicas,
        scratch=[shape((blocks, rows, LANES // 2), bf16)],
        sems=replicas * blocks + 1,
        far=1,
    )
    parts = [parts[0]] + [
        lax.ppermute(parts[s], "dp", [(i, (i + s) % replicas) for i in range(replicas)])
        for s in range(1, replicas)
    ]
    table = pl.pallas_call(
        table_kernel,
        out_shape=pltpu.SMEM((SLOTS + groups + blocks,), jnp.int32),
        in_specs=[SMEM] * 4,
        out_specs=SMEM,
        name="table",
    )(share, group, owner, offset)
    lbasis_t, old_part, back_basis = run(
        "prepare",
        prepare_kernel,
        [table],
        [lbasis, rbasis, moment],
        [shape(square, bf16), shape(square, f32), shape((columns, 2 * LANES), bf16)],
        scratch=[shape(square, bf16)] * 3,
        sems=3,
        far=3,
        flops=2 * product,
    )
    parts, lbasis_t, old_part, back_basis = lax.optimization_barrier(
        (parts, lbasis_t, old_part, back_basis)
    )
    (outgoing,) = run(
        "route",
        route_kernel,
        [table],
        parts,
        [shape((replicas * groups,) + packed.shape[1:], bf16)],
        scratch=[packed],
    )
    arrived = lax.all_to_all(outgoing, ("dp", "mp"), split_axis=0, concat_axis=0, tiled=True)
    chunks = shape((groups, rows + 2 * SUBLANES, LANES), bf16)
    factor_t = shape(left_t.shape, f32)
    gradient, new_second, back = run(
        "owner_step",
        owner_kernel,
        [table],
        [arrived, lbasis, rbasis, lbasis_t, old_part, back_basis, second],
        [shape(square, bf16), shape(square, f32), chunks],
        scratch=[shape(square, bf16)] * 2 + [chunks],
        sems=groups,
        far_outs=1,
        flops=3 * product,
    )
    returned = lax.all_to_all(
        back,
        "mp",
        split_axis=0,
        concat_axis=0,
        tiled=True,
        axis_index_groups=[list(range(groups))[::-1]],
    )
    new_second, new_moment, new_left_t, new_right_t = run(
        "factors",
        factor_kernel,
        [table],
        [gradient, new_second, moment, left_t, right_t],
        [shape(square, f32), shape(square, bf16), factor_t, factor_t],
        scratch=[shape(square, bf16), factor_t, factor_t] * 2,
        sems=10,
        far=3,
        far_outs=4,
        flops=product,
    )
    (update,) = run(
        "place",
        place_kernel,
        [table],
        [returned],
        [shape((blocks, rows, col_share), bf16)],
        scratch=[shape((blocks, rows, col_share - LANES), bf16)],
        sems=2 * blocks,
        far_outs=1,
    )
    return (
        update,
        new_left_t.T[None],
        new_right_t.T[None],
        new_moment[None],
        new_second[None],
    )


def per_device(grad_partial, *rest):
    _, _, rows, columns = grad_partial.shape
    fits = packed_fits(rows, columns, lax.axis_size("dp"))
    return (per_device_packed if fits else per_device_general)(grad_partial, *rest)


def per_device_general(
    grad_partial,
    owner,
    offset,
    left_factor,
    right_factor,
    left_basis,
    right_basis,
    momentum,
    second_moment,
):
    pieces = grad_partial[0]
    blocks, row_count, columns = pieces.shape
    groups = lax.axis_size("mp")
    replicas = lax.axis_size("dp")
    col_share = columns // replicas
    column = lax.axis_index("dp") * col_share
    my_group = lax.axis_index("mp")
    targets = lax.broadcasted_iota(jnp.int32, (groups, blocks), 0)
    positions = lax.broadcasted_iota(jnp.int32, (blocks, blocks), 0)
    routing = (owner[None, :] == targets).astype(jnp.float32)
    where_at = (offset[None, :] == positions).astype(jnp.float32)
    select = contract_last(routing, where_at).astype(jnp.bfloat16)
    occupied = jnp.any(owner == my_group)
    swapped = lax.all_to_all(grad_partial, "dp", split_axis=3, concat_axis=0, tiled=True)
    summed = jnp.sum(swapped.astype(jnp.float32), axis=0).astype(jnp.bfloat16)
    outgoing = jnp.dot(
        select, summed.reshape(blocks, row_count * col_share), preferred_element_type=jnp.float32
    )
    outgoing = outgoing.astype(jnp.bfloat16).reshape(groups, row_count, col_share)
    landed = lax.all_to_all(outgoing, "mp", split_axis=0, concat_axis=0, tiled=True)
    arrived = lax.all_gather(landed, "dp", axis=2, tiled=True)
    gradient = arrived.reshape(groups * row_count, columns)

    def refresh(operands):
        grad_in, left_fac, right_fac, lbasis, rbasis, moment, second = operands
        grad_rows = lax.dynamic_slice_in_dim(grad_in, column, col_share, 0)
        grad_cols = lax.dynamic_slice_in_dim(grad_in, column, col_share, 1)
        new_left = 0.95 * left_fac + 0.05 * contract_last(grad_in, grad_rows)
        new_right = 0.95 * right_fac + 0.05 * contract_first(grad_in, grad_cols)
        new_moment = (0.9 * moment.astype(jnp.float32) + 0.1 * grad_in.astype(jnp.float32)).astype(
            jnp.bfloat16
        )
        turned = contract_first(lbasis, grad_in).astype(jnp.bfloat16)
        rotated = jnp.dot(turned, rbasis, preferred_element_type=jnp.float32)
        turned_mom = contract_first(lbasis, new_moment).astype(jnp.bfloat16)
        rotated_mom = jnp.dot(turned_mom, rbasis, preferred_element_type=jnp.float32)
        new_second = 0.95 * second + 0.05 * rotated * rotated
        scaled = (rotated_mom / (jnp.sqrt(new_second) + 1e-08)).astype(jnp.bfloat16)
        unrotated = jnp.dot(lbasis, scaled, preferred_element_type=jnp.float32).astype(jnp.bfloat16)
        back_rows = lax.dynamic_slice_in_dim(rbasis, column, col_share, 0)
        return (new_left, new_right, new_moment, new_second, contract_last(unrotated, back_rows))

    def keep_old(operands):
        grad_in, left_fac, right_fac, lbasis, rbasis, moment, second = operands
        return (left_fac, right_fac, moment, second, jnp.zeros((columns, col_share), jnp.float32))

    operands = (
        gradient,
        left_factor[0],
        right_factor[0],
        left_basis[0],
        right_basis[0],
        momentum[0],
        second_moment[0],
    )
    new_left, new_right, new_moment, new_second, turned_cols = lax.cond(
        occupied, refresh, keep_old, operands
    )
    outgoing_back = turned_cols.astype(jnp.bfloat16).reshape(groups, row_count, col_share)
    returned = lax.all_to_all(outgoing_back, "mp", split_axis=0, concat_axis=0, tiled=True)
    update = contract_first(select, returned.reshape(groups, row_count * col_share)).astype(
        jnp.bfloat16
    )
    update = update.reshape(blocks, row_count, col_share)
    return (update, new_left[None], new_right[None], new_moment[None], new_second[None])


def solution(mesh):
    placed = (
        P("dp", None, "mp", None),
        P(),
        P(),
        P("mp", None, "dp"),
        P("mp", None, "dp"),
        P("mp", None, None),
        P("mp", None, None),
        P("mp", None, None),
        P("mp", None, None),
    )
    return jax.shard_map(
        per_device,
        mesh=mesh,
        in_specs=placed,
        out_specs=(
            P(None, "mp", "dp"),
            P("mp", None, "dp"),
            P("mp", None, "dp"),
            P("mp", None, None),
            P("mp", None, None),
        ),
        check_vma=False,
    )
```

```python
import jax
import jax.numpy as jnp
from jax import lax
from jax.experimental import pallas as pl
from jax.experimental.pallas import tpu as pltpu
from jax.sharding import PartitionSpec as P

LANES = 128
SUBLANES = 8
VMEM = pl.BlockSpec(memory_space=pltpu.VMEM)
SMEM = pl.BlockSpec(memory_space=pltpu.SMEM)
FAR = pl.BlockSpec(memory_space=pltpu.HBM)
VMEM_GRANT = 16 * 2**20
CUT = 2 * LANES
STRIP = 48

def contract_first(matrix_a, matrix_b):
    return lax.dot_general(
        matrix_a, matrix_b, (((0,), (0,)), ((), ())), preferred_element_type=jnp.float32
    )


def contract_last(matrix_a, matrix_b):
    return lax.dot_general(
        matrix_a, matrix_b, (((1,), (1,)), ((), ())), preferred_element_type=jnp.float32
    )


def matmul(matrix_a, matrix_b):
    return jnp.dot(matrix_a, matrix_b, preferred_element_type=jnp.float32)


def tail_start(share):
    return jnp.where(share == 0, 0, 2 * share + 1) if not isinstance(share, int) else (
        0 if share == 0 else 2 * share + 1
    )


def packed_fits(rows, columns, replicas):
    width = columns // replicas - LANES
    return (
        columns == replicas * LANES + LANES // 2
        and rows == (2 * replicas + 1) * SUBLANES
        and width * replicas == LANES // 2
        and width % 16 == 0
        and LANES // width == rows // SUBLANES - 1
    )


def tail_places(blocks, rows):
    for b in range(blocks):
        for g in range(3):
            place = 3 * b + g
            yield b, g, blocks * rows + place // 2 * SUBLANES, place % 2 * (LANES // 2)


def chunk_rows(blocks, rows):
    return blocks * rows + -(-3 * blocks // 2) * SUBLANES


def pack_kernel(me_ref, grad_hbm, *refs):
    outs, grad, sems = refs[:-2], refs[-2], refs[-1]
    replicas = len(outs)
    blocks, rows, columns = grad_hbm.shape
    half = LANES // 2
    copies = [
        pltpu.make_async_copy(grad_hbm.at[b], grad.at[b], sems.at[b]) for b in range(blocks)
    ]
    for copy in copies:
        copy.start()
    shares = [lax.rem(me_ref[0] + step, replicas) for step in range(replicas)]
    places = list(tail_places(blocks, rows))
    for b in range(blocks):
        copies[b].wait()
        for step in range(replicas):
            col = pl.multiple_of(shares[step] * LANES, LANES)
            outs[step][b * rows : (b + 1) * rows, :] = grad[b, :, pl.ds(col, LANES)]
            start = tail_start(shares[step])
            for _, g, row, lane in places[3 * b : 3 * b + 3]:
                source = pl.multiple_of(
                    jnp.minimum(start + g, rows // SUBLANES - 1) * SUBLANES, SUBLANES
                )
                outs[step][row : row + SUBLANES, lane : lane + half] = grad[
                    b, pl.ds(source, SUBLANES), columns - half :
                ]


SHARE, GROUP, FOUND, SLOTS = 0, 1, 2, 3


def table_kernel(share_ref, group_ref, owner_ref, offset_ref, table):
    blocks = owner_ref.shape[0]
    groups = table.shape[0] - SLOTS - blocks
    table[SHARE] = share_ref[0]
    table[GROUP] = group_ref[0]
    found = jnp.int32(0)
    for b in range(blocks):
        found = jnp.where(owner_ref[b] == group_ref[0], 1, found)
    table[FOUND] = found
    for group in range(groups):
        table[SLOTS + group] = jnp.int32(0)
    for b in range(blocks):
        table[SLOTS + owner_ref[b]] = offset_ref[b]
        table[SLOTS + groups + offset_ref[b]] = groups - 1 - owner_ref[b]


def route_kernel(table, *refs):
    parts, out, summed = refs[:-2], refs[-2], refs[-1]
    replicas = len(parts)
    groups = out.shape[0] // replicas
    blocks = summed.shape[0]
    rows = summed.shape[1] - 2 * SUBLANES
    half = LANES // 2

    def add(*index):
        total = parts[0][index].astype(jnp.float32)
        for part in parts[1:]:
            total = total + part[index].astype(jnp.float32)
        return total.astype(jnp.bfloat16)

    for b in range(blocks):
        summed[b, :rows, :] = add(slice(b * rows, (b + 1) * rows), slice(None))
        summed[b, rows + SUBLANES :, half:] = jnp.zeros((SUBLANES, half), jnp.bfloat16)
    for b, g, row, lane in tail_places(blocks, rows):
        below = rows + (g % 2) * SUBLANES
        beside = (g // 2) * half
        summed[b, below : below + SUBLANES, beside : beside + half] = add(
            slice(row, row + SUBLANES), slice(lane, lane + half)
        )
    for group in range(groups):
        piece = summed[table[SLOTS + group]]
        for r in range(replicas):
            out[r * groups + group] = piece


def prepare_kernel(
    table, lbasis_hbm, rbasis_hbm, moment_hbm,
    lbasis_t, old_part, back_basis, lbasis, rbasis, moment, sems,
):
    found = table[FOUND]

    @pl.when(found == 1)
    def _():
        copies = [
            pltpu.make_async_copy(source, target, sems.at[n])
            for n, (source, target) in enumerate(
                ((lbasis_hbm, lbasis), (moment_hbm, moment), (rbasis_hbm, rbasis))
            )
        ]
        for copy in copies:
            copy.start()
        copies[0].wait()
        transposed = lbasis[...].T
        lbasis_t[...] = transposed
        copies[1].wait()
        turned = matmul(transposed, moment[...]).astype(jnp.bfloat16)
        copies[2].wait()
        old_part[...] = 0.9 * matmul(turned, rbasis[...])
        columns = rbasis.shape[0]
        col_share = columns // (columns // LANES)
        tail = col_share - LANES
        first = pl.multiple_of(table[SHARE] * col_share, tail)
        main = rbasis[pl.ds(first, LANES), :]
        last = rbasis[pl.ds(pl.multiple_of(first + LANES, tail), tail), :]
        back_basis[...] = jnp.concatenate([main] + [last] * (LANES // tail), axis=0).T


def assemble(arrived, gradient, groups, rows):
    half = LANES // 2
    tail = gradient.shape[1] - half
    for r in range(arrived.shape[0] // groups):
        start = tail_start(r)
        for m in range(groups):
            piece = r * groups + m
            base = m * rows
            gradient[base : base + rows, r * LANES : (r + 1) * LANES] = arrived[piece, :rows, :]
            for g in range(3 if r == 0 else 2):
                row = base + (start + g) * SUBLANES
                below = rows + (g % 2) * SUBLANES
                beside = (g // 2) * half
                gradient[row : row + SUBLANES, tail:] = arrived[
                    piece, below : below + SUBLANES, beside : beside + half
                ]


def owner_kernel(
    table, arrived, lbasis, rbasis, lbasis_t, old_part, back_basis, second,
    gradient, new_second, back_out, turned, scaled, back, sems,
):
    found = table[FOUND]
    groups = back.shape[0]
    copies = [
        pltpu.make_async_copy(back.at[n], back_out.at[n], sems.at[n]) for n in range(groups)
    ]
    columns = gradient.shape[1]
    rows = columns // groups

    @pl.when(found == 1)
    def _():
        assemble(arrived, gradient, groups, rows)
        turned[...] = matmul(lbasis_t[...], gradient[...]).astype(jnp.bfloat16)
        for low in range(0, columns, CUT):
            cols = slice(low, min(low + CUT, columns))
            rotated = matmul(turned[...], rbasis[:, cols])
            fresh = 0.95 * second[:, cols] + 0.05 * rotated * rotated
            new_second[:, cols] = fresh
            rotated_mom = old_part[:, cols] + 0.1 * rotated
            spread = fresh * lax.rsqrt(fresh) + 1e-08
            scaled[:, cols] = (rotated_mom * lax.rsqrt(spread * spread)).astype(jnp.bfloat16)
        total = matmul(scaled[...], back_basis[...])
        sums = total.astype(jnp.bfloat16)
        lane = lax.broadcasted_iota(jnp.int32, (SUBLANES, LANES), 1)
        tail_groups = rows // SUBLANES - 1
        width = LANES // tail_groups
        half_groups = groups // 2
        for side in range(2):
            first = side * half_groups
            result = matmul(lbasis[first * rows : (first + half_groups) * rows, :], sums)
            for m in range(first, first + half_groups):
                off = (m - first) * rows
                back[groups - 1 - m, :rows, :] = result[off : off + rows, :LANES].astype(jnp.bfloat16)
                mixed = result[off : off + SUBLANES, LANES:]
                for g in range(1, tail_groups):
                    row = off + g * SUBLANES
                    mixed = jnp.where(
                        lane < g * width, mixed, result[row : row + SUBLANES, LANES:]
                    )
                back[groups - 1 - m, rows : rows + SUBLANES, :] = mixed.astype(jnp.bfloat16)
                back[groups - 1 - m, rows + SUBLANES :, :] = result[
                    off + rows - SUBLANES : off + rows, LANES:
                ].astype(jnp.bfloat16)
            for m in range(first, first + half_groups):
                copies[groups - 1 - m].start()
        for copy in copies:
            copy.wait()

    @pl.when(found == 0)
    def _():
        new_second[...] = second[...]


def factor_kernel(
    table, gradient, second, moment_hbm, left_hbm, right_hbm,
    second_out, moment_out, left_out, right_out,
    moment, left_t, right_t, new_moment, new_left_t, new_right_t, sems,
):
    found = table[FOUND]
    col_share, columns = left_t.shape
    held = (moment, left_t, right_t)
    outs = (moment_out, left_out, right_out)

    def copies_of(first, sources, targets):
        return [
            pltpu.make_async_copy(a, b, sems.at[first + n])
            for n, (a, b) in enumerate(zip(sources, targets))
        ]

    loads = copies_of(0, (left_hbm, right_hbm, moment_hbm), (left_t, right_t, moment))
    fresh = copies_of(3, (new_left_t, new_right_t, new_moment), (left_out, right_out, moment_out))
    kept = copies_of(6, held, outs)
    second_copy = pltpu.make_async_copy(second, second_out, sems.at[9])
    for copy in loads + [second_copy]:
        copy.start()

    @pl.when(found == 1)
    def _():
        first = pl.multiple_of(table[SHARE] * col_share, 16)
        grad = gradient[...]
        left_term = 0.05 * contract_last(gradient[pl.ds(first, col_share), :], grad)
        picked = lax.broadcasted_iota(jnp.int32, (col_share, columns), 0) + first
        places = lax.broadcasted_iota(jnp.int32, (col_share, columns), 1)
        pick = jnp.where(picked == places, 1.0, 0.0).astype(jnp.bfloat16)
        grad_cols_t = contract_last(pick, grad).astype(jnp.bfloat16)
        right_term = 0.05 * matmul(grad_cols_t, grad)
        for copy in loads:
            copy.wait()
        new_left_t[...] = 0.95 * left_t[...] + left_term
        new_right_t[...] = 0.95 * right_t[...] + right_term
        for low in range(0, columns, STRIP):
            strip = slice(low, min(low + STRIP, columns))
            new_moment[strip, :] = (
                0.9 * moment[strip, :].astype(jnp.float32)
                + 0.1 * gradient[strip, :].astype(jnp.float32)
            ).astype(jnp.bfloat16)
        for copy in fresh:
            copy.start()
        for copy in fresh:
            copy.wait()

    @pl.when(found == 0)
    def _():
        for copy in loads:
            copy.wait()
        for copy in kept:
            copy.start()
        for copy in kept:
            copy.wait()

    second_copy.wait()


def place_kernel(table, returned, update, tails, sems):
    blocks, rows, col_share = update.shape
    groups = returned.shape[0]
    tail_groups = rows // SUBLANES - 1
    width = col_share - LANES
    copies = []
    for place in range(blocks):
        slot = table[SLOTS + groups + place]
        copies.append(
            pltpu.make_async_copy(
                returned.at[slot, :rows], update.at[place, :, :LANES], sems.at[place]
            )
        )
        copies[-1].start()
    for place in range(blocks):
        slot = table[SLOTS + groups + place]
        for g in range(tail_groups):
            tails[place, g * SUBLANES : (g + 1) * SUBLANES, :] = returned[
                slot, rows : rows + SUBLANES, g * width : (g + 1) * width
            ]
        tails[place, rows - SUBLANES :, :] = returned[slot, rows + SUBLANES :, :width]
        copies.append(
            pltpu.make_async_copy(
                tails.at[place], update.at[place, :, LANES:], sems.at[blocks + place]
            )
        )
        copies[-1].start()
    for copy in copies:
        copy.wait()


def run(name, kernel, scalars, arrays, outs, scratch=(), flops=0, sems=0, far=0, far_outs=0):
    moved = sum(a.size * a.dtype.itemsize for a in list(arrays) + list(outs))
    near = len(arrays) - far
    near_outs = len(outs) - far_outs
    return pl.pallas_call(
        kernel,
        out_shape=[pltpu.VMEM(o.shape, o.dtype) for o in outs[:near_outs]]
        + [pltpu.HBM(o.shape, o.dtype) for o in outs[near_outs:]],
        in_specs=[SMEM] * len(scalars) + [VMEM] * near + [FAR] * far,
        out_specs=[VMEM] * near_outs + [FAR] * far_outs,
        scratch_shapes=[pltpu.VMEM(o.shape, o.dtype) for o in scratch]
        + [pltpu.SemaphoreType.DMA((sems,))] * (sems > 0),
        compiler_params=pltpu.CompilerParams(vmem_limit_bytes=VMEM_GRANT),
        cost_estimate=pl.CostEstimate(flops=flops, bytes_accessed=moved, transcendentals=0),
        name=name,
    )(
        *scalars,
        *(pltpu.with_memory_space_constraint(a, pltpu.VMEM) for a in arrays[:near]),
        *(pltpu.with_memory_space_constraint(a, pltpu.HBM) for a in arrays[near:]),
    )


def per_device_packed(
    grad_partial,
    owner,
    offset,
    left_factor,
    right_factor,
    left_basis,
    right_basis,
    momentum,
    second_moment,
):
    pieces = grad_partial[0]
    blocks, rows, columns = pieces.shape
    groups = lax.axis_size("mp")
    replicas = lax.axis_size("dp")
    col_share = columns // replicas
    share = lax.axis_index("dp").astype(jnp.int32).reshape(1)
    group = lax.axis_index("mp").astype(jnp.int32).reshape(1)
    bf16, f32 = jnp.bfloat16, jnp.float32
    shape = jax.ShapeDtypeStruct
    packed = shape((blocks, rows + 2 * SUBLANES, LANES), bf16)
    sent = shape((chunk_rows(blocks, rows), LANES), bf16)
    square = (columns, columns)
    lbasis, rbasis, moment, second = left_basis[0], right_basis[0], momentum[0], second_moment[0]
    left_t, right_t = left_factor[0].T, right_factor[0].T
    product = 2 * columns**3

    parts = run(
        "pack",
        pack_kernel,
        [share],
        [pieces],
        [sent] * replicas,
        scratch=[shape(pieces.shape, bf16)],
        sems=blocks,
        far=1,
    )
    parts = [parts[0]] + [
        lax.ppermute(parts[s], "dp", [(i, (i + s) % replicas) for i in range(replicas)])
        for s in range(1, replicas)
    ]
    table = pl.pallas_call(
        table_kernel,
        out_shape=pltpu.SMEM((SLOTS + groups + blocks,), jnp.int32),
        in_specs=[SMEM] * 4,
        out_specs=SMEM,
        name="table",
    )(share, group, owner, offset)
    lbasis_t, old_part, back_basis = run(
        "prepare",
        prepare_kernel,
        [table],
        [lbasis, rbasis, moment],
        [shape(square, bf16), shape(square, f32), shape((columns, 2 * LANES), bf16)],
        scratch=[shape(square, bf16)] * 3,
        sems=3,
        far=3,
        flops=2 * product,
    )
    parts, lbasis_t, old_part, back_basis = lax.optimization_barrier(
        (parts, lbasis_t, old_part, back_basis)
    )
    (outgoing,) = run(
        "route",
        route_kernel,
        [table],
        parts,
        [shape((replicas * groups,) + packed.shape[1:], bf16)],
        scratch=[packed],
    )
    arrived = lax.all_to_all(outgoing, ("dp", "mp"), split_axis=0, concat_axis=0, tiled=True)
    chunks = shape((groups, rows + 2 * SUBLANES, LANES), bf16)
    factor_t = shape(left_t.shape, f32)
    gradient, new_second, back = run(
        "owner_step",
        owner_kernel,
        [table],
        [arrived, lbasis, rbasis, lbasis_t, old_part, back_basis, second],
        [shape(square, bf16), shape(square, f32), chunks],
        scratch=[shape(square, bf16)] * 2 + [chunks],
        sems=groups,
        far_outs=1,
        flops=3 * product,
    )
    returned = lax.all_to_all(
        back,
        "mp",
        split_axis=0,
        concat_axis=0,
        tiled=True,
        axis_index_groups=[list(range(groups))[::-1]],
    )
    new_second, new_moment, new_left_t, new_right_t = run(
        "factors",
        factor_kernel,
        [table],
        [gradient, new_second, moment, left_t, right_t],
        [shape(square, f32), shape(square, bf16), factor_t, factor_t],
        scratch=[shape(square, bf16), factor_t, factor_t] * 2,
        sems=10,
        far=3,
        far_outs=4,
        flops=product,
    )
    (update,) = run(
        "place",
        place_kernel,
        [table],
        [returned],
        [shape((blocks, rows, col_share), bf16)],
        scratch=[shape((blocks, rows, col_share - LANES), bf16)],
        sems=2 * blocks,
        far_outs=1,
    )
    return (
        update,
        new_left_t.T[None],
        new_right_t.T[None],
        new_moment[None],
        new_second[None],
    )


def per_device(grad_partial, *rest):
    _, _, rows, columns = grad_partial.shape
    fits = packed_fits(rows, columns, lax.axis_size("dp"))
    return (per_device_packed if fits else per_device_general)(grad_partial, *rest)


def per_device_general(
    grad_partial,
    owner,
    offset,
    left_factor,
    right_factor,
    left_basis,
    right_basis,
    momentum,
    second_moment,
):
    pieces = grad_partial[0]
    blocks, row_count, columns = pieces.shape
    groups = lax.axis_size("mp")
    replicas = lax.axis_size("dp")
    col_share = columns // replicas
    column = lax.axis_index("dp") * col_share
    my_group = lax.axis_index("mp")
    targets = lax.broadcasted_iota(jnp.int32, (groups, blocks), 0)
    positions = lax.broadcasted_iota(jnp.int32, (blocks, blocks), 0)
    routing = (owner[None, :] == targets).astype(jnp.float32)
    where_at = (offset[None, :] == positions).astype(jnp.float32)
    select = contract_last(routing, where_at).astype(jnp.bfloat16)
    occupied = jnp.any(owner == my_group)
    swapped = lax.all_to_all(grad_partial, "dp", split_axis=3, concat_axis=0, tiled=True)
    summed = jnp.sum(swapped.astype(jnp.float32), axis=0).astype(jnp.bfloat16)
    outgoing = jnp.dot(
        select, summed.reshape(blocks, row_count * col_share), preferred_element_type=jnp.float32
    )
    outgoing = outgoing.astype(jnp.bfloat16).reshape(groups, row_count, col_share)
    landed = lax.all_to_all(outgoing, "mp", split_axis=0, concat_axis=0, tiled=True)
    arrived = lax.all_gather(landed, "dp", axis=2, tiled=True)
    gradient = arrived.reshape(groups * row_count, columns)

    def refresh(operands):
        grad_in, left_fac, right_fac, lbasis, rbasis, moment, second = operands
        grad_rows = lax.dynamic_slice_in_dim(grad_in, column, col_share, 0)
        grad_cols = lax.dynamic_slice_in_dim(grad_in, column, col_share, 1)
        new_left = 0.95 * left_fac + 0.05 * contract_last(grad_in, grad_rows)
        new_right = 0.95 * right_fac + 0.05 * contract_first(grad_in, grad_cols)
        new_moment = (0.9 * moment.astype(jnp.float32) + 0.1 * grad_in.astype(jnp.float32)).astype(
            jnp.bfloat16
        )
        turned = contract_first(lbasis, grad_in).astype(jnp.bfloat16)
        rotated = jnp.dot(turned, rbasis, preferred_element_type=jnp.float32)
        turned_mom = contract_first(lbasis, new_moment).astype(jnp.bfloat16)
        rotated_mom = jnp.dot(turned_mom, rbasis, preferred_element_type=jnp.float32)
        new_second = 0.95 * second + 0.05 * rotated * rotated
        scaled = (rotated_mom / (jnp.sqrt(new_second) + 1e-08)).astype(jnp.bfloat16)
        unrotated = jnp.dot(lbasis, scaled, preferred_element_type=jnp.float32).astype(jnp.bfloat16)
        back_rows = lax.dynamic_slice_in_dim(rbasis, column, col_share, 0)
        return (new_left, new_right, new_moment, new_second, contract_last(unrotated, back_rows))

    def keep_old(operands):
        grad_in, left_fac, right_fac, lbasis, rbasis, moment, second = operands
        return (left_fac, right_fac, moment, second, jnp.zeros((columns, col_share), jnp.float32))

    operands = (
        gradient,
        left_factor[0],
        right_factor[0],
        left_basis[0],
        right_basis[0],
        momentum[0],
        second_moment[0],
    )
    new_left, new_right, new_moment, new_second, turned_cols = lax.cond(
        occupied, refresh, keep_old, operands
    )
    outgoing_back = turned_cols.astype(jnp.bfloat16).reshape(groups, row_count, col_share)
    returned = lax.all_to_all(outgoing_back, "mp", split_axis=0, concat_axis=0, tiled=True)
    update = contract_first(select, returned.reshape(groups, row_count * col_share)).astype(
        jnp.bfloat16
    )
    update = update.reshape(blocks, row_count, col_share)
    return (update, new_left[None], new_right[None], new_moment[None], new_second[None])


def solution(mesh):
    placed = (
        P("dp", None, "mp", None),
        P(),
        P(),
        P("mp", None, "dp"),
        P("mp", None, "dp"),
        P("mp", None, None),
        P("mp", None, None),
        P("mp", None, None),
        P("mp", None, None),
    )
    return jax.shard_map(
        per_device,
        mesh=mesh,
        in_specs=placed,
        out_specs=(
            P(None, "mp", "dp"),
            P("mp", None, "dp"),
            P("mp", None, "dp"),
            P("mp", None, None),
            P("mp", None, None),
        ),
        check_vma=False,
    )
```

```python
import jax
import jax.numpy as jnp
from jax import lax
from jax.experimental import pallas as pl
from jax.experimental.pallas import tpu as pltpu
from jax.sharding import PartitionSpec as P

LANES = 128
SUBLANES = 8
VMEM = pl.BlockSpec(memory_space=pltpu.VMEM)
SMEM = pl.BlockSpec(memory_space=pltpu.SMEM)
FAR = pl.BlockSpec(memory_space=pltpu.HBM)
VMEM_GRANT = 16 * 2**20
CUT = 2 * LANES
STRIP = 48

def contract_first(matrix_a, matrix_b):
    return lax.dot_general(
        matrix_a, matrix_b, (((0,), (0,)), ((), ())), preferred_element_type=jnp.float32
    )


def contract_last(matrix_a, matrix_b):
    return lax.dot_general(
        matrix_a, matrix_b, (((1,), (1,)), ((), ())), preferred_element_type=jnp.float32
    )


def matmul(matrix_a, matrix_b):
    return jnp.dot(matrix_a, matrix_b, preferred_element_type=jnp.float32)


def tail_start(share):
    return jnp.where(share == 0, 0, 2 * share + 1) if not isinstance(share, int) else (
        0 if share == 0 else 2 * share + 1
    )


def packed_fits(rows, columns, replicas):
    width = columns // replicas - LANES
    return (
        columns == replicas * LANES + LANES // 2
        and rows == (2 * replicas + 1) * SUBLANES
        and width * replicas == LANES // 2
        and width % 16 == 0
        and LANES // width == rows // SUBLANES - 1
    )


def tail_places(blocks, rows):
    for b in range(blocks):
        for g in range(3):
            place = 3 * b + g
            yield b, g, blocks * rows + place // 2 * SUBLANES, place % 2 * (LANES // 2)


def chunk_rows(blocks, rows):
    return blocks * rows + -(-3 * blocks // 2) * SUBLANES


def pack_kernel(me_ref, grad_hbm, *refs):
    outs, last, sems = refs[:-2], refs[-2], refs[-1]
    replicas = len(outs)
    blocks, rows, columns = grad_hbm.shape
    half = LANES // 2
    shares = [lax.rem(me_ref[0] + step, replicas) for step in range(replicas)]
    copies = [
        pltpu.make_async_copy(
            grad_hbm.at[:, :, columns - half :], last, sems.at[replicas]
        )
    ]
    for step in range(replicas):
        col = pl.multiple_of(shares[step] * LANES, LANES)
        copies.append(
            pltpu.make_async_copy(
                grad_hbm.at[:, :, pl.ds(col, LANES)],
                outs[step].at[: blocks * rows, :].reshape(blocks, rows, LANES),
                sems.at[step],
            )
        )
    for copy in copies:
        copy.start()
    copies[0].wait()
    for step in range(replicas):
        start = tail_start(shares[step])
        for b, g, row, lane in tail_places(blocks, rows):
            source = pl.multiple_of(
                jnp.minimum(start + g, rows // SUBLANES - 1) * SUBLANES, SUBLANES
            )
            outs[step][row : row + SUBLANES, lane : lane + half] = last[
                b, pl.ds(source, SUBLANES), :
            ]
    for copy in copies[1:]:
        copy.wait()


SHARE, GROUP, FOUND, SLOTS = 0, 1, 2, 3


def table_kernel(share_ref, group_ref, owner_ref, offset_ref, table):
    blocks = owner_ref.shape[0]
    groups = table.shape[0] - SLOTS - blocks
    table[SHARE] = share_ref[0]
    table[GROUP] = group_ref[0]
    found = jnp.int32(0)
    for b in range(blocks):
        found = jnp.where(owner_ref[b] == group_ref[0], 1, found)
    table[FOUND] = found
    for group in range(groups):
        table[SLOTS + group] = jnp.int32(0)
    for b in range(blocks):
        table[SLOTS + owner_ref[b]] = offset_ref[b]
        table[SLOTS + groups + offset_ref[b]] = groups - 1 - owner_ref[b]


def route_kernel(table, *refs):
    parts, out, summed = refs[:-2], refs[-2], refs[-1]
    replicas = len(parts)
    groups = out.shape[0] // replicas
    blocks = summed.shape[0]
    rows = summed.shape[1] - 2 * SUBLANES
    half = LANES // 2

    def add(*index):
        total = parts[0][index].astype(jnp.float32)
        for part in parts[1:]:
            total = total + part[index].astype(jnp.float32)
        return total.astype(jnp.bfloat16)

    for b in range(blocks):
        summed[b, :rows, :] = add(slice(b * rows, (b + 1) * rows), slice(None))
        summed[b, rows + SUBLANES :, half:] = jnp.zeros((SUBLANES, half), jnp.bfloat16)
    for b, g, row, lane in tail_places(blocks, rows):
        below = rows + (g % 2) * SUBLANES
        beside = (g // 2) * half
        summed[b, below : below + SUBLANES, beside : beside + half] = add(
            slice(row, row + SUBLANES), slice(lane, lane + half)
        )
    for group in range(groups):
        piece = summed[table[SLOTS + group]]
        for r in range(replicas):
            out[r * groups + group] = piece


def prepare_kernel(
    table, lbasis_hbm, rbasis_hbm, moment_hbm,
    lbasis_t, old_part, back_basis, lbasis, rbasis, moment, sems,
):
    found = table[FOUND]

    @pl.when(found == 1)
    def _():
        copies = [
            pltpu.make_async_copy(source, target, sems.at[n])
            for n, (source, target) in enumerate(
                ((lbasis_hbm, lbasis), (moment_hbm, moment), (rbasis_hbm, rbasis))
            )
        ]
        for copy in copies:
            copy.start()
        copies[0].wait()
        transposed = lbasis[...].T
        lbasis_t[...] = transposed
        copies[1].wait()
        turned = matmul(transposed, moment[...]).astype(jnp.bfloat16)
        copies[2].wait()
        old_part[...] = 9.0 * matmul(turned, rbasis[...])
        columns = rbasis.shape[0]
        col_share = columns // (columns // LANES)
        tail = col_share - LANES
        first = pl.multiple_of(table[SHARE] * col_share, tail)
        main = rbasis[pl.ds(first, LANES), :]
        last = rbasis[pl.ds(pl.multiple_of(first + LANES, tail), tail), :]
        back_basis[...] = jnp.concatenate([main] + [last] * (LANES // tail), axis=0).T


def assemble(arrived, gradient, groups, rows):
    half = LANES // 2
    tail = gradient.shape[1] - half
    for r in range(arrived.shape[0] // groups):
        start = tail_start(r)
        for m in range(groups):
            piece = r * groups + m
            base = m * rows
            gradient[base : base + rows, r * LANES : (r + 1) * LANES] = arrived[piece, :rows, :]
            for g in range(3 if r == 0 else 2):
                row = base + (start + g) * SUBLANES
                below = rows + (g % 2) * SUBLANES
                beside = (g // 2) * half
                gradient[row : row + SUBLANES, tail:] = arrived[
                    piece, below : below + SUBLANES, beside : beside + half
                ]


def owner_kernel(
    table, arrived, lbasis, rbasis, lbasis_t, old_part, back_basis, second,
    gradient, new_second, back_out, turned, scaled, back, sems,
):
    found = table[FOUND]
    groups = back.shape[0]
    copies = [
        pltpu.make_async_copy(back.at[n], back_out.at[n], sems.at[n]) for n in range(groups)
    ]
    columns = gradient.shape[1]
    rows = columns // groups

    @pl.when(found == 1)
    def _():
        assemble(arrived, gradient, groups, rows)
        turned[...] = matmul(lbasis_t[...], gradient[...]).astype(jnp.bfloat16)
        for low in range(0, columns, CUT):
            cols = slice(low, min(low + CUT, columns))
            rotated = matmul(turned[...], rbasis[:, cols])
            fresh = 0.95 * second[:, cols] + 0.05 * rotated * rotated
            new_second[:, cols] = fresh
            rotated_mom = old_part[:, cols] + rotated
            spread = fresh * lax.rsqrt(fresh) + 1e-08
            scaled[:, cols] = (rotated_mom * lax.rsqrt(spread * spread)).astype(jnp.bfloat16)
        total = 0.1 * matmul(scaled[...], back_basis[...])
        sums = total.astype(jnp.bfloat16)
        lane = lax.broadcasted_iota(jnp.int32, (SUBLANES, LANES), 1)
        tail_groups = rows // SUBLANES - 1
        width = LANES // tail_groups
        half_groups = groups // 2
        for side in range(2):
            first = side * half_groups
            result = matmul(lbasis[first * rows : (first + half_groups) * rows, :], sums)
            for m in range(first, first + half_groups):
                off = (m - first) * rows
                back[groups - 1 - m, :rows, :] = result[off : off + rows, :LANES].astype(jnp.bfloat16)
                mixed = result[off : off + SUBLANES, LANES:]
                for g in range(1, tail_groups):
                    row = off + g * SUBLANES
                    mixed = jnp.where(
                        lane < g * width, mixed, result[row : row + SUBLANES, LANES:]
                    )
                back[groups - 1 - m, rows : rows + SUBLANES, :] = mixed.astype(jnp.bfloat16)
                back[groups - 1 - m, rows + SUBLANES :, :] = result[
                    off + rows - SUBLANES : off + rows, LANES:
                ].astype(jnp.bfloat16)
            for m in range(first, first + half_groups):
                copies[groups - 1 - m].start()
        for copy in copies:
            copy.wait()

    @pl.when(found == 0)
    def _():
        new_second[...] = second[...]


def factor_kernel(
    table, gradient, second, moment_hbm, left_hbm, right_hbm,
    second_out, moment_out, left_out, right_out,
    moment, left_t, right_t, new_moment, new_left_t, new_right_t, sems,
):
    found = table[FOUND]
    col_share, columns = left_t.shape
    held = (moment, left_t, right_t)
    outs = (moment_out, left_out, right_out)

    def copies_of(first, sources, targets):
        return [
            pltpu.make_async_copy(a, b, sems.at[first + n])
            for n, (a, b) in enumerate(zip(sources, targets))
        ]

    loads = copies_of(0, (left_hbm, right_hbm, moment_hbm), (left_t, right_t, moment))
    fresh = copies_of(3, (new_left_t, new_right_t, new_moment), (left_out, right_out, moment_out))
    kept = copies_of(6, held, outs)
    second_copy = pltpu.make_async_copy(second, second_out, sems.at[9])
    for copy in loads + [second_copy]:
        copy.start()

    @pl.when(found == 1)
    def _():
        first = pl.multiple_of(table[SHARE] * col_share, 16)
        grad = gradient[...]
        left_term = 0.05 * contract_last(gradient[pl.ds(first, col_share), :], grad)
        picked = lax.broadcasted_iota(jnp.int32, (col_share, columns), 0) + first
        places = lax.broadcasted_iota(jnp.int32, (col_share, columns), 1)
        pick = jnp.where(picked == places, 1.0, 0.0).astype(jnp.bfloat16)
        grad_cols_t = contract_last(pick, grad).astype(jnp.bfloat16)
        right_term = 0.05 * matmul(grad_cols_t, grad)
        for copy in loads:
            copy.wait()
        new_left_t[...] = 0.95 * left_t[...] + left_term
        new_right_t[...] = 0.95 * right_t[...] + right_term
        for low in range(0, columns, STRIP):
            strip = slice(low, min(low + STRIP, columns))
            new_moment[strip, :] = (
                0.9 * moment[strip, :].astype(jnp.float32)
                + 0.1 * gradient[strip, :].astype(jnp.float32)
            ).astype(jnp.bfloat16)
        for copy in fresh:
            copy.start()
        for copy in fresh:
            copy.wait()

    @pl.when(found == 0)
    def _():
        for copy in loads:
            copy.wait()
        for copy in kept:
            copy.start()
        for copy in kept:
            copy.wait()

    second_copy.wait()


def place_kernel(table, returned, update, tails, sems):
    blocks, rows, col_share = update.shape
    groups = returned.shape[0]
    tail_groups = rows // SUBLANES - 1
    width = col_share - LANES
    copies = []
    for place in range(blocks):
        slot = table[SLOTS + groups + place]
        copies.append(
            pltpu.make_async_copy(
                returned.at[slot, :rows], update.at[place, :, :LANES], sems.at[place]
            )
        )
        copies[-1].start()
    for place in range(blocks):
        slot = table[SLOTS + groups + place]
        for g in range(tail_groups):
            tails[place, g * SUBLANES : (g + 1) * SUBLANES, :] = returned[
                slot, rows : rows + SUBLANES, g * width : (g + 1) * width
            ]
        tails[place, rows - SUBLANES :, :] = returned[slot, rows + SUBLANES :, :width]
        copies.append(
            pltpu.make_async_copy(
                tails.at[place], update.at[place, :, LANES:], sems.at[blocks + place]
            )
        )
        copies[-1].start()
    for copy in copies:
        copy.wait()


def run(name, kernel, scalars, arrays, outs, scratch=(), flops=0, sems=0, far=0, far_outs=0):
    moved = sum(a.size * a.dtype.itemsize for a in list(arrays) + list(outs))
    near = len(arrays) - far
    near_outs = len(outs) - far_outs
    return pl.pallas_call(
        kernel,
        out_shape=[pltpu.VMEM(o.shape, o.dtype) for o in outs[:near_outs]]
        + [pltpu.HBM(o.shape, o.dtype) for o in outs[near_outs:]],
        in_specs=[SMEM] * len(scalars) + [VMEM] * near + [FAR] * far,
        out_specs=[VMEM] * near_outs + [FAR] * far_outs,
        scratch_shapes=[pltpu.VMEM(o.shape, o.dtype) for o in scratch]
        + [pltpu.SemaphoreType.DMA((sems,))] * (sems > 0),
        compiler_params=pltpu.CompilerParams(vmem_limit_bytes=VMEM_GRANT),
        cost_estimate=pl.CostEstimate(flops=flops, bytes_accessed=moved, transcendentals=0),
        name=name,
    )(
        *scalars,
        *(pltpu.with_memory_space_constraint(a, pltpu.VMEM) for a in arrays[:near]),
        *(pltpu.with_memory_space_constraint(a, pltpu.HBM) for a in arrays[near:]),
    )


def per_device_packed(
    grad_partial,
    owner,
    offset,
    left_factor,
    right_factor,
    left_basis,
    right_basis,
    momentum,
    second_moment,
):
    pieces = grad_partial[0]
    blocks, rows, columns = pieces.shape
    groups = lax.axis_size("mp")
    replicas = lax.axis_size("dp")
    col_share = columns // replicas
    share = lax.axis_index("dp").astype(jnp.int32).reshape(1)
    group = lax.axis_index("mp").astype(jnp.int32).reshape(1)
    bf16, f32 = jnp.bfloat16, jnp.float32
    shape = jax.ShapeDtypeStruct
    packed = shape((blocks, rows + 2 * SUBLANES, LANES), bf16)
    sent = shape((chunk_rows(blocks, rows), LANES), bf16)
    square = (columns, columns)
    lbasis, rbasis, moment, second = left_basis[0], right_basis[0], momentum[0], second_moment[0]
    left_t, right_t = left_factor[0].T, right_factor[0].T
    product = 2 * columns**3

    parts = run(
        "pack",
        pack_kernel,
        [share],
        [pieces],
        [sent] * replicas,
        scratch=[shape((blocks, rows, LANES // 2), bf16)],
        sems=replicas + 1,
        far=1,
    )
    parts = [parts[0]] + [
        lax.ppermute(parts[s], "dp", [(i, (i + s) % replicas) for i in range(replicas)])
        for s in range(1, replicas)
    ]
    table = pl.pallas_call(
        table_kernel,
        out_shape=pltpu.SMEM((SLOTS + groups + blocks,), jnp.int32),
        in_specs=[SMEM] * 4,
        out_specs=SMEM,
        name="table",
    )(share, group, owner, offset)
    lbasis_t, old_part, back_basis = run(
        "prepare",
        prepare_kernel,
        [table],
        [lbasis, rbasis, moment],
        [shape(square, bf16), shape(square, f32), shape((columns, 2 * LANES), bf16)],
        scratch=[shape(square, bf16)] * 3,
        sems=3,
        far=3,
        flops=2 * product,
    )
    parts, lbasis_t, old_part, back_basis = lax.optimization_barrier(
        (parts, lbasis_t, old_part, back_basis)
    )
    (outgoing,) = run(
        "route",
        route_kernel,
        [table],
        parts,
        [shape((replicas * groups,) + packed.shape[1:], bf16)],
        scratch=[packed],
    )
    arrived = lax.all_to_all(outgoing, ("dp", "mp"), split_axis=0, concat_axis=0, tiled=True)
    chunks = shape((groups, rows + 2 * SUBLANES, LANES), bf16)
    factor_t = shape(left_t.shape, f32)
    gradient, new_second, back = run(
        "owner_step",
        owner_kernel,
        [table],
        [arrived, lbasis, rbasis, lbasis_t, old_part, back_basis, second],
        [shape(square, bf16), shape(square, f32), chunks],
        scratch=[shape(square, bf16)] * 2 + [chunks],
        sems=groups,
        far_outs=1,
        flops=3 * product,
    )
    returned = lax.all_to_all(
        back,
        "mp",
        split_axis=0,
        concat_axis=0,
        tiled=True,
        axis_index_groups=[list(range(groups))[::-1]],
    )
    new_second, new_moment, new_left_t, new_right_t = run(
        "factors",
        factor_kernel,
        [table],
        [gradient, new_second, moment, left_t, right_t],
        [shape(square, f32), shape(square, bf16), factor_t, factor_t],
        scratch=[shape(square, bf16), factor_t, factor_t] * 2,
        sems=10,
        far=3,
        far_outs=4,
        flops=product,
    )
    (update,) = run(
        "place",
        place_kernel,
        [table],
        [returned],
        [shape((blocks, rows, col_share), bf16)],
        scratch=[shape((blocks, rows, col_share - LANES), bf16)],
        sems=2 * blocks,
        far_outs=1,
    )
    return (
        update,
        new_left_t.T[None],
        new_right_t.T[None],
        new_moment[None],
        new_second[None],
    )


def per_device(grad_partial, *rest):
    _, _, rows, columns = grad_partial.shape
    fits = packed_fits(rows, columns, lax.axis_size("dp"))
    return (per_device_packed if fits else per_device_general)(grad_partial, *rest)


def per_device_general(
    grad_partial,
    owner,
    offset,
    left_factor,
    right_factor,
    left_basis,
    right_basis,
    momentum,
    second_moment,
):
    pieces = grad_partial[0]
    blocks, row_count, columns = pieces.shape
    groups = lax.axis_size("mp")
    replicas = lax.axis_size("dp")
    col_share = columns // replicas
    column = lax.axis_index("dp") * col_share
    my_group = lax.axis_index("mp")
    targets = lax.broadcasted_iota(jnp.int32, (groups, blocks), 0)
    positions = lax.broadcasted_iota(jnp.int32, (blocks, blocks), 0)
    routing = (owner[None, :] == targets).astype(jnp.float32)
    where_at = (offset[None, :] == positions).astype(jnp.float32)
    select = contract_last(routing, where_at).astype(jnp.bfloat16)
    occupied = jnp.any(owner == my_group)
    swapped = lax.all_to_all(grad_partial, "dp", split_axis=3, concat_axis=0, tiled=True)
    summed = jnp.sum(swapped.astype(jnp.float32), axis=0).astype(jnp.bfloat16)
    outgoing = jnp.dot(
        select, summed.reshape(blocks, row_count * col_share), preferred_element_type=jnp.float32
    )
    outgoing = outgoing.astype(jnp.bfloat16).reshape(groups, row_count, col_share)
    landed = lax.all_to_all(outgoing, "mp", split_axis=0, concat_axis=0, tiled=True)
    arrived = lax.all_gather(landed, "dp", axis=2, tiled=True)
    gradient = arrived.reshape(groups * row_count, columns)

    def refresh(operands):
        grad_in, left_fac, right_fac, lbasis, rbasis, moment, second = operands
        grad_rows = lax.dynamic_slice_in_dim(grad_in, column, col_share, 0)
        grad_cols = lax.dynamic_slice_in_dim(grad_in, column, col_share, 1)
        new_left = 0.95 * left_fac + 0.05 * contract_last(grad_in, grad_rows)
        new_right = 0.95 * right_fac + 0.05 * contract_first(grad_in, grad_cols)
        new_moment = (0.9 * moment.astype(jnp.float32) + 0.1 * grad_in.astype(jnp.float32)).astype(
            jnp.bfloat16
        )
        turned = contract_first(lbasis, grad_in).astype(jnp.bfloat16)
        rotated = jnp.dot(turned, rbasis, preferred_element_type=jnp.float32)
        turned_mom = contract_first(lbasis, new_moment).astype(jnp.bfloat16)
        rotated_mom = jnp.dot(turned_mom, rbasis, preferred_element_type=jnp.float32)
        new_second = 0.95 * second + 0.05 * rotated * rotated
        scaled = (rotated_mom / (jnp.sqrt(new_second) + 1e-08)).astype(jnp.bfloat16)
        unrotated = jnp.dot(lbasis, scaled, preferred_element_type=jnp.float32).astype(jnp.bfloat16)
        back_rows = lax.dynamic_slice_in_dim(rbasis, column, col_share, 0)
        return (new_left, new_right, new_moment, new_second, contract_last(unrotated, back_rows))

    def keep_old(operands):
        grad_in, left_fac, right_fac, lbasis, rbasis, moment, second = operands
        return (left_fac, right_fac, moment, second, jnp.zeros((columns, col_share), jnp.float32))

    operands = (
        gradient,
        left_factor[0],
        right_factor[0],
        left_basis[0],
        right_basis[0],
        momentum[0],
        second_moment[0],
    )
    new_left, new_right, new_moment, new_second, turned_cols = lax.cond(
        occupied, refresh, keep_old, operands
    )
    outgoing_back = turned_cols.astype(jnp.bfloat16).reshape(groups, row_count, col_share)
    returned = lax.all_to_all(outgoing_back, "mp", split_axis=0, concat_axis=0, tiled=True)
    update = contract_first(select, returned.reshape(groups, row_count * col_share)).astype(
        jnp.bfloat16
    )
    update = update.reshape(blocks, row_count, col_share)
    return (update, new_left[None], new_right[None], new_moment[None], new_second[None])


def solution(mesh):
    placed = (
        P("dp", None, "mp", None),
        P(),
        P(),
        P("mp", None, "dp"),
        P("mp", None, "dp"),
        P("mp", None, None),
        P("mp", None, None),
        P("mp", None, None),
        P("mp", None, None),
    )
    return jax.shard_map(
        per_device,
        mesh=mesh,
        in_specs=placed,
        out_specs=(
            P(None, "mp", "dp"),
            P("mp", None, "dp"),
            P("mp", None, "dp"),
            P("mp", None, None),
            P("mp", None, None),
        ),
        check_vma=False,
    )
```

```python
import jax
import jax.numpy as jnp
from jax import lax
from jax.experimental import pallas as pl
from jax.experimental.pallas import tpu as pltpu
from jax.sharding import PartitionSpec as P

LANES = 128
SUBLANES = 8
VMEM = pl.BlockSpec(memory_space=pltpu.VMEM)
SMEM = pl.BlockSpec(memory_space=pltpu.SMEM)
FAR = pl.BlockSpec(memory_space=pltpu.HBM)
VMEM_GRANT = 16 * 2**20
CUT = 2 * LANES
STRIP = 48

def contract_first(matrix_a, matrix_b):
    return lax.dot_general(
        matrix_a, matrix_b, (((0,), (0,)), ((), ())), preferred_element_type=jnp.float32
    )


def contract_last(matrix_a, matrix_b):
    return lax.dot_general(
        matrix_a, matrix_b, (((1,), (1,)), ((), ())), preferred_element_type=jnp.float32
    )


def matmul(matrix_a, matrix_b):
    return jnp.dot(matrix_a, matrix_b, preferred_element_type=jnp.float32)


def tail_start(share):
    return jnp.where(share == 0, 0, 2 * share + 1) if not isinstance(share, int) else (
        0 if share == 0 else 2 * share + 1
    )


def packed_fits(rows, columns, replicas):
    width = columns // replicas - LANES
    return (
        columns == replicas * LANES + LANES // 2
        and rows == (2 * replicas + 1) * SUBLANES
        and width * replicas == LANES // 2
        and width % 16 == 0
        and LANES // width == rows // SUBLANES - 1
    )


def tail_places(blocks, rows):
    for b in range(blocks):
        for g in range(3):
            place = 3 * b + g
            yield b, g, blocks * rows + place // 2 * SUBLANES, place % 2 * (LANES // 2)


def chunk_rows(blocks, rows):
    return blocks * rows + -(-3 * blocks // 2) * SUBLANES


def pack_kernel(me_ref, grad_hbm, *refs):
    outs, last, sems = refs[:-2], refs[-2], refs[-1]
    replicas = len(outs)
    blocks, rows, columns = grad_hbm.shape
    half = LANES // 2
    shares = [lax.rem(me_ref[0] + step, replicas) for step in range(replicas)]
    copies = [
        pltpu.make_async_copy(
            grad_hbm.at[:, :, columns - half :], last, sems.at[replicas]
        )
    ]
    for step in range(replicas):
        col = pl.multiple_of(shares[step] * LANES, LANES)
        copies.append(
            pltpu.make_async_copy(
                grad_hbm.at[:, :, pl.ds(col, LANES)],
                outs[step].at[: blocks * rows, :].reshape(blocks, rows, LANES),
                sems.at[step],
            )
        )
    for copy in copies:
        copy.start()
    copies[0].wait()
    for step in range(replicas):
        start = tail_start(shares[step])
        for b, g, row, lane in tail_places(blocks, rows):
            source = pl.multiple_of(
                jnp.minimum(start + g, rows // SUBLANES - 1) * SUBLANES, SUBLANES
            )
            outs[step][row : row + SUBLANES, lane : lane + half] = last[
                b, pl.ds(source, SUBLANES), :
            ]
    for copy in copies[1:]:
        copy.wait()


SHARE, GROUP, FOUND, SLOTS = 0, 1, 2, 3


def table_kernel(share_ref, group_ref, owner_ref, offset_ref, table):
    blocks = owner_ref.shape[0]
    groups = table.shape[0] - SLOTS - blocks
    table[SHARE] = share_ref[0]
    table[GROUP] = group_ref[0]
    found = jnp.int32(0)
    for b in range(blocks):
        found = jnp.where(owner_ref[b] == group_ref[0], 1, found)
    table[FOUND] = found
    for group in range(groups):
        table[SLOTS + group] = jnp.int32(0)
    for b in range(blocks):
        table[SLOTS + owner_ref[b]] = offset_ref[b]
        table[SLOTS + groups + offset_ref[b]] = groups - 1 - owner_ref[b]


def route_kernel(table, *refs):
    parts, out, summed = refs[:-2], refs[-2], refs[-1]
    replicas = len(parts)
    groups = out.shape[0] // replicas
    blocks = summed.shape[0]
    rows = summed.shape[1] - 2 * SUBLANES
    half = LANES // 2

    def add(*index):
        total = parts[0][index].astype(jnp.float32)
        for part in parts[1:]:
            total = total + part[index].astype(jnp.float32)
        return total.astype(jnp.bfloat16)

    for b in range(blocks):
        summed[b, :rows, :] = add(slice(b * rows, (b + 1) * rows), slice(None))
        summed[b, rows + SUBLANES :, half:] = jnp.zeros((SUBLANES, half), jnp.bfloat16)
    for b, g, row, lane in tail_places(blocks, rows):
        below = rows + (g % 2) * SUBLANES
        beside = (g // 2) * half
        summed[b, below : below + SUBLANES, beside : beside + half] = add(
            slice(row, row + SUBLANES), slice(lane, lane + half)
        )
    for group in range(groups):
        piece = summed[table[SLOTS + group]]
        for r in range(replicas):
            out[r * groups + group] = piece


def prepare_kernel(
    table, lbasis_hbm, rbasis_hbm, moment_hbm,
    lbasis_t, old_part, back_basis, lbasis, rbasis, moment, sems,
):
    found = table[FOUND]

    @pl.when(found == 1)
    def _():
        copies = [
            pltpu.make_async_copy(source, target, sems.at[n])
            for n, (source, target) in enumerate(
                ((lbasis_hbm, lbasis), (moment_hbm, moment), (rbasis_hbm, rbasis))
            )
        ]
        for copy in copies:
            copy.start()
        copies[0].wait()
        transposed = lbasis[...].T
        lbasis_t[...] = transposed
        copies[1].wait()
        turned = matmul(transposed, moment[...]).astype(jnp.bfloat16)
        copies[2].wait()
        old_part[...] = 9.0 * matmul(turned, rbasis[...])
        columns = rbasis.shape[0]
        col_share = columns // (columns // LANES)
        tail = col_share - LANES
        first = pl.multiple_of(table[SHARE] * col_share, tail)
        main = rbasis[pl.ds(first, LANES), :]
        last = rbasis[pl.ds(pl.multiple_of(first + LANES, tail), tail), :]
        back_basis[...] = jnp.concatenate([main] + [last] * (LANES // tail), axis=0).T


def assemble(arrived, gradient, groups, rows):
    half = LANES // 2
    tail = gradient.shape[1] - half
    for r in range(arrived.shape[0] // groups):
        start = tail_start(r)
        for m in range(groups):
            piece = r * groups + m
            base = m * rows
            gradient[base : base + rows, r * LANES : (r + 1) * LANES] = arrived[piece, :rows, :]
            for g in range(3 if r == 0 else 2):
                row = base + (start + g) * SUBLANES
                below = rows + (g % 2) * SUBLANES
                beside = (g // 2) * half
                gradient[row : row + SUBLANES, tail:] = arrived[
                    piece, below : below + SUBLANES, beside : beside + half
                ]


def owner_kernel(
    table, arrived, lbasis, rbasis, lbasis_t, old_part, back_basis, second,
    gradient, new_second, back_out, turned, scaled, back, sems,
):
    found = table[FOUND]
    groups = back.shape[0]
    copies = [
        pltpu.make_async_copy(back.at[n], back_out.at[n], sems.at[n]) for n in range(groups)
    ]
    columns = gradient.shape[1]
    rows = columns // groups

    @pl.when(found == 1)
    def _():
        assemble(arrived, gradient, groups, rows)
        turned[...] = matmul(lbasis_t[...], gradient[...]).astype(jnp.bfloat16)
        for low in range(0, columns, CUT):
            cols = slice(low, min(low + CUT, columns))
            rotated = matmul(turned[...], rbasis[:, cols])
            fresh = 0.95 * second[:, cols] + 0.05 * rotated * rotated
            new_second[:, cols] = fresh
            rotated_mom = old_part[:, cols] + rotated
            spread = fresh * lax.rsqrt(fresh) + 1e-08
            scaled[:, cols] = (rotated_mom * lax.rsqrt(spread * spread)).astype(jnp.bfloat16)
        total = 0.1 * matmul(scaled[...], back_basis[...])
        sums = total.astype(jnp.bfloat16)
        lane = lax.broadcasted_iota(jnp.int32, (SUBLANES, LANES), 1)
        tail_groups = rows // SUBLANES - 1
        width = LANES // tail_groups
        half_groups = groups // 2
        for side in range(2):
            first = side * half_groups
            result = matmul(lbasis[first * rows : (first + half_groups) * rows, :], sums)
            for m in range(first, first + half_groups):
                off = (m - first) * rows
                back[groups - 1 - m, :rows, :] = result[off : off + rows, :LANES].astype(jnp.bfloat16)
                mixed = result[off : off + SUBLANES, LANES:]
                for g in range(1, tail_groups):
                    row = off + g * SUBLANES
                    mixed = jnp.where(
                        lane < g * width, mixed, result[row : row + SUBLANES, LANES:]
                    )
                back[groups - 1 - m, rows : rows + SUBLANES, :] = mixed.astype(jnp.bfloat16)
                back[groups - 1 - m, rows + SUBLANES :, :] = result[
                    off + rows - SUBLANES : off + rows, LANES:
                ].astype(jnp.bfloat16)
            for m in range(first, first + half_groups):
                copies[groups - 1 - m].start()
        for copy in copies:
            copy.wait()

    @pl.when(found == 0)
    def _():
        new_second[...] = second[...]


def factor_kernel(
    table, gradient, second, moment_hbm, left_hbm, right_hbm,
    second_out, moment_out, left_out, right_out,
    moment, left_t, right_t, new_moment, new_left_t, new_right_t, sems,
):
    found = table[FOUND]
    col_share, columns = left_t.shape
    held = (moment, left_t, right_t)
    outs = (moment_out, left_out, right_out)

    def copies_of(first, sources, targets):
        return [
            pltpu.make_async_copy(a, b, sems.at[first + n])
            for n, (a, b) in enumerate(zip(sources, targets))
        ]

    loads = copies_of(0, (left_hbm, right_hbm, moment_hbm), (left_t, right_t, moment))
    fresh = copies_of(3, (new_left_t, new_right_t, new_moment), (left_out, right_out, moment_out))
    kept = copies_of(6, held, outs)
    second_copy = pltpu.make_async_copy(second, second_out, sems.at[9])
    for copy in loads + [second_copy]:
        copy.start()

    @pl.when(found == 1)
    def _():
        first = pl.multiple_of(table[SHARE] * col_share, 16)
        grad = gradient[...]
        left_term = 0.05 * contract_last(gradient[pl.ds(first, col_share), :], grad)
        picked = lax.broadcasted_iota(jnp.int32, (col_share, columns), 0) + first
        places = lax.broadcasted_iota(jnp.int32, (col_share, columns), 1)
        pick = jnp.where(picked == places, 1.0, 0.0).astype(jnp.bfloat16)
        grad_cols_t = contract_last(pick, grad).astype(jnp.bfloat16)
        right_term = 0.05 * matmul(grad_cols_t, grad)
        for copy in loads:
            copy.wait()
        new_left_t[...] = 0.95 * left_t[...] + left_term
        new_right_t[...] = 0.95 * right_t[...] + right_term
        for low in range(0, columns, STRIP):
            strip = slice(low, min(low + STRIP, columns))
            new_moment[strip, :] = (
                0.9 * moment[strip, :].astype(jnp.float32)
                + 0.1 * gradient[strip, :].astype(jnp.float32)
            ).astype(jnp.bfloat16)
        for copy in fresh:
            copy.start()
        for copy in fresh:
            copy.wait()

    @pl.when(found == 0)
    def _():
        for copy in loads:
            copy.wait()
        for copy in kept:
            copy.start()
        for copy in kept:
            copy.wait()

    second_copy.wait()


def place_kernel(table, returned, update, full, sems):
    blocks, rows, col_share = update.shape
    groups = returned.shape[0]
    tail_groups = rows // SUBLANES - 1
    width = col_share - LANES
    copies = [
        pltpu.make_async_copy(full.at[place], update.at[place], sems.at[place])
        for place in range(blocks)
    ]
    for place in range(blocks):
        slot = table[SLOTS + groups + place]
        full[place, :, :LANES] = returned[slot, :rows, :]
        for g in range(tail_groups):
            full[place, g * SUBLANES : (g + 1) * SUBLANES, LANES:] = returned[
                slot, rows : rows + SUBLANES, g * width : (g + 1) * width
            ]
        full[place, rows - SUBLANES :, LANES:] = returned[slot, rows + SUBLANES :, :width]
        copies[place].start()
    for copy in copies:
        copy.wait()


def run(name, kernel, scalars, arrays, outs, scratch=(), flops=0, sems=0, far=0, far_outs=0):
    moved = sum(a.size * a.dtype.itemsize for a in list(arrays) + list(outs))
    near = len(arrays) - far
    near_outs = len(outs) - far_outs
    return pl.pallas_call(
        kernel,
        out_shape=[pltpu.VMEM(o.shape, o.dtype) for o in outs[:near_outs]]
        + [pltpu.HBM(o.shape, o.dtype) for o in outs[near_outs:]],
        in_specs=[SMEM] * len(scalars) + [VMEM] * near + [FAR] * far,
        out_specs=[VMEM] * near_outs + [FAR] * far_outs,
        scratch_shapes=[pltpu.VMEM(o.shape, o.dtype) for o in scratch]
        + [pltpu.SemaphoreType.DMA((sems,))] * (sems > 0),
        compiler_params=pltpu.CompilerParams(vmem_limit_bytes=VMEM_GRANT),
        cost_estimate=pl.CostEstimate(flops=flops, bytes_accessed=moved, transcendentals=0),
        name=name,
    )(
        *scalars,
        *(pltpu.with_memory_space_constraint(a, pltpu.VMEM) for a in arrays[:near]),
        *(pltpu.with_memory_space_constraint(a, pltpu.HBM) for a in arrays[near:]),
    )


def per_device_packed(
    grad_partial,
    owner,
    offset,
    left_factor,
    right_factor,
    left_basis,
    right_basis,
    momentum,
    second_moment,
):
    pieces = grad_partial[0]
    blocks, rows, columns = pieces.shape
    groups = lax.axis_size("mp")
    replicas = lax.axis_size("dp")
    col_share = columns // replicas
    share = lax.axis_index("dp").astype(jnp.int32).reshape(1)
    group = lax.axis_index("mp").astype(jnp.int32).reshape(1)
    bf16, f32 = jnp.bfloat16, jnp.float32
    shape = jax.ShapeDtypeStruct
    packed = shape((blocks, rows + 2 * SUBLANES, LANES), bf16)
    sent = shape((chunk_rows(blocks, rows), LANES), bf16)
    square = (columns, columns)
    lbasis, rbasis, moment, second = left_basis[0], right_basis[0], momentum[0], second_moment[0]
    left_t, right_t = left_factor[0].T, right_factor[0].T
    product = 2 * columns**3

    parts = run(
        "pack",
        pack_kernel,
        [share],
        [pieces],
        [sent] * replicas,
        scratch=[shape((blocks, rows, LANES // 2), bf16)],
        sems=replicas + 1,
        far=1,
    )
    parts = [parts[0]] + [
        lax.ppermute(parts[s], "dp", [(i, (i + s) % replicas) for i in range(replicas)])
        for s in range(1, replicas)
    ]
    table = pl.pallas_call(
        table_kernel,
        out_shape=pltpu.SMEM((SLOTS + groups + blocks,), jnp.int32),
        in_specs=[SMEM] * 4,
        out_specs=SMEM,
        name="table",
    )(share, group, owner, offset)
    lbasis_t, old_part, back_basis = run(
        "prepare",
        prepare_kernel,
        [table],
        [lbasis, rbasis, moment],
        [shape(square, bf16), shape(square, f32), shape((columns, 2 * LANES), bf16)],
        scratch=[shape(square, bf16)] * 3,
        sems=3,
        far=3,
        flops=2 * product,
    )
    parts, lbasis_t, old_part, back_basis = lax.optimization_barrier(
        (parts, lbasis_t, old_part, back_basis)
    )
    (outgoing,) = run(
        "route",
        route_kernel,
        [table],
        parts,
        [shape((replicas * groups,) + packed.shape[1:], bf16)],
        scratch=[packed],
    )
    arrived = lax.all_to_all(outgoing, ("dp", "mp"), split_axis=0, concat_axis=0, tiled=True)
    chunks = shape((groups, rows + 2 * SUBLANES, LANES), bf16)
    factor_t = shape(left_t.shape, f32)
    gradient, new_second, back = run(
        "owner_step",
        owner_kernel,
        [table],
        [arrived, lbasis, rbasis, lbasis_t, old_part, back_basis, second],
        [shape(square, bf16), shape(square, f32), chunks],
        scratch=[shape(square, bf16)] * 2 + [chunks],
        sems=groups,
        far_outs=1,
        flops=3 * product,
    )
    returned = lax.all_to_all(
        back,
        "mp",
        split_axis=0,
        concat_axis=0,
        tiled=True,
        axis_index_groups=[list(range(groups))[::-1]],
    )
    new_second, new_moment, new_left_t, new_right_t = run(
        "factors",
        factor_kernel,
        [table],
        [gradient, new_second, moment, left_t, right_t],
        [shape(square, f32), shape(square, bf16), factor_t, factor_t],
        scratch=[shape(square, bf16), factor_t, factor_t] * 2,
        sems=10,
        far=3,
        far_outs=4,
        flops=product,
    )
    (update,) = run(
        "place",
        place_kernel,
        [table],
        [returned],
        [shape((blocks, rows, col_share), bf16)],
        scratch=[shape((blocks, rows, col_share), bf16)],
        sems=blocks,
        far_outs=1,
    )
    return (
        update,
        new_left_t.T[None],
        new_right_t.T[None],
        new_moment[None],
        new_second[None],
    )


def per_device(grad_partial, *rest):
    _, _, rows, columns = grad_partial.shape
    fits = packed_fits(rows, columns, lax.axis_size("dp"))
    return (per_device_packed if fits else per_device_general)(grad_partial, *rest)


def per_device_general(
    grad_partial,
    owner,
    offset,
    left_factor,
    right_factor,
    left_basis,
    right_basis,
    momentum,
    second_moment,
):
    pieces = grad_partial[0]
    blocks, row_count, columns = pieces.shape
    groups = lax.axis_size("mp")
    replicas = lax.axis_size("dp")
    col_share = columns // replicas
    column = lax.axis_index("dp") * col_share
    my_group = lax.axis_index("mp")
    targets = lax.broadcasted_iota(jnp.int32, (groups, blocks), 0)
    positions = lax.broadcasted_iota(jnp.int32, (blocks, blocks), 0)
    routing = (owner[None, :] == targets).astype(jnp.float32)
    where_at = (offset[None, :] == positions).astype(jnp.float32)
    select = contract_last(routing, where_at).astype(jnp.bfloat16)
    occupied = jnp.any(owner == my_group)
    swapped = lax.all_to_all(grad_partial, "dp", split_axis=3, concat_axis=0, tiled=True)
    summed = jnp.sum(swapped.astype(jnp.float32), axis=0).astype(jnp.bfloat16)
    outgoing = jnp.dot(
        select, summed.reshape(blocks, row_count * col_share), preferred_element_type=jnp.float32
    )
    outgoing = outgoing.astype(jnp.bfloat16).reshape(groups, row_count, col_share)
    landed = lax.all_to_all(outgoing, "mp", split_axis=0, concat_axis=0, tiled=True)
    arrived = lax.all_gather(landed, "dp", axis=2, tiled=True)
    gradient = arrived.reshape(groups * row_count, columns)

    def refresh(operands):
        grad_in, left_fac, right_fac, lbasis, rbasis, moment, second = operands
        grad_rows = lax.dynamic_slice_in_dim(grad_in, column, col_share, 0)
        grad_cols = lax.dynamic_slice_in_dim(grad_in, column, col_share, 1)
        new_left = 0.95 * left_fac + 0.05 * contract_last(grad_in, grad_rows)
        new_right = 0.95 * right_fac + 0.05 * contract_first(grad_in, grad_cols)
        new_moment = (0.9 * moment.astype(jnp.float32) + 0.1 * grad_in.astype(jnp.float32)).astype(
            jnp.bfloat16
        )
        turned = contract_first(lbasis, grad_in).astype(jnp.bfloat16)
        rotated = jnp.dot(turned, rbasis, preferred_element_type=jnp.float32)
        turned_mom = contract_first(lbasis, new_moment).astype(jnp.bfloat16)
        rotated_mom = jnp.dot(turned_mom, rbasis, preferred_element_type=jnp.float32)
        new_second = 0.95 * second + 0.05 * rotated * rotated
        scaled = (rotated_mom / (jnp.sqrt(new_second) + 1e-08)).astype(jnp.bfloat16)
        unrotated = jnp.dot(lbasis, scaled, preferred_element_type=jnp.float32).astype(jnp.bfloat16)
        back_rows = lax.dynamic_slice_in_dim(rbasis, column, col_share, 0)
        return (new_left, new_right, new_moment, new_second, contract_last(unrotated, back_rows))

    def keep_old(operands):
        grad_in, left_fac, right_fac, lbasis, rbasis, moment, second = operands
        return (left_fac, right_fac, moment, second, jnp.zeros((columns, col_share), jnp.float32))

    operands = (
        gradient,
        left_factor[0],
        right_factor[0],
        left_basis[0],
        right_basis[0],
        momentum[0],
        second_moment[0],
    )
    new_left, new_right, new_moment, new_second, turned_cols = lax.cond(
        occupied, refresh, keep_old, operands
    )
    outgoing_back = turned_cols.astype(jnp.bfloat16).reshape(groups, row_count, col_share)
    returned = lax.all_to_all(outgoing_back, "mp", split_axis=0, concat_axis=0, tiled=True)
    update = contract_first(select, returned.reshape(groups, row_count * col_share)).astype(
        jnp.bfloat16
    )
    update = update.reshape(blocks, row_count, col_share)
    return (update, new_left[None], new_right[None], new_moment[None], new_second[None])


def solution(mesh):
    placed = (
        P("dp", None, "mp", None),
        P(),
        P(),
        P("mp", None, "dp"),
        P("mp", None, "dp"),
        P("mp", None, None),
        P("mp", None, None),
        P("mp", None, None),
        P("mp", None, None),
    )
    return jax.shard_map(
        per_device,
        mesh=mesh,
        in_specs=placed,
        out_specs=(
            P(None, "mp", "dp"),
            P("mp", None, "dp"),
            P("mp", None, "dp"),
            P("mp", None, None),
            P("mp", None, None),
        ),
        check_vma=False,
    )
```
